128 devices in a mesh: ctx: 8 (over x, z_hi), tp: 16 (over y, z_lo, core).
Axes of the slice: x: 4, y: 4, z: 4 (z_hi: 2, z_lo: 2; z = z_hi * 2 + z_lo), core: 2. Of those that a mesh axis runs over, the one named last changes fastest.
Arguments:
- token_ids: int32 [3072], P('ctx'), may hold values from 65 to 84, as said below
- embed_table: bfloat16 [512, 4096], replicated, may hold values from -6 to 6
- norm_gain: float32 [4096], replicated, may hold values from 0.5 to 1.5
- input_weight: bfloat16 [4096, 3, 4096], P(None, None, 'tp'), may hold values from -0.09375 to 0.09375
- short_weight: float32 [3, 3, 4096], P(None, None, 'tp'), may hold values from -3 to 3
- filters: float32 [256, 3072], P('tp', 'ctx'), may hold values from -1.1 to 1.1
- skip_gain: float32 [4096], P('tp'), may hold values from 0.1 to 1.9
- output_weight: bfloat16 [4096, 4096], P(None, 'tp'), may hold values from -0.09375 to 0.09375
- output_grad: bfloat16 [3072, 4096], P('ctx'), may hold values from -6 to 6
Outputs:
- block_output: bfloat16 [3072, 4096], P('ctx')
- output_weight_grad: float32 [4096, 4096], P('ctx', 'tp')
- projection_grad: bfloat16 [3072, 3, 4096], P('ctx', None, 'tp')
- normed_grad: float32 [3072, 4096], P(('ctx', 'tp'))
The draws below stay inside these ranges and needn't reach their ends.
Inputs may be any that keep to these rules, and one draw needn't show every extreme that they name: `token_ids`: each id is the byte code of A, C, G, T or N.
All inputs are finite; a program needn't handle non-finite values.
Results may differ from the reference program's by a relative error of at most 0.0065.
Values may be sent and summed in bfloat16 or wider, within the bound.
A program may use at most 256 MiB of HBM per device.

```python
import jax
import jax.numpy as jnp
from jax import lax

D = 4096
VOCAB = 512
GROUPS = 256
SHORT = 3
TOKENS = 3072


def draw_token_ids(key, part):
    nucleotide_codes = jnp.array([65, 67, 71, 84, 78], dtype=jnp.int32)
    picks = jax.random.randint(key, (TOKENS,), 0, 5)
    picks = picks.at[0].set(0).at[1].set(3)
    return nucleotide_codes[picks]


def draw_filters(key, part):
    rate_key, noise_key = jax.random.split(jax.random.fold_in(key, 17), 2)
    positions = jnp.arange(TOKENS, dtype=jnp.float32)[None, :]
    scales = jnp.exp(jax.random.uniform(rate_key, (GROUPS, 1), minval=jnp.log(30.0), maxval=jnp.log(16.0 * TOKENS)))
    noise = jnp.clip(jax.random.normal(noise_key, (GROUPS, TOKENS)), -4.0, 4.0)
    amplitude = jnp.sqrt(2.0 / scales + 1.0 / TOKENS)
    return (amplitude * noise * jnp.exp(-positions / scales)).astype(jnp.float32)


def levels(stream_key, shape, pieces, low, largest):
    loudness = 1.0
    for dim, shards_of in pieces:
        draws = jax.random.uniform(jax.random.fold_in(jax.random.fold_in(stream_key, 6), dim), (shards_of,), jnp.float32, low / len(pieces), largest / len(pieces))
        loudness = loudness * jnp.repeat(jnp.exp(draws), shape[dim] // shards_of).reshape((-1,) + (1,) * (len(shape) - 1 - dim))
    return loudness


def scatter_about(rng, dims, deviation, most, shards=(), kind=jnp.bfloat16):
    loudness = levels(rng, dims, shards, -0.22, 0.18) if shards else 1.0
    drawn = jax.random.normal(rng, dims, jnp.float32) * deviation * loudness
    return jnp.minimum(jnp.maximum(drawn, -most), most).astype(kind)


def setup_inputs(seed: int = 0) -> dict:
    splits = jax.random.split(jax.random.key(seed), 10)
    token_ids = draw_token_ids(jax.random.fold_in(splits[9], 71), 0)
    embed_table = scatter_about(splits[1], (VOCAB, D), 1.0, 6.0)
    norm_gain = jnp.clip(1.0 + 0.1 * jax.random.normal(splits[2], (D,), jnp.float32), 0.5, 1.5)
    input_weight = scatter_about(splits[3], (D, 3, D), D ** -0.5, 0.09375, ((2, 16),))
    short_weight = scatter_about(splits[4], (SHORT, 3, D), 0.6, 3.0, ((2, 16),), jnp.float32)
    filters = draw_filters(jax.random.fold_in(splits[9], 71), 0)
    skip_gain = jnp.clip(1.0 + 0.18 * jax.random.normal(splits[6], (D,), jnp.float32), 0.1, 1.9)
    output_weight = scatter_about(splits[7], (D, D), D ** -0.5, 0.09375, ((1, 16),))
    output_grad = scatter_about(splits[8], (TOKENS, D), 1.0, 6.0, ((0, 8),))
    return {"token_ids": token_ids, "embed_table": embed_table, "norm_gain": norm_gain, "input_weight": input_weight, "short_weight": short_weight, "filters": filters, "skip_gain": skip_gain, "output_weight": output_weight, "output_grad": output_grad}


def causal_apply(signal, channel_taps, adjoint):
    length = signal.shape[0]
    signal_spec = jnp.fft.rfft(signal, n=2 * length, axis=0)
    filter_spec = jnp.fft.rfft(channel_taps, n=2 * length, axis=0)
    if adjoint:
        filter_spec = jnp.conj(filter_spec)
    return jnp.fft.irfft(signal_spec * filter_spec, n=2 * length, axis=0)[:length].astype(jnp.float32)

def reference(token_ids, embed_table, norm_gain, input_weight, short_weight, filters, skip_gain, output_weight, output_grad):
    tokens = embed_table[token_ids]
    token_values = tokens.astype(jnp.float32)
    inverse_rms = lax.rsqrt(lax.optimization_barrier(jnp.mean(token_values * token_values, axis=-1, keepdims=True)) + 1e-06)
    normed = (token_values * inverse_rms * norm_gain).astype(jnp.bfloat16)
    projected = jnp.einsum('td,djc->tjc', normed.astype(jnp.float32), input_weight.astype(jnp.float32))
    short_taps = short_weight.shape[0]
    length = projected.shape[0]
    padded = jnp.pad(projected, ((short_taps - 1, 0), (0, 0), (0, 0)))
    features = sum((short_weight[tap_index] * padded[short_taps - 1 - tap_index:short_taps - 1 - tap_index + length] for tap_index in range(short_taps)))
    query_part = features[:, 0]
    key_part = features[:, 1]
    value_part = features[:, 2]
    mixture = key_part * value_part
    group_width = mixture.shape[1] // filters.shape[0]
    channel_taps = jnp.repeat(filters.T, group_width, axis=1)
    mixed_out = skip_gain * mixture + causal_apply(mixture, channel_taps, False)
    hidden = (query_part * mixed_out).astype(jnp.bfloat16)
    block_output = (token_values + jnp.dot(hidden, output_weight.T, preferred_element_type=jnp.float32)).astype(jnp.bfloat16)
    hidden_grad = jnp.dot(output_grad, output_weight, preferred_element_type=jnp.float32)
    output_weight_grad = jnp.dot(output_grad.T, hidden, preferred_element_type=jnp.float32)
    mixed_grad = hidden_grad * query_part
    mixture_grad = skip_gain * mixed_grad + causal_apply(mixed_grad, channel_taps, True)
    feature_grad = jnp.stack([hidden_grad * mixed_out, mixture_grad * value_part, mixture_grad * key_part], axis=1)
    padded_grad = jnp.pad(feature_grad, ((0, short_taps - 1), (0, 0), (0, 0)))
    projection_grad = sum((short_weight[tap_index] * padded_grad[tap_index:tap_index + length] for tap_index in range(short_taps))).astype(jnp.bfloat16)
    normed_grad = jnp.einsum('tjc,djc->td', projection_grad.astype(jnp.float32), input_weight.astype(jnp.float32))
    return (block_output, output_weight_grad, projection_grad, normed_grad)
```

```python
import jax
import jax.numpy as jnp
from jax import lax
from jax.sharding import PartitionSpec as P

precise = lax.Precision.HIGHEST
BLOCK = 256


def from_behind(value, axis, steps):
    count = lax.axis_size(axis)
    first, last = (max(0, -steps), min(count, count - steps))
    return lax.ppermute(value, axis, [(source, source + steps) for source in range(first, last)])


def upper_toeplitz(taps, block):
    groups, length = taps.shape
    padded = jnp.concatenate(
        [jnp.zeros((groups, block), taps.dtype), taps, jnp.zeros((groups, 1), taps.dtype)], axis=1
    )
    width = length + block + 1
    tiled = jnp.tile(padded, (1, block))[:, : block * (width - 1)]
    skewed = tiled.reshape(groups, block, width - 1)
    return skewed[:, :, block : block + length]


def adjoint_conv(toeplitz, signal, block):
    length, channels = signal.shape
    groups = toeplitz.shape[0]
    width = channels // groups
    count = length // block
    blocks = signal.reshape(count, block, groups, width)
    padded = jnp.concatenate([blocks, jnp.zeros((count - 1,) + blocks.shape[1:], blocks.dtype)], axis=0)
    shifted = jnp.stack([padded[lag : lag + count] for lag in range(count)], axis=0)
    shifted = shifted.transpose(3, 0, 2, 1, 4).reshape(groups, length, count * width)
    result = jnp.einsum("grk,gkn->grn", toeplitz, shifted, precision=precise)
    result = result.reshape(groups, block, count, width).transpose(2, 1, 0, 3)
    return result.reshape(length, channels)


def to_channels(value):
    return lax.all_to_all(value, "ctx", 1, 0, tiled=True)


def to_rows(value):
    return lax.all_to_all(value, "ctx", 0, 1, tiled=True)


def body(
    token_ids,
    embed_table,
    norm_gain,
    input_weight,
    short_weight,
    filters,
    skip_gain,
    output_weight,
    output_grad,
):
    local_rows = token_ids.shape[0]
    tokens = jnp.take(embed_table, token_ids, axis=0)
    token_values = tokens.astype(jnp.float32)
    inverse_rms = lax.rsqrt(jnp.mean(token_values * token_values, axis=-1, keepdims=True) + 1e-06)
    normed = (token_values * inverse_rms * norm_gain).astype(jnp.bfloat16)
    projected = jnp.einsum("td,djc->tjc", normed, input_weight, preferred_element_type=jnp.float32)
    short_taps = short_weight.shape[0]
    before = from_behind(projected[local_rows - (short_taps - 1) :], "ctx", 1)
    extended = jnp.concatenate([before, projected], axis=0)
    features = sum(
        (
            short_weight[tap_index]
            * extended[short_taps - 1 - tap_index : short_taps - 1 - tap_index + local_rows]
            for tap_index in range(short_taps)
        )
    )
    queries = features[:, 0]
    key_part = features[:, 1]
    value_part = features[:, 2]
    mixture = key_part * value_part

    group_taps = lax.all_to_all(filters, "ctx", 0, 1, tiled=True)
    toeplitz = upper_toeplitz(group_taps, BLOCK)
    mixture_full = to_channels(mixture)
    long_full = adjoint_conv(toeplitz, mixture_full[::-1], BLOCK)[::-1]
    long_part = to_rows(long_full)
    mixed_out = skip_gain * mixture + long_part
    hidden = (queries * mixed_out).astype(jnp.bfloat16)

    partial_sums = jnp.einsum(
        "tc,dc->td", hidden, output_weight, preferred_element_type=jnp.float32
    )
    tp_size = lax.axis_size("tp")
    width = partial_sums.shape[1] // tp_size
    own_sums = lax.psum_scatter(partial_sums, "tp", scatter_dimension=1, tiled=True)
    own_tokens = lax.dynamic_slice_in_dim(token_values, lax.axis_index("tp") * width, width, axis=1)
    own_output = (own_tokens + own_sums).astype(jnp.bfloat16)
    block_output = lax.all_gather(own_output, "tp", axis=1, tiled=True)

    hidden_grad = jnp.dot(output_grad, output_weight, preferred_element_type=jnp.float32)
    output_weight_grad = lax.psum_scatter(
        jnp.einsum("td,tc->dc", output_grad, hidden, preferred_element_type=jnp.float32),
        "ctx",
        scatter_dimension=0,
        tiled=True,
    )
    mixed_grad = hidden_grad * queries
    carried = to_rows(adjoint_conv(toeplitz, to_channels(mixed_grad), BLOCK))
    mixture_grad = skip_gain * mixed_grad + carried
    feature_grad = jnp.stack(
        [hidden_grad * mixed_out, mixture_grad * value_part, mixture_grad * key_part], axis=1
    )
    following = from_behind(feature_grad[: short_taps - 1], "ctx", -1)
    extended_grads = jnp.concatenate([feature_grad, following], axis=0)
    projection_grad = sum(
        (
            short_weight[tap_index] * extended_grads[tap_index : tap_index + local_rows]
            for tap_index in range(short_taps)
        )
    ).astype(jnp.bfloat16)
    normed_grad = lax.psum_scatter(
        jnp.einsum(
            "tjc,djc->td", projection_grad, input_weight, preferred_element_type=jnp.float32
        ),
        "tp",
        scatter_dimension=0,
        tiled=True,
    )
    return (block_output, output_weight_grad, projection_grad, normed_grad)


def solution(mesh):
    in_specs = (
        P("ctx"),
        P(),
        P(),
        P(None, None, "tp"),
        P(None, None, "tp"),
        P("tp", "ctx"),
        P("tp"),
        P(None, "tp"),
        P("ctx", None),
    )
    out_specs = (P("ctx", None), P("ctx", "tp"), P("ctx", None, "tp"), P(("ctx", "tp"), None))
    return jax.shard_map(body, mesh=mesh, in_specs=in_specs, out_specs=out_specs, check_vma=False)
```

```python
import jax
import jax.numpy as jnp
from jax import lax
from jax.experimental import pallas as pl
from jax.experimental.pallas import tpu as pltpu
from jax.sharding import PartitionSpec as P

precise = lax.Precision.HIGHEST
BLOCK = 256


def from_behind(value, axis, steps):
    count = lax.axis_size(axis)
    first, last = (max(0, -steps), min(count, count - steps))
    return lax.ppermute(value, axis, [(source, source + steps) for source in range(first, last)])


def skew_kernel(taps_ref, out_ref):
    block, length = out_ref.shape[1], out_ref.shape[2]
    wide = jnp.broadcast_to(taps_ref[0], (block, taps_ref.shape[2]))
    rolled = pltpu.roll(wide, 0, 1, stride=1, stride_axis=0)
    out_ref[0] = rolled[:, block : block + length]


def toeplitz_rows(padded, block):
    groups, _, width = padded.shape
    length = width - block
    return pl.pallas_call(
        skew_kernel,
        out_shape=jax.ShapeDtypeStruct((groups, block, length), padded.dtype),
        grid=(groups,),
        in_specs=[pl.BlockSpec((1, 1, width), lambda g: (g, 0, 0))],
        out_specs=pl.BlockSpec((1, block, length), lambda g: (g, 0, 0)),
    )(padded)


def conv_matrices(taps, block):
    groups, length = taps.shape
    one = jnp.zeros((groups, 1), taps.dtype)
    causal = jnp.concatenate([one, taps[:, ::-1], jnp.zeros((groups, block - 1), taps.dtype)], axis=1)
    anti = jnp.concatenate([jnp.zeros((groups, block), taps.dtype), taps], axis=1)
    both = toeplitz_rows(jnp.concatenate([causal, anti], axis=0)[:, None, :], block)
    return both[:groups], both[groups:]


def windowed_conv(matrix, signal, block, causal):
    channels, length = signal.shape
    groups = matrix.shape[0]
    count = length // block
    zeros = jnp.zeros((channels, length - block), signal.dtype)
    padded = jnp.concatenate([zeros, signal] if causal else [signal, zeros], axis=1)
    windows = jnp.stack([padded[:, i * block : i * block + length] for i in range(count)], axis=1)
    windows = windows.reshape(groups, channels // groups * count, length)
    result = jnp.einsum("gmk,grk->gmr", windows, matrix, precision=precise)
    return result.reshape(channels, length)


def to_channels(value):
    return lax.all_to_all(value.T, "ctx", 0, 1, tiled=True)


def to_rows(value):
    return lax.all_to_all(value, "ctx", 1, 0, tiled=True).T


def body(
    token_ids,
    embed_table,
    norm_gain,
    input_weight,
    short_weight,
    filters,
    skip_gain,
    output_weight,
    output_grad,
):
    local_rows = token_ids.shape[0]
    tokens = jnp.take(embed_table, token_ids, axis=0)
    token_values = tokens.astype(jnp.float32)
    inverse_rms = lax.rsqrt(jnp.mean(token_values * token_values, axis=-1, keepdims=True) + 1e-06)
    normed = (token_values * inverse_rms * norm_gain).astype(jnp.bfloat16)
    projected = jnp.einsum("td,djc->tjc", normed, input_weight, preferred_element_type=jnp.float32)
    short_taps = short_weight.shape[0]
    before = from_behind(projected[local_rows - (short_taps - 1) :], "ctx", 1)
    extended = jnp.concatenate([before, projected], axis=0)
    features = sum(
        (
            short_weight[tap_index]
            * extended[short_taps - 1 - tap_index : short_taps - 1 - tap_index + local_rows]
            for tap_index in range(short_taps)
        )
    )
    queries = features[:, 0]
    key_part = features[:, 1]
    value_part = features[:, 2]
    mixture = key_part * value_part

    group_taps = lax.all_to_all(filters, "ctx", 0, 1, tiled=True)
    causal_matrix, anti_matrix = conv_matrices(group_taps, BLOCK)
    long_part = to_rows(windowed_conv(causal_matrix, to_channels(mixture), BLOCK, True))
    mixed_out = skip_gain * mixture + long_part
    hidden = (queries * mixed_out).astype(jnp.bfloat16)

    partial_sums = jnp.einsum(
        "tc,dc->td", hidden, output_weight, preferred_element_type=jnp.float32
    )
    tp_size = lax.axis_size("tp")
    width = partial_sums.shape[1] // tp_size
    own_sums = lax.psum_scatter(partial_sums, "tp", scatter_dimension=1, tiled=True)
    own_tokens = lax.dynamic_slice_in_dim(token_values, lax.axis_index("tp") * width, width, axis=1)
    own_output = (own_tokens + own_sums).astype(jnp.bfloat16)
    block_output = lax.all_gather(own_output, "tp", axis=1, tiled=True)

    hidden_grad = jnp.dot(output_grad, output_weight, preferred_element_type=jnp.float32)
    output_weight_grad = lax.psum_scatter(
        jnp.einsum("td,tc->dc", output_grad, hidden, preferred_element_type=jnp.float32),
        "ctx",
        scatter_dimension=0,
        tiled=True,
    )
    mixed_grad = hidden_grad * queries
    carried = to_rows(windowed_conv(anti_matrix, to_channels(mixed_grad), BLOCK, False))
    mixture_grad = skip_gain * mixed_grad + carried
    feature_grad = jnp.stack(
        [hidden_grad * mixed_out, mixture_grad * value_part, mixture_grad * key_part], axis=1
    )
    following = from_behind(feature_grad[: short_taps - 1], "ctx", -1)
    extended_grads = jnp.concatenate([feature_grad, following], axis=0)
    projection_grad = sum(
        (
            short_weight[tap_index] * extended_grads[tap_index : tap_index + local_rows]
            for tap_index in range(short_taps)
        )
    ).astype(jnp.bfloat16)
    normed_grad = lax.psum_scatter(
        jnp.einsum(
            "tjc,djc->td", projection_grad, input_weight, preferred_element_type=jnp.float32
        ),
        "tp",
        scatter_dimension=0,
        tiled=True,
    )
    return (block_output, output_weight_grad, projection_grad, normed_grad)


def solution(mesh):
    in_specs = (
        P("ctx"),
        P(),
        P(),
        P(None, None, "tp"),
        P(None, None, "tp"),
        P("tp", "ctx"),
        P("tp"),
        P(None, "tp"),
        P("ctx", None),
    )
    out_specs = (P("ctx", None), P("ctx", "tp"), P("ctx", None, "tp"), P(("ctx", "tp"), None))
    return jax.shard_map(body, mesh=mesh, in_specs=in_specs, out_specs=out_specs, check_vma=False)
```

```python
import jax
import jax.numpy as jnp
from jax import lax
from jax.experimental import pallas as pl
from jax.experimental.pallas import tpu as pltpu
from jax.sharding import PartitionSpec as P

precise = lax.Precision.HIGHEST
BLOCK = 256


def from_behind(value, axis, steps):
    count = lax.axis_size(axis)
    first, last = (max(0, -steps), min(count, count - steps))
    return lax.ppermute(value, axis, [(source, source + steps) for source in range(first, last)])


def skew_kernel(taps_ref, out_ref):
    block, length = out_ref.shape[1], out_ref.shape[2]
    wide = jnp.broadcast_to(taps_ref[0], (block, taps_ref.shape[2]))
    rolled = pltpu.roll(wide, 0, 1, stride=1, stride_axis=0)
    out_ref[0] = rolled[:, block : block + length]


def toeplitz_rows(padded, block):
    groups, _, width = padded.shape
    length = width - block
    return pl.pallas_call(
        skew_kernel,
        out_shape=jax.ShapeDtypeStruct((groups, block, length), padded.dtype),
        grid=(groups,),
        in_specs=[pl.BlockSpec((1, 1, width), lambda g: (g, 0, 0))],
        out_specs=pl.BlockSpec((1, block, length), lambda g: (g, 0, 0)),
    )(padded)


def conv_matrices(taps, reversed_taps, block):
    groups, length = taps.shape
    one = jnp.zeros((groups, 1), taps.dtype)
    causal = jnp.concatenate([one, reversed_taps, jnp.zeros((groups, block - 1), taps.dtype)], axis=1)
    anti = jnp.concatenate([jnp.zeros((groups, block), taps.dtype), taps], axis=1)
    both = toeplitz_rows(jnp.concatenate([causal, anti], axis=0)[:, None, :], block)
    return both[:groups], both[groups:]


def gather_taps(filters):
    width = filters.shape[1]
    rows = lax.broadcasted_iota(jnp.int32, (width, width), 0)
    cols = lax.broadcasted_iota(jnp.int32, (width, width), 1)
    exchange = (rows + cols == width - 1).astype(filters.dtype)
    flipped = jnp.dot(filters, exchange, precision=precise)
    both = lax.all_to_all(jnp.stack([filters, flipped]), "ctx", 1, 2, tiled=True)
    shards = lax.axis_size("ctx")
    pieces = both[1].reshape(both.shape[1], shards, width)
    reversed_taps = jnp.concatenate([pieces[:, k] for k in reversed(range(shards))], axis=1)
    return both[0], reversed_taps


def windowed_conv(matrix, signal, block, causal):
    channels, length = signal.shape
    groups = matrix.shape[0]
    count = length // block
    zeros = jnp.zeros((channels, length - block), signal.dtype)
    padded = jnp.concatenate([zeros, signal] if causal else [signal, zeros], axis=1)
    windows = jnp.stack([padded[:, i * block : i * block + length] for i in range(count)], axis=1)
    windows = windows.reshape(groups, channels // groups * count, length)
    result = jnp.einsum("gmk,grk->gmr", windows, matrix, precision=precise)
    return result.reshape(channels, length)


def to_channels(value):
    return lax.all_to_all(value.T, "ctx", 0, 1, tiled=True)


def to_rows(value):
    return lax.all_to_all(value, "ctx", 1, 0, tiled=True).T


def body(
    token_ids,
    embed_table,
    norm_gain,
    input_weight,
    short_weight,
    filters,
    skip_gain,
    output_weight,
    output_grad,
):
    local_rows = token_ids.shape[0]
    tokens = jnp.take(embed_table, token_ids, axis=0)
    token_values = tokens.astype(jnp.float32)
    inverse_rms = lax.rsqrt(jnp.mean(token_values * token_values, axis=-1, keepdims=True) + 1e-06)
    normed = (token_values * inverse_rms * norm_gain).astype(jnp.bfloat16)
    projected = jnp.einsum("td,djc->tjc", normed, input_weight, preferred_element_type=jnp.float32)
    short_taps = short_weight.shape[0]
    before = from_behind(projected[local_rows - (short_taps - 1) :], "ctx", 1)
    extended = jnp.concatenate([before, projected], axis=0)
    features = sum(
        (
            short_weight[tap_index]
            * extended[short_taps - 1 - tap_index : short_taps - 1 - tap_index + local_rows]
            for tap_index in range(short_taps)
        )
    )
    queries = features[:, 0]
    key_part = features[:, 1]
    value_part = features[:, 2]
    mixture = key_part * value_part

    group_taps, reversed_taps = gather_taps(filters)
    causal_matrix, anti_matrix = conv_matrices(group_taps, reversed_taps, BLOCK)
    long_part = to_rows(windowed_conv(causal_matrix, to_channels(mixture), BLOCK, True))
    mixed_out = skip_gain * mixture + long_part
    hidden = (queries * mixed_out).astype(jnp.bfloat16)

    tp_size = lax.axis_size("tp")
    width = token_values.shape[1] // tp_size
    weight_rows = lax.all_to_all(output_weight, "tp", 0, 1, tiled=True)
    grad_columns = lax.all_to_all(output_grad, "ctx", 1, 0, tiled=True)
    hidden_wide = lax.all_gather(hidden, "tp", axis=1, tiled=True)
    own_sums = jnp.einsum("tc,dc->td", hidden_wide, weight_rows, preferred_element_type=jnp.float32)
    own_tokens = lax.dynamic_slice_in_dim(token_values, lax.axis_index("tp") * width, width, axis=1)
    own_output = (own_tokens + own_sums).astype(jnp.bfloat16)
    block_output = lax.all_gather(own_output, "tp", axis=1, tiled=True)

    hidden_grad = jnp.dot(output_grad, output_weight, preferred_element_type=jnp.float32)
    hidden_long = lax.all_gather(hidden, "ctx", axis=0, tiled=True)
    output_weight_grad = jnp.einsum(
        "td,tc->dc", grad_columns, hidden_long, preferred_element_type=jnp.float32
    )
    mixed_grad = hidden_grad * queries
    carried = to_rows(windowed_conv(anti_matrix, to_channels(mixed_grad), BLOCK, False))
    mixture_grad = skip_gain * mixed_grad + carried
    feature_grad = jnp.stack(
        [hidden_grad * mixed_out, mixture_grad * value_part, mixture_grad * key_part], axis=1
    )
    following = from_behind(feature_grad[: short_taps - 1], "ctx", -1)
    extended_grads = jnp.concatenate([feature_grad, following], axis=0)
    projection_grad = sum(
        (
            short_weight[tap_index] * extended_grads[tap_index : tap_index + local_rows]
            for tap_index in range(short_taps)
        )
    ).astype(jnp.bfloat16)
    partial_grad = jnp.einsum(
        "tjc,djc->td", projection_grad, input_weight, preferred_element_type=jnp.float32
    ).astype(jnp.bfloat16)
    pieces = partial_grad.reshape(tp_size, local_rows // tp_size, partial_grad.shape[1])
    received = lax.all_to_all(pieces, "tp", 0, 0)
    normed_grad = jnp.sum(received.astype(jnp.float32), axis=0)
    return (block_output, output_weight_grad, projection_grad, normed_grad)


def solution(mesh):
    in_specs = (
        P("ctx"),
        P(),
        P(),
        P(None, None, "tp"),
        P(None, None, "tp"),
        P("tp", "ctx"),
        P("tp"),
        P(None, "tp"),
        P("ctx", None),
    )
    out_specs = (P("ctx", None), P("ctx", "tp"), P("ctx", None, "tp"), P(("ctx", "tp"), None))
    return jax.shard_map(body, mesh=mesh, in_specs=in_specs, out_specs=out_specs, check_vma=False)
```

```python
import jax
import jax.numpy as jnp
from jax import lax
from jax.experimental import pallas as pl
from jax.experimental.pallas import tpu as pltpu
from jax.sharding import PartitionSpec as P

precise = lax.Precision.HIGHEST
BLOCK = 256


def from_behind(value, axis, steps):
    count = lax.axis_size(axis)
    first, last = (max(0, -steps), min(count, count - steps))
    return lax.ppermute(value, axis, [(source, source + steps) for source in range(first, last)])


def skew_kernel(taps_ref, out_ref):
    block, length = out_ref.shape[1], out_ref.shape[2]
    wide = jnp.broadcast_to(taps_ref[0], (block, taps_ref.shape[2]))
    rolled = pltpu.roll(wide, 0, 1, stride=1, stride_axis=0)
    out_ref[0] = rolled[:, block : block + length]


def toeplitz_rows(padded, block):
    groups, _, width = padded.shape
    length = width - block
    return pl.pallas_call(
        skew_kernel,
        out_shape=jax.ShapeDtypeStruct((groups, block, length), padded.dtype),
        grid=(groups,),
        in_specs=[pl.BlockSpec((1, 1, width), lambda g: (g, 0, 0))],
        out_specs=pl.BlockSpec((1, block, length), lambda g: (g, 0, 0)),
    )(padded)


def conv_matrices(taps, reversed_taps, block):
    groups, length = taps.shape
    one = jnp.zeros((groups, 1), taps.dtype)
    causal = jnp.concatenate([one, reversed_taps, jnp.zeros((groups, block - 1), taps.dtype)], axis=1)
    anti = jnp.concatenate([jnp.zeros((groups, block), taps.dtype), taps], axis=1)
    both = toeplitz_rows(jnp.concatenate([causal, anti], axis=0)[:, None, :], block)
    return both[:groups], both[groups:]


def gather_taps(filters):
    width = filters.shape[1]
    rows = lax.broadcasted_iota(jnp.int32, (width, width), 0)
    cols = lax.broadcasted_iota(jnp.int32, (width, width), 1)
    exchange = (rows + cols == width - 1).astype(filters.dtype)
    flipped = jnp.dot(filters, exchange, precision=precise)
    both = lax.all_to_all(jnp.stack([filters, flipped]), "ctx", 1, 2, tiled=True)
    shards = lax.axis_size("ctx")
    pieces = both[1].reshape(both.shape[1], shards, width)
    reversed_taps = jnp.concatenate([pieces[:, k] for k in reversed(range(shards))], axis=1)
    return both[0], reversed_taps


def windowed_conv(matrix, signal, block, causal):
    channels, length = signal.shape
    groups = matrix.shape[0]
    count = length // block
    zeros = jnp.zeros((channels, length - block), signal.dtype)
    padded = jnp.concatenate([zeros, signal] if causal else [signal, zeros], axis=1)
    windows = jnp.stack([padded[:, i * block : i * block + length] for i in range(count)], axis=1)
    windows = windows.reshape(groups, channels // groups * count, length)
    result = jnp.einsum("gmk,grk->gmr", windows, matrix, precision=precise)
    return result.reshape(channels, length)


def to_channels(value):
    return lax.all_to_all(value.T, "ctx", 0, 1, tiled=True)


def to_rows(value):
    return lax.all_to_all(value, "ctx", 1, 0, tiled=True).T


def body(
    token_ids,
    embed_table,
    norm_gain,
    input_weight,
    short_weight,
    filters,
    skip_gain,
    output_weight,
    output_grad,
):
    local_rows = token_ids.shape[0]
    tokens = jnp.take(embed_table, token_ids, axis=0)
    token_values = tokens.astype(jnp.float32)
    inverse_rms = lax.rsqrt(jnp.mean(token_values * token_values, axis=-1, keepdims=True) + 1e-06)
    normed = (token_values * inverse_rms * norm_gain).astype(jnp.bfloat16)
    projected = jnp.einsum("td,djc->tjc", normed, input_weight, preferred_element_type=jnp.float32)
    short_taps = short_weight.shape[0]
    before = from_behind(projected[local_rows - (short_taps - 1) :], "ctx", 1)
    extended = jnp.concatenate([before, projected], axis=0)
    features = sum(
        (
            short_weight[tap_index]
            * extended[short_taps - 1 - tap_index : short_taps - 1 - tap_index + local_rows]
            for tap_index in range(short_taps)
        )
    )
    queries = features[:, 0]
    key_part = features[:, 1]
    value_part = features[:, 2]
    mixture = key_part * value_part

    group_taps, reversed_taps = gather_taps(filters)
    causal_matrix, anti_matrix = conv_matrices(group_taps, reversed_taps, BLOCK)
    long_part = to_rows(windowed_conv(causal_matrix, to_channels(mixture), BLOCK, True))
    mixed_out = skip_gain * mixture + long_part
    hidden = (queries * mixed_out).astype(jnp.bfloat16)

    tp_size = lax.axis_size("tp")
    width = token_values.shape[1] // tp_size
    weight_rows = lax.all_to_all(output_weight, "tp", 0, 1, tiled=True)
    grad_columns = lax.all_to_all(output_grad, "ctx", 1, 0, tiled=True)
    hidden_grad = jnp.dot(output_grad, output_weight, preferred_element_type=jnp.float32)
    mixed_grad = hidden_grad * queries
    hidden, mixed_grad, weight_rows, grad_columns = lax.optimization_barrier(
        (hidden, mixed_grad, weight_rows, grad_columns)
    )
    hidden_wide = lax.all_gather(hidden, "tp", axis=1, tiled=True)
    hidden_long = lax.all_gather(hidden, "ctx", axis=0, tiled=True)
    own_sums = jnp.einsum("tc,dc->td", hidden_wide, weight_rows, preferred_element_type=jnp.float32)
    own_tokens = lax.dynamic_slice_in_dim(token_values, lax.axis_index("tp") * width, width, axis=1)
    own_output = (own_tokens + own_sums).astype(jnp.bfloat16)
    block_output = lax.all_gather(own_output, "tp", axis=1, tiled=True)
    output_weight_grad = jnp.einsum(
        "td,tc->dc", grad_columns, hidden_long, preferred_element_type=jnp.float32
    )
    carried = to_rows(windowed_conv(anti_matrix, to_channels(mixed_grad), BLOCK, False))
    mixture_grad = skip_gain * mixed_grad + carried
    feature_grad = jnp.stack(
        [hidden_grad * mixed_out, mixture_grad * value_part, mixture_grad * key_part], axis=1
    )
    following = from_behind(feature_grad[: short_taps - 1], "ctx", -1)
    extended_grads = jnp.concatenate([feature_grad, following], axis=0)
    projection_grad = sum(
        (
            short_weight[tap_index] * extended_grads[tap_index : tap_index + local_rows]
            for tap_index in range(short_taps)
        )
    ).astype(jnp.bfloat16)
    partial_grad = jnp.einsum(
        "tjc,djc->td", projection_grad, input_weight, preferred_element_type=jnp.float32
    ).astype(jnp.bfloat16)
    pieces = partial_grad.reshape(tp_size, local_rows // tp_size, partial_grad.shape[1])
    received = lax.all_to_all(pieces, "tp", 0, 0)
    normed_grad = jnp.sum(received.astype(jnp.float32), axis=0)
    return (block_output, output_weight_grad, projection_grad, normed_grad)


def solution(mesh):
    in_specs = (
        P("ctx"),
        P(),
        P(),
        P(None, None, "tp"),
        P(None, None, "tp"),
        P("tp", "ctx"),
        P("tp"),
        P(None, "tp"),
        P("ctx", None),
    )
    out_specs = (P("ctx", None), P("ctx", "tp"), P("ctx", None, "tp"), P(("ctx", "tp"), None))
    return jax.shard_map(body, mesh=mesh, in_specs=in_specs, out_specs=out_specs, check_vma=False)
```

```python
import jax
import jax.numpy as jnp
from jax import lax
from jax.experimental import pallas as pl
from jax.experimental.pallas import tpu as pltpu
from jax.sharding import PartitionSpec as P

precise = lax.Precision.HIGHEST
BLOCK = 256
TP = ("chip", "core")


def from_behind(value, axis, steps):
    count = lax.axis_size(axis)
    first, last = (max(0, -steps), min(count, count - steps))
    return lax.ppermute(value, axis, [(source, source + steps) for source in range(first, last)])


def skew_kernel(taps_ref, out_ref):
    block, length = out_ref.shape[1], out_ref.shape[2]
    wide = jnp.broadcast_to(taps_ref[0], (block, taps_ref.shape[2]))
    rolled = pltpu.roll(wide, 0, 1, stride=1, stride_axis=0)
    out_ref[0] = rolled[:, block : block + length]


def toeplitz_rows(padded, block):
    groups, _, width = padded.shape
    length = width - block
    return pl.pallas_call(
        skew_kernel,
        out_shape=jax.ShapeDtypeStruct((groups, block, length), padded.dtype),
        grid=(groups,),
        in_specs=[pl.BlockSpec((1, 1, width), lambda g: (g, 0, 0))],
        out_specs=pl.BlockSpec((1, block, length), lambda g: (g, 0, 0)),
    )(padded)


def conv_matrices(taps, reversed_taps, block):
    groups, length = taps.shape
    one = jnp.zeros((groups, 1), taps.dtype)
    causal = jnp.concatenate([one, reversed_taps, jnp.zeros((groups, block - 1), taps.dtype)], axis=1)
    anti = jnp.concatenate([jnp.zeros((groups, block), taps.dtype), taps], axis=1)
    both = toeplitz_rows(jnp.concatenate([causal, anti], axis=0)[:, None, :], block)
    return both[:groups], both[groups:]


def gather_taps(filters):
    width = filters.shape[1]
    rows = lax.broadcasted_iota(jnp.int32, (width, width), 0)
    cols = lax.broadcasted_iota(jnp.int32, (width, width), 1)
    exchange = (rows + cols == width - 1).astype(filters.dtype)
    flipped = jnp.dot(filters, exchange, precision=precise)
    both = lax.all_to_all(jnp.stack([filters, flipped]), "ctx", 1, 2, tiled=True)
    shards = lax.axis_size("ctx")
    pieces = both[1].reshape(both.shape[1], shards, width)
    reversed_taps = jnp.concatenate([pieces[:, k] for k in reversed(range(shards))], axis=1)
    return both[0], reversed_taps


def windowed_conv(matrix, signal, block, causal):
    channels, length = signal.shape
    groups = matrix.shape[0]
    count = length // block
    zeros = jnp.zeros((channels, length - block), signal.dtype)
    padded = jnp.concatenate([zeros, signal] if causal else [signal, zeros], axis=1)
    windows = jnp.stack([padded[:, i * block : i * block + length] for i in range(count)], axis=1)
    windows = windows.reshape(groups, channels // groups * count, length)
    result = jnp.einsum("gmk,grk->gmr", windows, matrix, precision=precise)
    return result.reshape(channels, length)


def to_channels(value):
    return lax.all_to_all(value.T, "ctx", 0, 1, tiled=True)


def to_rows(value):
    return lax.all_to_all(value, "ctx", 1, 0, tiled=True).T


def body(
    token_ids,
    embed_table,
    norm_gain,
    input_weight,
    short_weight,
    filters,
    skip_gain,
    output_weight,
    output_grad,
):
    local_rows = token_ids.shape[0]
    tokens = jnp.take(embed_table, token_ids, axis=0)
    token_values = tokens.astype(jnp.float32)
    inverse_rms = lax.rsqrt(jnp.mean(token_values * token_values, axis=-1, keepdims=True) + 1e-06)
    normed = (token_values * inverse_rms * norm_gain).astype(jnp.bfloat16)
    projected = jnp.einsum("td,djc->tjc", normed, input_weight, preferred_element_type=jnp.float32)
    short_taps = short_weight.shape[0]
    before = from_behind(projected[local_rows - (short_taps - 1) :], "ctx", 1)
    extended = jnp.concatenate([before, projected], axis=0)
    features = sum(
        (
            short_weight[tap_index]
            * extended[short_taps - 1 - tap_index : short_taps - 1 - tap_index + local_rows]
            for tap_index in range(short_taps)
        )
    )
    queries = features[:, 0]
    key_part = features[:, 1]
    value_part = features[:, 2]
    mixture = key_part * value_part
    weight_rows = lax.all_to_all(output_weight, TP, 0, 1, tiled=True)
    grad_columns = lax.all_to_all(output_grad, "ctx", 1, 0, tiled=True)
    mixture, weight_rows, grad_columns = lax.optimization_barrier((mixture, weight_rows, grad_columns))

    group_taps, reversed_taps = gather_taps(filters)
    causal_matrix, anti_matrix = conv_matrices(group_taps, reversed_taps, BLOCK)
    long_part = to_rows(windowed_conv(causal_matrix, to_channels(mixture), BLOCK, True))
    mixed_out = skip_gain * mixture + long_part
    hidden = (queries * mixed_out).astype(jnp.bfloat16)

    tp_size = lax.axis_size(TP)
    width = token_values.shape[1] // tp_size
    hidden_grad = jnp.dot(output_grad, output_weight, preferred_element_type=jnp.float32)
    mixed_grad = hidden_grad * queries
    hidden, mixed_grad, weight_rows, grad_columns = lax.optimization_barrier(
        (hidden, mixed_grad, weight_rows, grad_columns)
    )
    hidden_wide = lax.all_gather(hidden, TP, axis=1, tiled=True)
    hidden_long = lax.all_gather(hidden, "ctx", axis=0, tiled=True)
    own_sums = jnp.einsum("tc,dc->td", hidden_wide, weight_rows, preferred_element_type=jnp.float32)
    own_tokens = lax.dynamic_slice_in_dim(token_values, lax.axis_index(TP) * width, width, axis=1)
    own_output = (own_tokens + own_sums).astype(jnp.bfloat16)
    block_output = lax.all_gather(own_output, TP, axis=1, tiled=True)
    output_weight_grad = jnp.einsum(
        "td,tc->dc", grad_columns, hidden_long, preferred_element_type=jnp.float32
    )
    carried = to_rows(windowed_conv(anti_matrix, to_channels(mixed_grad), BLOCK, False))
    mixture_grad = skip_gain * mixed_grad + carried
    feature_grad = jnp.stack(
        [hidden_grad * mixed_out, mixture_grad * value_part, mixture_grad * key_part], axis=1
    )
    following = from_behind(feature_grad[: short_taps - 1], "ctx", -1)
    extended_grads = jnp.concatenate([feature_grad, following], axis=0)
    projection_grad = sum(
        (
            short_weight[tap_index] * extended_grads[tap_index : tap_index + local_rows]
            for tap_index in range(short_taps)
        )
    ).astype(jnp.bfloat16)
    chips = lax.axis_size("chip")
    cores = lax.axis_size("core")
    chip_weight = lax.all_gather(input_weight, "core", axis=2, tiled=True)
    row_blocks = projection_grad.reshape(
        chips, cores, local_rows // tp_size, short_taps, projection_grad.shape[2]
    )
    chip_rows = lax.all_to_all(row_blocks, "core", 1, 4, tiled=True)[:, 0]
    partial_grad = jnp.einsum(
        "qujc,djc->qud", chip_rows, chip_weight, preferred_element_type=jnp.float32
    ).astype(jnp.bfloat16)
    received = lax.all_to_all(partial_grad, "chip", 0, 0)
    normed_grad = jnp.sum(received.astype(jnp.float32), axis=0)
    return (block_output, output_weight_grad, projection_grad, normed_grad)


def solution(mesh):
    ctx_size, tp_size = mesh.devices.shape
    devices = mesh.devices.reshape(ctx_size, tp_size // 2, 2)
    split_mesh = jax.sharding.Mesh(devices, ("ctx", "chip", "core"))
    in_specs = (
        P("ctx"),
        P(),
        P(),
        P(None, None, TP),
        P(None, None, TP),
        P(TP, "ctx"),
        P(TP),
        P(None, TP),
        P("ctx", None),
    )
    out_specs = (P("ctx", None), P("ctx", TP), P("ctx", None, TP), P(("ctx",) + TP, None))
    return jax.shard_map(body, mesh=split_mesh, in_specs=in_specs, out_specs=out_specs, check_vma=False)
```

```python
import jax
import jax.numpy as jnp
from jax import lax
from jax.experimental import pallas as pl
from jax.experimental.pallas import tpu as pltpu
from jax.sharding import PartitionSpec as P

precise = lax.Precision.HIGHEST
BLOCK = 256
TP = ("chip", "core")


def from_behind(value, axis, steps):
    count = lax.axis_size(axis)
    first, last = (max(0, -steps), min(count, count - steps))
    return lax.ppermute(value, axis, [(source, source + steps) for source in range(first, last)])


def skew_kernel(taps_ref, out_ref):
    block, length = out_ref.shape[1], out_ref.shape[2]
    wide = jnp.broadcast_to(taps_ref[0], (block, taps_ref.shape[2]))
    rolled = pltpu.roll(wide, 0, 1, stride=1, stride_axis=0)
    out_ref[0] = rolled[:, block : block + length]


def toeplitz_rows(padded, block):
    groups, _, width = padded.shape
    length = width - block
    return pl.pallas_call(
        skew_kernel,
        out_shape=jax.ShapeDtypeStruct((groups, block, length), padded.dtype),
        grid=(groups,),
        in_specs=[pl.BlockSpec((1, 1, width), lambda g: (g, 0, 0))],
        out_specs=pl.BlockSpec((1, block, length), lambda g: (g, 0, 0)),
    )(padded)


def conv_matrices(taps, reversed_taps, block):
    groups, length = taps.shape
    one = jnp.zeros((groups, 1), taps.dtype)
    causal = jnp.concatenate([one, reversed_taps, jnp.zeros((groups, block - 1), taps.dtype)], axis=1)
    anti = jnp.concatenate([jnp.zeros((groups, block), taps.dtype), taps], axis=1)
    both = toeplitz_rows(jnp.concatenate([causal, anti], axis=0)[:, None, :], block)
    return both[:groups], both[groups:]


def gather_taps(filters):
    width = filters.shape[1]
    rows = lax.broadcasted_iota(jnp.int32, (width, width), 0)
    cols = lax.broadcasted_iota(jnp.int32, (width, width), 1)
    exchange = (rows + cols == width - 1).astype(filters.dtype)
    flipped = jnp.dot(filters, exchange, precision=precise)
    both = lax.all_to_all(jnp.stack([filters, flipped]), "ctx", 1, 2, tiled=True)
    shards = lax.axis_size("ctx")
    pieces = both[1].reshape(both.shape[1], shards, width)
    reversed_taps = jnp.concatenate([pieces[:, k] for k in reversed(range(shards))], axis=1)
    return both[0], reversed_taps


def windowed_conv(matrix, signal, block, causal):
    channels, length = signal.shape
    groups = matrix.shape[0]
    count = length // block
    zeros = jnp.zeros((channels, length - block), signal.dtype)
    padded = jnp.concatenate([zeros, signal] if causal else [signal, zeros], axis=1)
    windows = jnp.stack([padded[:, i * block : i * block + length] for i in range(count)], axis=1)
    windows = windows.reshape(groups, channels // groups * count, length)
    result = jnp.einsum("gmk,grk->gmr", windows, matrix, precision=precise)
    return result.reshape(channels, length)


def exchange_kernel(x_ref, o_ref, send_sems, recv_sems, local_sem):
    count = x_ref.shape[0]
    me = lax.axis_index("ctx")
    chip = lax.axis_index("chip")
    core = lax.axis_index("core")
    mesh_id = pl.DeviceIdType.MESH
    barrier = pltpu.get_barrier_semaphore()
    for offset in range(1, count):
        peer = lax.rem(me + offset, count)
        pl.semaphore_signal(barrier, 1, device_id=(peer, chip, core), device_id_type=mesh_id)
    pl.semaphore_wait(barrier, count - 1)
    local = pltpu.make_async_copy(x_ref.at[me], o_ref.at[me], local_sem)
    local.start()
    sends = []
    for offset in range(1, count):
        peer = lax.rem(me + offset, count)
        copy = pltpu.make_async_remote_copy(
            src_ref=x_ref.at[peer],
            dst_ref=o_ref.at[me],
            send_sem=send_sems.at[offset],
            recv_sem=recv_sems.at[offset],
            device_id=(peer, chip, core),
            device_id_type=mesh_id,
        )
        copy.start()
        sends.append(copy)
    for copy in sends:
        copy.wait_send()
    for offset in range(1, count):
        source = lax.rem(me + count - offset, count)
        pltpu.make_async_remote_copy(
            src_ref=x_ref.at[source],
            dst_ref=o_ref.at[source],
            send_sem=send_sems.at[offset],
            recv_sem=recv_sems.at[offset],
            device_id=(source, chip, core),
            device_id_type=mesh_id,
        ).wait_recv()
    local.wait()


def exchange(chunks):
    count = chunks.shape[0]
    return pl.pallas_call(
        exchange_kernel,
        out_shape=jax.ShapeDtypeStruct(chunks.shape, chunks.dtype),
        in_specs=[pl.BlockSpec(memory_space=pl.ANY)],
        out_specs=pl.BlockSpec(memory_space=pl.ANY),
        scratch_shapes=[
            pltpu.SemaphoreType.DMA((count,)),
            pltpu.SemaphoreType.DMA((count,)),
            pltpu.SemaphoreType.DMA,
        ],
        compiler_params=pltpu.CompilerParams(collective_id=0, has_side_effects=True),
    )(chunks)


def to_channels(value):
    rows, channels = value.shape
    count = lax.axis_size("ctx")
    chunks = value.T.reshape(count, channels // count, rows)
    return exchange(chunks).transpose(1, 0, 2).reshape(channels // count, count * rows)


def to_rows(value):
    channels, length = value.shape
    count = lax.axis_size("ctx")
    chunks = value.reshape(channels, count, length // count).transpose(1, 0, 2)
    return exchange(chunks).reshape(count * channels, length // count).T


def body(
    token_ids,
    embed_table,
    norm_gain,
    input_weight,
    short_weight,
    filters,
    skip_gain,
    output_weight,
    output_grad,
):
    local_rows = token_ids.shape[0]
    tokens = jnp.take(embed_table, token_ids, axis=0)
    token_values = tokens.astype(jnp.float32)
    inverse_rms = lax.rsqrt(jnp.mean(token_values * token_values, axis=-1, keepdims=True) + 1e-06)
    normed = (token_values * inverse_rms * norm_gain).astype(jnp.bfloat16)
    projected = jnp.einsum("td,djc->tjc", normed, input_weight, preferred_element_type=jnp.float32)
    short_taps = short_weight.shape[0]
    before = from_behind(projected[local_rows - (short_taps - 1) :], "ctx", 1)
    extended = jnp.concatenate([before, projected], axis=0)
    features = sum(
        (
            short_weight[tap_index]
            * extended[short_taps - 1 - tap_index : short_taps - 1 - tap_index + local_rows]
            for tap_index in range(short_taps)
        )
    )
    queries = features[:, 0]
    key_part = features[:, 1]
    value_part = features[:, 2]
    mixture = key_part * value_part
    weight_rows = lax.all_to_all(output_weight, TP, 0, 1, tiled=True)
    grad_columns = lax.all_to_all(output_grad, "ctx", 1, 0, tiled=True)
    mixture, weight_rows, grad_columns = lax.optimization_barrier((mixture, weight_rows, grad_columns))

    group_taps, reversed_taps = gather_taps(filters)
    causal_matrix, anti_matrix = conv_matrices(group_taps, reversed_taps, BLOCK)
    long_part = to_rows(windowed_conv(causal_matrix, to_channels(mixture), BLOCK, True))
    mixed_out = skip_gain * mixture + long_part
    hidden = (queries * mixed_out).astype(jnp.bfloat16)

    tp_size = lax.axis_size(TP)
    width = token_values.shape[1] // tp_size
    hidden_grad = jnp.dot(output_grad, output_weight, preferred_element_type=jnp.float32)
    mixed_grad = hidden_grad * queries
    hidden, mixed_grad, weight_rows, grad_columns = lax.optimization_barrier(
        (hidden, mixed_grad, weight_rows, grad_columns)
    )
    hidden_wide = lax.all_gather(hidden, TP, axis=1, tiled=True)
    hidden_long = lax.all_gather(hidden, "ctx", axis=0, tiled=True)
    own_sums = jnp.einsum("tc,dc->td", hidden_wide, weight_rows, preferred_element_type=jnp.float32)
    own_tokens = lax.dynamic_slice_in_dim(token_values, lax.axis_index(TP) * width, width, axis=1)
    own_output = (own_tokens + own_sums).astype(jnp.bfloat16)
    block_output = lax.all_gather(own_output, TP, axis=1, tiled=True)
    output_weight_grad = jnp.einsum(
        "td,tc->dc", grad_columns, hidden_long, preferred_element_type=jnp.float32
    )
    carried = to_rows(windowed_conv(anti_matrix, to_channels(mixed_grad), BLOCK, False))
    mixture_grad = skip_gain * mixed_grad + carried
    feature_grad = jnp.stack(
        [hidden_grad * mixed_out, mixture_grad * value_part, mixture_grad * key_part], axis=1
    )
    following = from_behind(feature_grad[: short_taps - 1], "ctx", -1)
    extended_grads = jnp.concatenate([feature_grad, following], axis=0)
    projection_grad = sum(
        (
            short_weight[tap_index] * extended_grads[tap_index : tap_index + local_rows]
            for tap_index in range(short_taps)
        )
    ).astype(jnp.bfloat16)
    chips = lax.axis_size("chip")
    cores = lax.axis_size("core")
    chip_weight = lax.all_gather(input_weight, "core", axis=2, tiled=True)
    row_blocks = projection_grad.reshape(
        chips, cores, local_rows // tp_size, short_taps, projection_grad.shape[2]
    )
    chip_rows = lax.all_to_all(row_blocks, "core", 1, 4, tiled=True)[:, 0]
    partial_grad = jnp.einsum(
        "qujc,djc->qud", chip_rows, chip_weight, preferred_element_type=jnp.float32
    ).astype(jnp.bfloat16)
    received = lax.all_to_all(partial_grad, "chip", 0, 0)
    normed_grad = jnp.sum(received.astype(jnp.float32), axis=0)
    return (block_output, output_weight_grad, projection_grad, normed_grad)


def solution(mesh):
    ctx_size, tp_size = mesh.devices.shape
    devices = mesh.devices.reshape(ctx_size, tp_size // 2, 2)
    split_mesh = jax.sharding.Mesh(devices, ("ctx", "chip", "core"))
    in_specs = (
        P("ctx"),
        P(),
        P(),
        P(None, None, TP),
        P(None, None, TP),
        P(TP, "ctx"),
        P(TP),
        P(None, TP),
        P("ctx", None),
    )
    out_specs = (P("ctx", None), P("ctx", TP), P("ctx", None, TP), P(("ctx",) + TP, None))
    return jax.shard_map(body, mesh=split_mesh, in_specs=in_specs, out_specs=out_specs, check_vma=False)
```

```python
import functools

import jax
import jax.numpy as jnp
from jax import lax
from jax.experimental import pallas as pl
from jax.experimental.pallas import tpu as pltpu
from jax.sharding import PartitionSpec as P

precise = lax.Precision.HIGHEST
BLOCK = 256
TP = ("chip", "core")


def from_behind(value, axis, steps):
    count = lax.axis_size(axis)
    first, last = (max(0, -steps), min(count, count - steps))
    return lax.ppermute(value, axis, [(source, source + steps) for source in range(first, last)])


def skew_kernel(taps_ref, out_ref):
    block, length = out_ref.shape[1], out_ref.shape[2]
    wide = jnp.broadcast_to(taps_ref[0], (block, taps_ref.shape[2]))
    rolled = pltpu.roll(wide, 0, 1, stride=1, stride_axis=0)
    out_ref[0] = rolled[:, block : block + length]


def toeplitz_rows(padded, block):
    groups, _, width = padded.shape
    length = width - block
    return pl.pallas_call(
        skew_kernel,
        out_shape=jax.ShapeDtypeStruct((groups, block, length), padded.dtype),
        grid=(groups,),
        in_specs=[pl.BlockSpec((1, 1, width), lambda g: (g, 0, 0))],
        out_specs=pl.BlockSpec((1, block, length), lambda g: (g, 0, 0)),
    )(padded)


def conv_matrices(taps, reversed_taps, block):
    groups, length = taps.shape
    one = jnp.zeros((groups, 1), taps.dtype)
    causal = jnp.concatenate([one, reversed_taps, jnp.zeros((groups, block - 1), taps.dtype)], axis=1)
    anti = jnp.concatenate([jnp.zeros((groups, block), taps.dtype), taps], axis=1)
    both = toeplitz_rows(jnp.concatenate([causal, anti], axis=0)[:, None, :], block)
    return both[:groups], both[groups:]


def gather_taps(filters):
    width = filters.shape[1]
    rows = lax.broadcasted_iota(jnp.int32, (width, width), 0)
    cols = lax.broadcasted_iota(jnp.int32, (width, width), 1)
    exchange = (rows + cols == width - 1).astype(filters.dtype)
    flipped = jnp.dot(filters, exchange, precision=precise)
    both = lax.all_to_all(jnp.stack([filters, flipped]), "ctx", 1, 2, tiled=True)
    shards = lax.axis_size("ctx")
    pieces = both[1].reshape(both.shape[1], shards, width)
    reversed_taps = jnp.concatenate([pieces[:, k] for k in reversed(range(shards))], axis=1)
    return both[0], reversed_taps


def conv_kernel(causal, x_ref, m_ref, o_ref):
    count, channels, rows = x_ref.shape
    block, length = m_ref.shape[1], m_ref.shape[2]
    signal = jnp.concatenate([x_ref[k] for k in range(count)], axis=1)
    zeros = jnp.zeros((channels, length - block), signal.dtype)
    padded = jnp.concatenate([zeros, signal] if causal else [signal, zeros], axis=1)
    steps = length // block
    windows = jnp.concatenate(
        [padded[:, i * block : i * block + length] for i in range(steps)], axis=0
    )
    result = lax.dot_general(
        windows, m_ref[0], (((1,), (1,)), ((), ())),
        precision=precise, preferred_element_type=jnp.float32,
    )
    line = jnp.concatenate(
        [result[i * channels : (i + 1) * channels] for i in range(steps)], axis=1
    )
    for k in range(count):
        o_ref[k] = line[:, k * rows : (k + 1) * rows]


def windowed_conv(matrix, chunks, causal):
    count, channels, rows = chunks.shape
    groups, block, length = matrix.shape
    width = channels // groups
    return pl.pallas_call(
        functools.partial(conv_kernel, causal),
        out_shape=jax.ShapeDtypeStruct(chunks.shape, chunks.dtype),
        grid=(groups,),
        in_specs=[
            pl.BlockSpec((count, width, rows), lambda g: (0, g, 0)),
            pl.BlockSpec((1, block, length), lambda g: (g, 0, 0)),
        ],
        out_specs=pl.BlockSpec((count, width, rows), lambda g: (0, g, 0)),
    )(chunks, matrix)


def exchange_kernel(x_ref, o_ref, send_sems, recv_sems, local_sem):
    count = x_ref.shape[0]
    me = lax.axis_index("ctx")
    chip = lax.axis_index("chip")
    core = lax.axis_index("core")
    mesh_id = pl.DeviceIdType.MESH
    barrier = pltpu.get_barrier_semaphore()
    for offset in range(1, count):
        peer = lax.rem(me + offset, count)
        pl.semaphore_signal(barrier, 1, device_id=(peer, chip, core), device_id_type=mesh_id)
    pl.semaphore_wait(barrier, count - 1)
    local = pltpu.make_async_copy(x_ref.at[me], o_ref.at[me], local_sem)
    local.start()
    sends = []
    for offset in range(1, count):
        peer = lax.rem(me + offset, count)
        copy = pltpu.make_async_remote_copy(
            src_ref=x_ref.at[peer],
            dst_ref=o_ref.at[me],
            send_sem=send_sems.at[offset],
            recv_sem=recv_sems.at[offset],
            device_id=(peer, chip, core),
            device_id_type=mesh_id,
        )
        copy.start()
        sends.append(copy)
    for copy in sends:
        copy.wait_send()
    for offset in range(1, count):
        source = lax.rem(me + count - offset, count)
        pltpu.make_async_remote_copy(
            src_ref=x_ref.at[source],
            dst_ref=o_ref.at[source],
            send_sem=send_sems.at[offset],
            recv_sem=recv_sems.at[offset],
            device_id=(source, chip, core),
            device_id_type=mesh_id,
        ).wait_recv()
    local.wait()


def exchange(chunks):
    count = chunks.shape[0]
    return pl.pallas_call(
        exchange_kernel,
        out_shape=jax.ShapeDtypeStruct(chunks.shape, chunks.dtype),
        in_specs=[pl.BlockSpec(memory_space=pl.ANY)],
        out_specs=pl.BlockSpec(memory_space=pl.ANY),
        scratch_shapes=[
            pltpu.SemaphoreType.DMA((count,)),
            pltpu.SemaphoreType.DMA((count,)),
            pltpu.SemaphoreType.DMA,
        ],
        compiler_params=pltpu.CompilerParams(collective_id=0, has_side_effects=True),
    )(chunks)


def to_channels(value):
    rows, channels = value.shape
    count = lax.axis_size("ctx")
    return exchange(value.T.reshape(count, channels // count, rows))


def to_rows(chunks):
    count, channels, rows = chunks.shape
    return exchange(chunks).reshape(count * channels, rows).T


def body(
    token_ids,
    embed_table,
    norm_gain,
    input_weight,
    short_weight,
    filters,
    skip_gain,
    output_weight,
    output_grad,
):
    local_rows = token_ids.shape[0]
    tokens = jnp.take(embed_table, token_ids, axis=0)
    token_values = tokens.astype(jnp.float32)
    inverse_rms = lax.rsqrt(jnp.mean(token_values * token_values, axis=-1, keepdims=True) + 1e-06)
    normed = (token_values * inverse_rms * norm_gain).astype(jnp.bfloat16)
    projected = jnp.einsum("td,djc->tjc", normed, input_weight, preferred_element_type=jnp.float32)
    short_taps = short_weight.shape[0]
    before = from_behind(projected[local_rows - (short_taps - 1) :], "ctx", 1)
    extended = jnp.concatenate([before, projected], axis=0)
    features = sum(
        (
            short_weight[tap_index]
            * extended[short_taps - 1 - tap_index : short_taps - 1 - tap_index + local_rows]
            for tap_index in range(short_taps)
        )
    )
    queries = features[:, 0]
    key_part = features[:, 1]
    value_part = features[:, 2]
    mixture = key_part * value_part
    weight_rows = lax.all_to_all(output_weight, TP, 0, 1, tiled=True)
    grad_columns = lax.all_to_all(output_grad, "ctx", 1, 0, tiled=True)
    mixture, weight_rows, grad_columns = lax.optimization_barrier((mixture, weight_rows, grad_columns))

    group_taps, reversed_taps = gather_taps(filters)
    causal_matrix, anti_matrix = conv_matrices(group_taps, reversed_taps, BLOCK)
    long_part = to_rows(windowed_conv(causal_matrix, to_channels(mixture), True))
    mixed_out = skip_gain * mixture + long_part
    hidden = (queries * mixed_out).astype(jnp.bfloat16)

    tp_size = lax.axis_size(TP)
    width = token_values.shape[1] // tp_size
    hidden_grad = jnp.dot(output_grad, output_weight, preferred_element_type=jnp.float32)
    mixed_grad = hidden_grad * queries
    hidden, mixed_grad, weight_rows, grad_columns = lax.optimization_barrier(
        (hidden, mixed_grad, weight_rows, grad_columns)
    )
    hidden_wide = lax.all_gather(hidden, TP, axis=1, tiled=True)
    hidden_long = lax.all_gather(hidden, "ctx", axis=0, tiled=True)
    own_sums = jnp.einsum("tc,dc->td", hidden_wide, weight_rows, preferred_element_type=jnp.float32)
    own_tokens = lax.dynamic_slice_in_dim(token_values, lax.axis_index(TP) * width, width, axis=1)
    own_output = (own_tokens + own_sums).astype(jnp.bfloat16)
    block_output = lax.all_gather(own_output, TP, axis=1, tiled=True)
    output_weight_grad = jnp.einsum(
        "td,tc->dc", grad_columns, hidden_long, preferred_element_type=jnp.float32
    )
    carried = to_rows(windowed_conv(anti_matrix, to_channels(mixed_grad), False))
    mixture_grad = skip_gain * mixed_grad + carried
    feature_grad = jnp.stack(
        [hidden_grad * mixed_out, mixture_grad * value_part, mixture_grad * key_part], axis=1
    )
    following = from_behind(feature_grad[: short_taps - 1], "ctx", -1)
    extended_grads = jnp.concatenate([feature_grad, following], axis=0)
    projection_grad = sum(
        (
            short_weight[tap_index] * extended_grads[tap_index : tap_index + local_rows]
            for tap_index in range(short_taps)
        )
    ).astype(jnp.bfloat16)
    chips = lax.axis_size("chip")
    cores = lax.axis_size("core")
    chip_weight = lax.all_gather(input_weight, "core", axis=2, tiled=True)
    row_blocks = projection_grad.reshape(
        chips, cores, local_rows // tp_size, short_taps, projection_grad.shape[2]
    )
    chip_rows = lax.all_to_all(row_blocks, "core", 1, 4, tiled=True)[:, 0]
    partial_grad = jnp.einsum(
        "qujc,djc->qud", chip_rows, chip_weight, preferred_element_type=jnp.float32
    ).astype(jnp.bfloat16)
    received = lax.all_to_all(partial_grad, "chip", 0, 0)
    normed_grad = jnp.sum(received.astype(jnp.float32), axis=0)
    return (block_output, output_weight_grad, projection_grad, normed_grad)


def solution(mesh):
    ctx_size, tp_size = mesh.devices.shape
    devices = mesh.devices.reshape(ctx_size, tp_size // 2, 2)
    split_mesh = jax.sharding.Mesh(devices, ("ctx", "chip", "core"))
    in_specs = (
        P("ctx"),
        P(),
        P(),
        P(None, None, TP),
        P(None, None, TP),
        P(TP, "ctx"),
        P(TP),
        P(None, TP),
        P("ctx", None),
    )
    out_specs = (P("ctx", None), P("ctx", TP), P("ctx", None, TP), P(("ctx",) + TP, None))
    return jax.shard_map(body, mesh=split_mesh, in_specs=in_specs, out_specs=out_specs, check_vma=False)
```

```python
import functools

import jax
import jax.numpy as jnp
from jax import lax
from jax.experimental import pallas as pl
from jax.experimental.pallas import tpu as pltpu
from jax.sharding import PartitionSpec as P

precise = lax.Precision.HIGHEST
BLOCK = 256
TP = ("chip", "core")


def from_behind(value, axis, steps):
    count = lax.axis_size(axis)
    first, last = (max(0, -steps), min(count, count - steps))
    return lax.ppermute(value, axis, [(source, source + steps) for source in range(first, last)])


def skew_kernel(taps_ref, out_ref):
    block, length = out_ref.shape[1], out_ref.shape[2]
    wide = jnp.broadcast_to(taps_ref[0], (block, taps_ref.shape[2]))
    rolled = pltpu.roll(wide, 0, 1, stride=1, stride_axis=0)
    out_ref[0] = rolled[:, block : block + length]


def toeplitz_rows(padded, block):
    groups, _, width = padded.shape
    length = width - block
    return pl.pallas_call(
        skew_kernel,
        out_shape=jax.ShapeDtypeStruct((groups, block, length), padded.dtype),
        grid=(groups,),
        in_specs=[pl.BlockSpec((1, 1, width), lambda g: (g, 0, 0))],
        out_specs=pl.BlockSpec((1, block, length), lambda g: (g, 0, 0)),
    )(padded)


def conv_matrices(taps, reversed_taps, block):
    groups, length = taps.shape
    one = jnp.zeros((groups, 1), taps.dtype)
    causal = jnp.concatenate([one, reversed_taps, jnp.zeros((groups, block - 1), taps.dtype)], axis=1)
    anti = jnp.concatenate([jnp.zeros((groups, block), taps.dtype), taps], axis=1)
    both = toeplitz_rows(jnp.concatenate([causal, anti], axis=0)[:, None, :], block)
    return both[:groups], both[groups:]


def gather_taps(filters):
    width = filters.shape[1]
    rows = lax.broadcasted_iota(jnp.int32, (width, width), 0)
    cols = lax.broadcasted_iota(jnp.int32, (width, width), 1)
    exchange = (rows + cols == width - 1).astype(filters.dtype)
    flipped = jnp.dot(filters, exchange, precision=precise)
    both = lax.all_to_all(jnp.stack([filters, flipped]), "ctx", 1, 2, tiled=True)
    shards = lax.axis_size("ctx")
    pieces = both[1].reshape(both.shape[1], shards, width)
    reversed_taps = jnp.concatenate([pieces[:, k] for k in reversed(range(shards))], axis=1)
    return both[0], reversed_taps


def conv_kernel(causal, x_ref, m_ref, o_ref):
    count, channels, rows = x_ref.shape
    block, length = m_ref.shape[1], m_ref.shape[2]
    signal = jnp.concatenate([x_ref[k] for k in range(count)], axis=1)
    zeros = jnp.zeros((channels, length - block), signal.dtype)
    padded = jnp.concatenate([zeros, signal] if causal else [signal, zeros], axis=1)
    steps = length // block
    windows = jnp.concatenate(
        [padded[:, i * block : i * block + length] for i in range(steps)], axis=0
    )
    result = lax.dot_general(
        windows, m_ref[0], (((1,), (1,)), ((), ())),
        precision=precise, preferred_element_type=jnp.float32,
    )
    line = jnp.concatenate(
        [result[i * channels : (i + 1) * channels] for i in range(steps)], axis=1
    )
    for k in range(count):
        o_ref[k] = line[:, k * rows : (k + 1) * rows]


def windowed_conv(matrix, chunks, causal):
    count, channels, rows = chunks.shape
    groups, block, length = matrix.shape
    width = channels // groups
    return pl.pallas_call(
        functools.partial(conv_kernel, causal),
        out_shape=jax.ShapeDtypeStruct(chunks.shape, chunks.dtype),
        grid=(groups,),
        in_specs=[
            pl.BlockSpec((count, width, rows), lambda g: (0, g, 0)),
            pl.BlockSpec((1, block, length), lambda g: (g, 0, 0)),
        ],
        out_specs=pl.BlockSpec((count, width, rows), lambda g: (0, g, 0)),
    )(chunks, matrix)


def exchange_kernel(x_ref, o_ref, send_sems, recv_sems, local_sem):
    count = x_ref.shape[0]
    me = lax.axis_index("ctx")
    chip = lax.axis_index("chip")
    core = lax.axis_index("core")
    mesh_id = pl.DeviceIdType.MESH
    barrier = pltpu.get_barrier_semaphore()
    for offset in range(1, count):
        peer = lax.rem(me + offset, count)
        pl.semaphore_signal(barrier, 1, device_id=(peer, chip, core), device_id_type=mesh_id)
    pl.semaphore_wait(barrier, count - 1)
    local = pltpu.make_async_copy(x_ref.at[me], o_ref.at[me], local_sem)
    local.start()
    sends = []
    for offset in range(1, count):
        peer = lax.rem(me + offset, count)
        copy = pltpu.make_async_remote_copy(
            src_ref=x_ref.at[peer],
            dst_ref=o_ref.at[me],
            send_sem=send_sems.at[offset],
            recv_sem=recv_sems.at[offset],
            device_id=(peer, chip, core),
            device_id_type=mesh_id,
        )
        copy.start()
        sends.append(copy)
    for copy in sends:
        copy.wait_send()
    for offset in range(1, count):
        source = lax.rem(me + count - offset, count)
        pltpu.make_async_remote_copy(
            src_ref=x_ref.at[source],
            dst_ref=o_ref.at[source],
            send_sem=send_sems.at[offset],
            recv_sem=recv_sems.at[offset],
            device_id=(source, chip, core),
            device_id_type=mesh_id,
        ).wait_recv()
    local.wait()


def exchange(chunks):
    count = chunks.shape[0]
    return pl.pallas_call(
        exchange_kernel,
        out_shape=jax.ShapeDtypeStruct(chunks.shape, chunks.dtype),
        in_specs=[pl.BlockSpec(memory_space=pl.ANY)],
        out_specs=pl.BlockSpec(memory_space=pl.ANY),
        scratch_shapes=[
            pltpu.SemaphoreType.DMA((count,)),
            pltpu.SemaphoreType.DMA((count,)),
            pltpu.SemaphoreType.DMA,
        ],
        compiler_params=pltpu.CompilerParams(collective_id=0, has_side_effects=True),
    )(chunks)


def gather_kernel(x_ref, o_ref, send_sems, recv_sems, local_sem):
    count = o_ref.shape[0]
    me = lax.axis_index("ctx")
    chip = lax.axis_index("chip")
    core = lax.axis_index("core")
    mesh_id = pl.DeviceIdType.MESH
    barrier = pltpu.get_barrier_semaphore()
    for offset in range(1, count):
        peer = lax.rem(me + offset, count)
        pl.semaphore_signal(barrier, 1, device_id=(peer, chip, core), device_id_type=mesh_id)
    pl.semaphore_wait(barrier, count - 1)
    local = pltpu.make_async_copy(x_ref, o_ref.at[me], local_sem)
    local.start()
    sends = []
    for offset in range(1, count):
        peer = lax.rem(me + offset, count)
        copy = pltpu.make_async_remote_copy(
            src_ref=x_ref,
            dst_ref=o_ref.at[me],
            send_sem=send_sems.at[offset],
            recv_sem=recv_sems.at[offset],
            device_id=(peer, chip, core),
            device_id_type=mesh_id,
        )
        copy.start()
        sends.append(copy)
    for copy in sends:
        copy.wait_send()
    for offset in range(1, count):
        source = lax.rem(me + count - offset, count)
        pltpu.make_async_remote_copy(
            src_ref=x_ref,
            dst_ref=o_ref.at[source],
            send_sem=send_sems.at[offset],
            recv_sem=recv_sems.at[offset],
            device_id=(source, chip, core),
            device_id_type=mesh_id,
        ).wait_recv()
    local.wait()


def gather_ctx(value):
    count = lax.axis_size("ctx")
    gathered = pl.pallas_call(
        gather_kernel,
        out_shape=jax.ShapeDtypeStruct((count,) + value.shape, value.dtype),
        in_specs=[pl.BlockSpec(memory_space=pl.ANY)],
        out_specs=pl.BlockSpec(memory_space=pl.ANY),
        scratch_shapes=[
            pltpu.SemaphoreType.DMA((count,)),
            pltpu.SemaphoreType.DMA((count,)),
            pltpu.SemaphoreType.DMA,
        ],
        compiler_params=pltpu.CompilerParams(collective_id=1, has_side_effects=True),
    )(value)
    return gathered.reshape((count * value.shape[0],) + value.shape[1:])


def to_channels(value):
    rows, channels = value.shape
    count = lax.axis_size("ctx")
    return exchange(value.T.reshape(count, channels // count, rows))


def to_rows(chunks):
    count, channels, rows = chunks.shape
    return exchange(chunks).reshape(count * channels, rows).T


def body(
    token_ids,
    embed_table,
    norm_gain,
    input_weight,
    short_weight,
    filters,
    skip_gain,
    output_weight,
    output_grad,
):
    local_rows = token_ids.shape[0]
    tokens = jnp.take(embed_table, token_ids, axis=0)
    token_values = tokens.astype(jnp.float32)
    inverse_rms = lax.rsqrt(jnp.mean(token_values * token_values, axis=-1, keepdims=True) + 1e-06)
    normed = (token_values * inverse_rms * norm_gain).astype(jnp.bfloat16)
    projected = jnp.einsum("td,djc->tjc", normed, input_weight, preferred_element_type=jnp.float32)
    short_taps = short_weight.shape[0]
    before = from_behind(projected[local_rows - (short_taps - 1) :], "ctx", 1)
    extended = jnp.concatenate([before, projected], axis=0)
    features = sum(
        (
            short_weight[tap_index]
            * extended[short_taps - 1 - tap_index : short_taps - 1 - tap_index + local_rows]
            for tap_index in range(short_taps)
        )
    )
    queries = features[:, 0]
    key_part = features[:, 1]
    value_part = features[:, 2]
    mixture = key_part * value_part
    weight_rows = lax.all_to_all(output_weight, TP, 0, 1, tiled=True)
    grad_columns = lax.all_to_all(output_grad, "ctx", 1, 0, tiled=True)
    mixture, weight_rows, grad_columns = lax.optimization_barrier((mixture, weight_rows, grad_columns))

    group_taps, reversed_taps = gather_taps(filters)
    causal_matrix, anti_matrix = conv_matrices(group_taps, reversed_taps, BLOCK)
    long_part = to_rows(windowed_conv(causal_matrix, to_channels(mixture), True))
    mixed_out = skip_gain * mixture + long_part
    hidden = (queries * mixed_out).astype(jnp.bfloat16)

    tp_size = lax.axis_size(TP)
    width = token_values.shape[1] // tp_size
    hidden_grad = jnp.dot(output_grad, output_weight, preferred_element_type=jnp.float32)
    mixed_grad = hidden_grad * queries
    hidden, mixed_grad, weight_rows, grad_columns = lax.optimization_barrier(
        (hidden, mixed_grad, weight_rows, grad_columns)
    )
    hidden_wide = lax.all_gather(hidden, TP, axis=1, tiled=True)
    hidden_long = gather_ctx(hidden)
    carried = to_rows(windowed_conv(anti_matrix, to_channels(mixed_grad), False))
    hidden_wide, carried = lax.optimization_barrier((hidden_wide, carried))
    own_sums = jnp.einsum("tc,dc->td", hidden_wide, weight_rows, preferred_element_type=jnp.float32)
    own_tokens = lax.dynamic_slice_in_dim(token_values, lax.axis_index(TP) * width, width, axis=1)
    own_output = (own_tokens + own_sums).astype(jnp.bfloat16)
    block_output = lax.all_gather(own_output, TP, axis=1, tiled=True)
    output_weight_grad = jnp.einsum(
        "td,tc->dc", grad_columns, hidden_long, preferred_element_type=jnp.float32
    )
    mixture_grad = skip_gain * mixed_grad + carried
    feature_grad = jnp.stack(
        [hidden_grad * mixed_out, mixture_grad * value_part, mixture_grad * key_part], axis=1
    )
    following = from_behind(feature_grad[: short_taps - 1], "ctx", -1)
    extended_grads = jnp.concatenate([feature_grad, following], axis=0)
    projection_grad = sum(
        (
            short_weight[tap_index] * extended_grads[tap_index : tap_index + local_rows]
            for tap_index in range(short_taps)
        )
    ).astype(jnp.bfloat16)
    chips = lax.axis_size("chip")
    cores = lax.axis_size("core")
    chip_weight = lax.all_gather(input_weight, "core", axis=2, tiled=True)
    row_blocks = projection_grad.reshape(
        chips, cores, local_rows // tp_size, short_taps, projection_grad.shape[2]
    )
    chip_rows = lax.all_to_all(row_blocks, "core", 1, 4, tiled=True)[:, 0]
    partial_grad = jnp.einsum(
        "qujc,djc->qud", chip_rows, chip_weight, preferred_element_type=jnp.float32
    ).astype(jnp.bfloat16)
    received = lax.all_to_all(partial_grad, "chip", 0, 0)
    normed_grad = jnp.sum(received.astype(jnp.float32), axis=0)
    return (block_output, output_weight_grad, projection_grad, normed_grad)


def solution(mesh):
    ctx_size, tp_size = mesh.devices.shape
    devices = mesh.devices.reshape(ctx_size, tp_size // 2, 2)
    split_mesh = jax.sharding.Mesh(devices, ("ctx", "chip", "core"))
    in_specs = (
        P("ctx"),
        P(),
        P(),
        P(None, None, TP),
        P(None, None, TP),
        P(TP, "ctx"),
        P(TP),
        P(None, TP),
        P("ctx", None),
    )
    out_specs = (P("ctx", None), P("ctx", TP), P("ctx", None, TP), P(("ctx",) + TP, None))
    return jax.shard_map(body, mesh=split_mesh, in_specs=in_specs, out_specs=out_specs, check_vma=False)
```

```python
import functools

import jax
import jax.numpy as jnp
from jax import lax
from jax.experimental import pallas as pl
from jax.experimental.pallas import tpu as pltpu
from jax.sharding import PartitionSpec as P

precise = lax.Precision.HIGHEST
BLOCK = 256
TP = ("chip", "core")


def from_behind(value, axis, steps):
    count = lax.axis_size(axis)
    first, last = (max(0, -steps), min(count, count - steps))
    return lax.ppermute(value, axis, [(source, source + steps) for source in range(first, last)])


def skew_kernel(taps_ref, out_ref):
    block, length = out_ref.shape[1], out_ref.shape[2]
    wide = jnp.broadcast_to(taps_ref[0], (block, taps_ref.shape[2]))
    rolled = pltpu.roll(wide, 0, 1, stride=1, stride_axis=0)
    out_ref[0] = rolled[:, block : block + length]


def toeplitz_rows(padded, block):
    groups, _, width = padded.shape
    length = width - block
    return pl.pallas_call(
        skew_kernel,
        out_shape=jax.ShapeDtypeStruct((groups, block, length), padded.dtype),
        grid=(groups,),
        in_specs=[pl.BlockSpec((1, 1, width), lambda g: (g, 0, 0))],
        out_specs=pl.BlockSpec((1, block, length), lambda g: (g, 0, 0)),
    )(padded)


def conv_matrices(taps, reversed_taps, block):
    groups, length = taps.shape
    one = jnp.zeros((groups, 1), taps.dtype)
    causal = jnp.concatenate([one, reversed_taps, jnp.zeros((groups, block - 1), taps.dtype)], axis=1)
    anti = jnp.concatenate([jnp.zeros((groups, block), taps.dtype), taps], axis=1)
    both = toeplitz_rows(jnp.concatenate([causal, anti], axis=0)[:, None, :], block)
    return both[:groups], both[groups:]


def gather_taps(filters):
    width = filters.shape[1]
    rows = lax.broadcasted_iota(jnp.int32, (width, width), 0)
    cols = lax.broadcasted_iota(jnp.int32, (width, width), 1)
    exchange = (rows + cols == width - 1).astype(filters.dtype)
    flipped = jnp.dot(filters, exchange, precision=precise)
    both = lax.all_to_all(jnp.stack([filters, flipped]), "ctx", 1, 2, tiled=True)
    shards = lax.axis_size("ctx")
    pieces = both[1].reshape(both.shape[1], shards, width)
    reversed_taps = jnp.concatenate([pieces[:, k] for k in reversed(range(shards))], axis=1)
    return both[0], reversed_taps


def conv_kernel(causal, x_ref, m_ref, o_ref):
    count, channels, rows = x_ref.shape
    block, length = m_ref.shape[1], m_ref.shape[2]
    signal = jnp.concatenate([x_ref[k] for k in range(count)], axis=1)
    zeros = jnp.zeros((channels, length - block), signal.dtype)
    padded = jnp.concatenate([zeros, signal] if causal else [signal, zeros], axis=1)
    steps = length // block
    windows = jnp.concatenate(
        [padded[:, i * block : i * block + length] for i in range(steps)], axis=0
    )
    result = lax.dot_general(
        windows, m_ref[0], (((1,), (1,)), ((), ())),
        precision=precise, preferred_element_type=jnp.float32,
    )
    line = jnp.concatenate(
        [result[i * channels : (i + 1) * channels] for i in range(steps)], axis=1
    )
    for k in range(count):
        o_ref[k] = line[:, k * rows : (k + 1) * rows]


def windowed_conv(matrix, chunks, causal):
    count, channels, rows = chunks.shape
    groups, block, length = matrix.shape
    width = channels // groups
    return pl.pallas_call(
        functools.partial(conv_kernel, causal),
        out_shape=jax.ShapeDtypeStruct(chunks.shape, chunks.dtype),
        grid=(groups,),
        in_specs=[
            pl.BlockSpec((count, width, rows), lambda g: (0, g, 0)),
            pl.BlockSpec((1, block, length), lambda g: (g, 0, 0)),
        ],
        out_specs=pl.BlockSpec((count, width, rows), lambda g: (0, g, 0)),
    )(chunks, matrix)


def exchange_kernel(x_ref, o_ref, send_sems, recv_sems, local_sem):
    count = x_ref.shape[0]
    me = lax.axis_index("ctx")
    chip = lax.axis_index("chip")
    core = lax.axis_index("core")
    mesh_id = pl.DeviceIdType.MESH
    barrier = pltpu.get_barrier_semaphore()
    for offset in range(1, count):
        peer = lax.rem(me + offset, count)
        pl.semaphore_signal(barrier, 1, device_id=(peer, chip, core), device_id_type=mesh_id)
    pl.semaphore_wait(barrier, count - 1)
    local = pltpu.make_async_copy(x_ref.at[me], o_ref.at[me], local_sem)
    local.start()
    sends = []
    for offset in range(1, count):
        peer = lax.rem(me + offset, count)
        copy = pltpu.make_async_remote_copy(
            src_ref=x_ref.at[peer],
            dst_ref=o_ref.at[me],
            send_sem=send_sems.at[offset],
            recv_sem=recv_sems.at[offset],
            device_id=(peer, chip, core),
            device_id_type=mesh_id,
        )
        copy.start()
        sends.append(copy)
    for copy in sends:
        copy.wait_send()
    for offset in range(1, count):
        source = lax.rem(me + count - offset, count)
        pltpu.make_async_remote_copy(
            src_ref=x_ref.at[source],
            dst_ref=o_ref.at[source],
            send_sem=send_sems.at[offset],
            recv_sem=recv_sems.at[offset],
            device_id=(source, chip, core),
            device_id_type=mesh_id,
        ).wait_recv()
    local.wait()


def exchange(chunks):
    count = chunks.shape[0]
    return pl.pallas_call(
        exchange_kernel,
        out_shape=jax.ShapeDtypeStruct(chunks.shape, chunks.dtype),
        in_specs=[pl.BlockSpec(memory_space=pl.ANY)],
        out_specs=pl.BlockSpec(memory_space=pl.ANY),
        scratch_shapes=[
            pltpu.SemaphoreType.DMA((count,)),
            pltpu.SemaphoreType.DMA((count,)),
            pltpu.SemaphoreType.DMA,
        ],
        compiler_params=pltpu.CompilerParams(collective_id=0, has_side_effects=True),
    )(chunks)


def gather_kernel(x_ref, o_ref, send_sems, recv_sems, local_sem):
    count = o_ref.shape[0]
    me = lax.axis_index("ctx")
    chip = lax.axis_index("chip")
    core = lax.axis_index("core")
    mesh_id = pl.DeviceIdType.MESH
    barrier = pltpu.get_barrier_semaphore()
    for offset in range(1, count):
        peer = lax.rem(me + offset, count)
        pl.semaphore_signal(barrier, 1, device_id=(peer, chip, core), device_id_type=mesh_id)
    pl.semaphore_wait(barrier, count - 1)
    local = pltpu.make_async_copy(x_ref, o_ref.at[me], local_sem)
    local.start()
    sends = []
    for offset in range(1, count):
        peer = lax.rem(me + offset, count)
        copy = pltpu.make_async_remote_copy(
            src_ref=x_ref,
            dst_ref=o_ref.at[me],
            send_sem=send_sems.at[offset],
            recv_sem=recv_sems.at[offset],
            device_id=(peer, chip, core),
            device_id_type=mesh_id,
        )
        copy.start()
        sends.append(copy)
    for copy in sends:
        copy.wait_send()
    for offset in range(1, count):
        source = lax.rem(me + count - offset, count)
        pltpu.make_async_remote_copy(
            src_ref=x_ref,
            dst_ref=o_ref.at[source],
            send_sem=send_sems.at[offset],
            recv_sem=recv_sems.at[offset],
            device_id=(source, chip, core),
            device_id_type=mesh_id,
        ).wait_recv()
    local.wait()


def gather_ctx(value):
    count = lax.axis_size("ctx")
    gathered = pl.pallas_call(
        gather_kernel,
        out_shape=jax.ShapeDtypeStruct((count,) + value.shape, value.dtype),
        in_specs=[pl.BlockSpec(memory_space=pl.ANY)],
        out_specs=pl.BlockSpec(memory_space=pl.ANY),
        scratch_shapes=[
            pltpu.SemaphoreType.DMA((count,)),
            pltpu.SemaphoreType.DMA((count,)),
            pltpu.SemaphoreType.DMA,
        ],
        compiler_params=pltpu.CompilerParams(collective_id=1, has_side_effects=True),
    )(value)
    return gathered.reshape((count * value.shape[0],) + value.shape[1:])


def to_channels(value):
    rows, channels = value.shape
    count = lax.axis_size("ctx")
    return exchange(value.T.reshape(count, channels // count, rows))


def to_rows(chunks):
    count, channels, rows = chunks.shape
    return exchange(chunks).reshape(count * channels, rows).T


def body(
    token_ids,
    embed_table,
    norm_gain,
    input_weight,
    short_weight,
    filters,
    skip_gain,
    output_weight,
    output_grad,
):
    local_rows = token_ids.shape[0]
    tokens = jnp.take(embed_table, token_ids, axis=0)
    token_values = tokens.astype(jnp.float32)
    inverse_rms = lax.rsqrt(jnp.mean(token_values * token_values, axis=-1, keepdims=True) + 1e-06)
    normed = (token_values * inverse_rms * norm_gain).astype(jnp.bfloat16)
    projected = jnp.einsum("td,djc->tjc", normed, input_weight, preferred_element_type=jnp.float32)
    short_taps = short_weight.shape[0]
    before = from_behind(projected[local_rows - (short_taps - 1) :], "ctx", 1)
    extended = jnp.concatenate([before, projected], axis=0)
    features = sum(
        (
            short_weight[tap_index]
            * extended[short_taps - 1 - tap_index : short_taps - 1 - tap_index + local_rows]
            for tap_index in range(short_taps)
        )
    )
    queries = features[:, 0]
    key_part = features[:, 1]
    value_part = features[:, 2]
    mixture = key_part * value_part
    weight_rows = lax.all_to_all(output_weight, TP, 0, 1, tiled=True)
    grad_columns = lax.all_to_all(output_grad, "ctx", 1, 0, tiled=True)
    chip_weight = lax.all_gather(input_weight, "core", axis=2, tiled=True)
    mixture, weight_rows, grad_columns, chip_weight = lax.optimization_barrier(
        (mixture, weight_rows, grad_columns, chip_weight)
    )

    group_taps, reversed_taps = gather_taps(filters)
    causal_matrix, anti_matrix = conv_matrices(group_taps, reversed_taps, BLOCK)
    long_part = to_rows(windowed_conv(causal_matrix, to_channels(mixture), True))
    mixed_out = skip_gain * mixture + long_part
    hidden = (queries * mixed_out).astype(jnp.bfloat16)

    tp_size = lax.axis_size(TP)
    width = token_values.shape[1] // tp_size
    hidden_grad = jnp.dot(output_grad, output_weight, preferred_element_type=jnp.float32)
    mixed_grad = hidden_grad * queries
    hidden, mixed_grad, weight_rows, grad_columns = lax.optimization_barrier(
        (hidden, mixed_grad, weight_rows, grad_columns)
    )
    hidden_wide = lax.all_gather(hidden, TP, axis=1, tiled=True)
    hidden_long, mixed_grad = lax.optimization_barrier((gather_ctx(hidden), mixed_grad))
    carried = to_rows(windowed_conv(anti_matrix, to_channels(mixed_grad), False))
    hidden_wide, carried = lax.optimization_barrier((hidden_wide, carried))
    own_sums = jnp.einsum("tc,dc->td", hidden_wide, weight_rows, preferred_element_type=jnp.float32)
    own_tokens = lax.dynamic_slice_in_dim(token_values, lax.axis_index(TP) * width, width, axis=1)
    own_output = (own_tokens + own_sums).astype(jnp.bfloat16)
    block_output = lax.all_gather(own_output, TP, axis=1, tiled=True)
    output_weight_grad = jnp.einsum(
        "td,tc->dc", grad_columns, hidden_long, preferred_element_type=jnp.float32
    )
    mixture_grad = skip_gain * mixed_grad + carried
    feature_grad = jnp.stack(
        [hidden_grad * mixed_out, mixture_grad * value_part, mixture_grad * key_part], axis=1
    )
    following = from_behind(feature_grad[: short_taps - 1], "ctx", -1)
    extended_grads = jnp.concatenate([feature_grad, following], axis=0)
    projection_grad = sum(
        (
            short_weight[tap_index] * extended_grads[tap_index : tap_index + local_rows]
            for tap_index in range(short_taps)
        )
    ).astype(jnp.bfloat16)
    chips = lax.axis_size("chip")
    cores = lax.axis_size("core")
    row_blocks = projection_grad.reshape(
        chips, cores, local_rows // tp_size, short_taps, projection_grad.shape[2]
    )
    chip_rows = lax.all_to_all(row_blocks, "core", 1, 4, tiled=True)[:, 0]
    partial_grad = jnp.einsum(
        "qujc,djc->qud", chip_rows, chip_weight, preferred_element_type=jnp.float32
    ).astype(jnp.bfloat16)
    received = lax.all_to_all(partial_grad, "chip", 0, 0)
    normed_grad = jnp.sum(received.astype(jnp.float32), axis=0)
    return (block_output, output_weight_grad, projection_grad, normed_grad)


def solution(mesh):
    ctx_size, tp_size = mesh.devices.shape
    devices = mesh.devices.reshape(ctx_size, tp_size // 2, 2)
    split_mesh = jax.sharding.Mesh(devices, ("ctx", "chip", "core"))
    in_specs = (
        P("ctx"),
        P(),
        P(),
        P(None, None, TP),
        P(None, None, TP),
        P(TP, "ctx"),
        P(TP),
        P(None, TP),
        P("ctx", None),
    )
    out_specs = (P("ctx", None), P("ctx", TP), P("ctx", None, TP), P(("ctx",) + TP, None))
    return jax.shard_map(body, mesh=split_mesh, in_specs=in_specs, out_specs=out_specs, check_vma=False)
```

```python
import functools

import jax
import jax.numpy as jnp
from jax import lax
from jax.experimental import pallas as pl
from jax.experimental.pallas import tpu as pltpu
from jax.sharding import PartitionSpec as P

precise = lax.Precision.HIGHEST
BLOCK = 256
TP = ("chip", "core")


def from_behind(value, axis, steps):
    count = lax.axis_size(axis)
    first, last = (max(0, -steps), min(count, count - steps))
    return lax.ppermute(value, axis, [(source, source + steps) for source in range(first, last)])


def conv_taps(taps, reversed_taps, block):
    groups, length = taps.shape
    one = jnp.zeros((groups, 1), taps.dtype)
    causal = jnp.concatenate([one, reversed_taps, jnp.zeros((groups, block - 1), taps.dtype)], axis=1)
    anti = jnp.concatenate([jnp.zeros((groups, block), taps.dtype), taps], axis=1)
    return causal[:, None, :], anti[:, None, :]


def gather_taps(filters):
    width = filters.shape[1]
    rows = lax.broadcasted_iota(jnp.int32, (width, width), 0)
    cols = lax.broadcasted_iota(jnp.int32, (width, width), 1)
    exchange = (rows + cols == width - 1).astype(filters.dtype)
    flipped = jnp.dot(filters, exchange, precision=precise)
    both = lax.all_to_all(jnp.stack([filters, flipped]), "ctx", 1, 2, tiled=True)
    shards = lax.axis_size("ctx")
    pieces = both[1].reshape(both.shape[1], shards, width)
    reversed_taps = jnp.concatenate([pieces[:, k] for k in reversed(range(shards))], axis=1)
    return both[0], reversed_taps


def conv_kernel(causal, block, x_ref, taps_ref, o_ref):
    count, channels, rows = x_ref.shape
    length = count * rows
    wide = jnp.broadcast_to(taps_ref[0], (block, taps_ref.shape[2]))
    matrix = pltpu.roll(wide, 0, 1, stride=1, stride_axis=0)[:, block : block + length]
    signal = jnp.concatenate([x_ref[k] for k in range(count)], axis=1)
    zeros = jnp.zeros((channels, length - block), signal.dtype)
    padded = jnp.concatenate([zeros, signal] if causal else [signal, zeros], axis=1)
    steps = length // block
    windows = jnp.concatenate(
        [padded[:, i * block : i * block + length] for i in range(steps)], axis=0
    )
    result = lax.dot_general(
        windows, matrix, (((1,), (1,)), ((), ())),
        precision=precise, preferred_element_type=jnp.float32,
    )
    line = jnp.concatenate(
        [result[i * channels : (i + 1) * channels] for i in range(steps)], axis=1
    )
    for k in range(count):
        o_ref[k] = line[:, k * rows : (k + 1) * rows]


def windowed_conv(padded_taps, chunks, causal, block):
    count, channels, rows = chunks.shape
    groups, _, width = padded_taps.shape
    share = channels // groups
    return pl.pallas_call(
        functools.partial(conv_kernel, causal, block),
        out_shape=jax.ShapeDtypeStruct(chunks.shape, chunks.dtype),
        grid=(groups,),
        in_specs=[
            pl.BlockSpec((count, share, rows), lambda g: (0, g, 0)),
            pl.BlockSpec((1, 1, width), lambda g: (g, 0, 0)),
        ],
        out_specs=pl.BlockSpec((count, share, rows), lambda g: (0, g, 0)),
    )(chunks, padded_taps)


def exchange_kernel(x_ref, o_ref, send_sems, recv_sems, local_sem):
    count = x_ref.shape[0]
    me = lax.axis_index("ctx")
    chip = lax.axis_index("chip")
    core = lax.axis_index("core")
    mesh_id = pl.DeviceIdType.MESH
    barrier = pltpu.get_barrier_semaphore()
    for offset in range(1, count):
        peer = lax.rem(me + offset, count)
        pl.semaphore_signal(barrier, 1, device_id=(peer, chip, core), device_id_type=mesh_id)
    pl.semaphore_wait(barrier, count - 1)
    local = pltpu.make_async_copy(x_ref.at[me], o_ref.at[me], local_sem)
    local.start()
    sends = []
    for offset in range(1, count):
        peer = lax.rem(me + offset, count)
        copy = pltpu.make_async_remote_copy(
            src_ref=x_ref.at[peer],
            dst_ref=o_ref.at[me],
            send_sem=send_sems.at[offset],
            recv_sem=recv_sems.at[offset],
            device_id=(peer, chip, core),
            device_id_type=mesh_id,
        )
        copy.start()
        sends.append(copy)
    for copy in sends:
        copy.wait_send()
    for offset in range(1, count):
        source = lax.rem(me + count - offset, count)
        pltpu.make_async_remote_copy(
            src_ref=x_ref.at[source],
            dst_ref=o_ref.at[source],
            send_sem=send_sems.at[offset],
            recv_sem=recv_sems.at[offset],
            device_id=(source, chip, core),
            device_id_type=mesh_id,
        ).wait_recv()
    local.wait()


def exchange(chunks):
    count = chunks.shape[0]
    return pl.pallas_call(
        exchange_kernel,
        out_shape=jax.ShapeDtypeStruct(chunks.shape, chunks.dtype),
        in_specs=[pl.BlockSpec(memory_space=pl.ANY)],
        out_specs=pl.BlockSpec(memory_space=pl.ANY),
        scratch_shapes=[
            pltpu.SemaphoreType.DMA((count,)),
            pltpu.SemaphoreType.DMA((count,)),
            pltpu.SemaphoreType.DMA,
        ],
        compiler_params=pltpu.CompilerParams(collective_id=0, has_side_effects=True),
    )(chunks)


def gather_kernel(x_ref, o_ref, send_sems, recv_sems, local_sem):
    count = o_ref.shape[0]
    me = lax.axis_index("ctx")
    chip = lax.axis_index("chip")
    core = lax.axis_index("core")
    mesh_id = pl.DeviceIdType.MESH
    barrier = pltpu.get_barrier_semaphore()
    for offset in range(1, count):
        peer = lax.rem(me + offset, count)
        pl.semaphore_signal(barrier, 1, device_id=(peer, chip, core), device_id_type=mesh_id)
    pl.semaphore_wait(barrier, count - 1)
    local = pltpu.make_async_copy(x_ref, o_ref.at[me], local_sem)
    local.start()
    sends = []
    for offset in range(1, count):
        peer = lax.rem(me + offset, count)
        copy = pltpu.make_async_remote_copy(
            src_ref=x_ref,
            dst_ref=o_ref.at[me],
            send_sem=send_sems.at[offset],
            recv_sem=recv_sems.at[offset],
            device_id=(peer, chip, core),
            device_id_type=mesh_id,
        )
        copy.start()
        sends.append(copy)
    for copy in sends:
        copy.wait_send()
    for offset in range(1, count):
        source = lax.rem(me + count - offset, count)
        pltpu.make_async_remote_copy(
            src_ref=x_ref,
            dst_ref=o_ref.at[source],
            send_sem=send_sems.at[offset],
            recv_sem=recv_sems.at[offset],
            device_id=(source, chip, core),
            device_id_type=mesh_id,
        ).wait_recv()
    local.wait()


def gather_ctx(value):
    count = lax.axis_size("ctx")
    gathered = pl.pallas_call(
        gather_kernel,
        out_shape=jax.ShapeDtypeStruct((count,) + value.shape, value.dtype),
        in_specs=[pl.BlockSpec(memory_space=pl.ANY)],
        out_specs=pl.BlockSpec(memory_space=pl.ANY),
        scratch_shapes=[
            pltpu.SemaphoreType.DMA((count,)),
            pltpu.SemaphoreType.DMA((count,)),
            pltpu.SemaphoreType.DMA,
        ],
        compiler_params=pltpu.CompilerParams(collective_id=1, has_side_effects=True),
    )(value)
    return gathered.reshape((count * value.shape[0],) + value.shape[1:])


def to_channels(value):
    rows, channels = value.shape
    count = lax.axis_size("ctx")
    return exchange(value.T.reshape(count, channels // count, rows))


def to_rows(chunks):
    count, channels, rows = chunks.shape
    return exchange(chunks).reshape(count * channels, rows).T


def body(
    token_ids,
    embed_table,
    norm_gain,
    input_weight,
    short_weight,
    filters,
    skip_gain,
    output_weight,
    output_grad,
):
    local_rows = token_ids.shape[0]
    tokens = jnp.take(embed_table, token_ids, axis=0)
    token_values = tokens.astype(jnp.float32)
    inverse_rms = lax.rsqrt(jnp.mean(token_values * token_values, axis=-1, keepdims=True) + 1e-06)
    normed = (token_values * inverse_rms * norm_gain).astype(jnp.bfloat16)
    projected = jnp.einsum("td,djc->tjc", normed, input_weight, preferred_element_type=jnp.float32)
    short_taps = short_weight.shape[0]
    before = from_behind(projected[local_rows - (short_taps - 1) :], "ctx", 1)
    extended = jnp.concatenate([before, projected], axis=0)
    features = sum(
        (
            short_weight[tap_index]
            * extended[short_taps - 1 - tap_index : short_taps - 1 - tap_index + local_rows]
            for tap_index in range(short_taps)
        )
    )
    queries = features[:, 0]
    key_part = features[:, 1]
    value_part = features[:, 2]
    mixture = key_part * value_part
    weight_rows = lax.all_to_all(output_weight, TP, 0, 1, tiled=True)
    grad_columns = lax.all_to_all(output_grad, "ctx", 1, 0, tiled=True)
    chip_weight = lax.all_gather(input_weight, "core", axis=2, tiled=True)
    mixture, weight_rows, grad_columns, chip_weight = lax.optimization_barrier(
        (mixture, weight_rows, grad_columns, chip_weight)
    )

    group_taps, reversed_taps = gather_taps(filters)
    causal_taps, anti_taps = conv_taps(group_taps, reversed_taps, BLOCK)
    long_part = to_rows(windowed_conv(causal_taps, to_channels(mixture), True, BLOCK))
    mixed_out = skip_gain * mixture + long_part
    hidden = (queries * mixed_out).astype(jnp.bfloat16)

    tp_size = lax.axis_size(TP)
    width = token_values.shape[1] // tp_size
    hidden_grad = jnp.dot(output_grad, output_weight, preferred_element_type=jnp.float32)
    mixed_grad = hidden_grad * queries
    hidden, mixed_grad, weight_rows, grad_columns = lax.optimization_barrier(
        (hidden, mixed_grad, weight_rows, grad_columns)
    )
    hidden_wide = lax.all_gather(hidden, TP, axis=1, tiled=True)
    hidden_long, mixed_grad = lax.optimization_barrier((gather_ctx(hidden), mixed_grad))
    carried = to_rows(windowed_conv(anti_taps, to_channels(mixed_grad), False, BLOCK))
    hidden_wide, carried = lax.optimization_barrier((hidden_wide, carried))
    own_sums = jnp.einsum("tc,dc->td", hidden_wide, weight_rows, preferred_element_type=jnp.float32)
    own_tokens = lax.dynamic_slice_in_dim(token_values, lax.axis_index(TP) * width, width, axis=1)
    own_output = (own_tokens + own_sums).astype(jnp.bfloat16)
    block_output = lax.all_gather(own_output, TP, axis=1, tiled=True)
    output_weight_grad = jnp.einsum(
        "td,tc->dc", grad_columns, hidden_long, preferred_element_type=jnp.float32
    )
    mixture_grad = skip_gain * mixed_grad + carried
    feature_grad = jnp.stack(
        [hidden_grad * mixed_out, mixture_grad * value_part, mixture_grad * key_part], axis=1
    )
    following = from_behind(feature_grad[: short_taps - 1], "ctx", -1)
    extended_grads = jnp.concatenate([feature_grad, following], axis=0)
    projection_grad = sum(
        (
            short_weight[tap_index] * extended_grads[tap_index : tap_index + local_rows]
            for tap_index in range(short_taps)
        )
    ).astype(jnp.bfloat16)
    chips = lax.axis_size("chip")
    cores = lax.axis_size("core")
    row_blocks = projection_grad.reshape(
        chips, cores, local_rows // tp_size, short_taps, projection_grad.shape[2]
    )
    chip_rows = lax.all_to_all(row_blocks, "core", 1, 4, tiled=True)
    chip_rows = chip_rows.reshape(local_rows // cores, short_taps, chip_rows.shape[4])
    partial_grad = jnp.einsum(
        "mjc,djc->md", chip_rows, chip_weight, preferred_element_type=jnp.float32
    ).astype(jnp.bfloat16)
    partial_grad = partial_grad.reshape(chips, local_rows // tp_size, partial_grad.shape[1])
    received = lax.all_to_all(partial_grad, "chip", 0, 0)
    normed_grad = jnp.sum(received.astype(jnp.float32), axis=0)
    return (block_output, output_weight_grad, projection_grad, normed_grad)


def solution(mesh):
    ctx_size, tp_size = mesh.devices.shape
    devices = mesh.devices.reshape(ctx_size, tp_size // 2, 2)
    split_mesh = jax.sharding.Mesh(devices, ("ctx", "chip", "core"))
    in_specs = (
        P("ctx"),
        P(),
        P(),
        P(None, None, TP),
        P(None, None, TP),
        P(TP, "ctx"),
        P(TP),
        P(None, TP),
        P("ctx", None),
    )
    out_specs = (P("ctx", None), P("ctx", TP), P("ctx", None, TP), P(("ctx",) + TP, None))
    return jax.shard_map(body, mesh=split_mesh, in_specs=in_specs, out_specs=out_specs, check_vma=False)
```

```python
import functools

import jax
import jax.numpy as jnp
from jax import lax
from jax.experimental import pallas as pl
from jax.experimental.pallas import tpu as pltpu
from jax.sharding import PartitionSpec as P

precise = lax.Precision.HIGHEST
BLOCK = 256
TP = ("chip", "core")


def from_behind(value, axis, steps):
    count = lax.axis_size(axis)
    first, last = (max(0, -steps), min(count, count - steps))
    return lax.ppermute(value, axis, [(source, source + steps) for source in range(first, last)])


def conv_taps(taps, reversed_taps, block):
    groups, length = taps.shape
    one = jnp.zeros((groups, 1), taps.dtype)
    causal = jnp.concatenate([one, reversed_taps, jnp.zeros((groups, block - 1), taps.dtype)], axis=1)
    anti = jnp.concatenate([jnp.zeros((groups, block), taps.dtype), taps], axis=1)
    return causal[:, None, :], anti[:, None, :]


def gather_taps(filters):
    width = filters.shape[1]
    rows = lax.broadcasted_iota(jnp.int32, (width, width), 0)
    cols = lax.broadcasted_iota(jnp.int32, (width, width), 1)
    exchange = (rows + cols == width - 1).astype(filters.dtype)
    flipped = jnp.dot(filters, exchange, precision=precise)
    both = lax.all_to_all(jnp.stack([filters, flipped]), "ctx", 1, 2, tiled=True)
    shards = lax.axis_size("ctx")
    pieces = both[1].reshape(both.shape[1], shards, width)
    reversed_taps = jnp.concatenate([pieces[:, k] for k in reversed(range(shards))], axis=1)
    return both[0], reversed_taps


def conv_kernel(causal, block, x_ref, taps_ref, o_ref):
    count, channels, rows = x_ref.shape
    length = count * rows
    wide = jnp.broadcast_to(taps_ref[0], (block, taps_ref.shape[2]))
    matrix = pltpu.roll(wide, 0, 1, stride=1, stride_axis=0)[:, block : block + length]
    signal = jnp.concatenate([x_ref[k] for k in range(count)], axis=1)
    zeros = jnp.zeros((channels, length - block), signal.dtype)
    padded = jnp.concatenate([zeros, signal] if causal else [signal, zeros], axis=1)
    steps = length // block
    windows = jnp.concatenate(
        [padded[:, i * block : i * block + length] for i in range(steps)], axis=0
    )
    result = lax.dot_general(
        windows, matrix, (((1,), (1,)), ((), ())),
        precision=precise, preferred_element_type=jnp.float32,
    )
    line = jnp.concatenate(
        [result[i * channels : (i + 1) * channels] for i in range(steps)], axis=1
    )
    for k in range(count):
        o_ref[k] = line[:, k * rows : (k + 1) * rows]


def windowed_conv(padded_taps, chunks, causal, block):
    count, channels, rows = chunks.shape
    groups, _, width = padded_taps.shape
    share = channels // groups
    return pl.pallas_call(
        functools.partial(conv_kernel, causal, block),
        out_shape=jax.ShapeDtypeStruct(chunks.shape, chunks.dtype),
        grid=(groups,),
        in_specs=[
            pl.BlockSpec((count, share, rows), lambda g: (0, g, 0)),
            pl.BlockSpec((1, 1, width), lambda g: (g, 0, 0)),
        ],
        out_specs=pl.BlockSpec((count, share, rows), lambda g: (0, g, 0)),
    )(chunks, padded_taps)


def exchange_kernel(x_ref, o_ref, send_sems, recv_sems, local_sem):
    count = x_ref.shape[0]
    me = lax.axis_index("ctx")
    chip = lax.axis_index("chip")
    core = lax.axis_index("core")
    mesh_id = pl.DeviceIdType.MESH
    barrier = pltpu.get_barrier_semaphore()
    for offset in range(1, count):
        peer = lax.rem(me + offset, count)
        pl.semaphore_signal(barrier, 1, device_id=(peer, chip, core), device_id_type=mesh_id)
    pl.semaphore_wait(barrier, count - 1)
    local = pltpu.make_async_copy(x_ref.at[me], o_ref.at[me], local_sem)
    local.start()
    sends = []
    for offset in range(1, count):
        peer = lax.rem(me + offset, count)
        copy = pltpu.make_async_remote_copy(
            src_ref=x_ref.at[peer],
            dst_ref=o_ref.at[me],
            send_sem=send_sems.at[offset],
            recv_sem=recv_sems.at[offset],
            device_id=(peer, chip, core),
            device_id_type=mesh_id,
        )
        copy.start()
        sends.append(copy)
    for copy in sends:
        copy.wait_send()
    for offset in range(1, count):
        source = lax.rem(me + count - offset, count)
        pltpu.make_async_remote_copy(
            src_ref=x_ref.at[source],
            dst_ref=o_ref.at[source],
            send_sem=send_sems.at[offset],
            recv_sem=recv_sems.at[offset],
            device_id=(source, chip, core),
            device_id_type=mesh_id,
        ).wait_recv()
    local.wait()


def exchange(chunks):
    count = chunks.shape[0]
    return pl.pallas_call(
        exchange_kernel,
        out_shape=jax.ShapeDtypeStruct(chunks.shape, chunks.dtype),
        in_specs=[pl.BlockSpec(memory_space=pl.ANY)],
        out_specs=pl.BlockSpec(memory_space=pl.ANY),
        scratch_shapes=[
            pltpu.SemaphoreType.DMA((count,)),
            pltpu.SemaphoreType.DMA((count,)),
            pltpu.SemaphoreType.DMA,
        ],
        compiler_params=pltpu.CompilerParams(collective_id=0, has_side_effects=True),
    )(chunks)


def to_channels(value):
    rows, channels = value.shape
    count = lax.axis_size("ctx")
    return exchange(value.T.reshape(count, channels // count, rows))


def to_rows(chunks):
    count, channels, rows = chunks.shape
    return exchange(chunks).reshape(count * channels, rows).T


def body(
    token_ids,
    embed_table,
    norm_gain,
    input_weight,
    short_weight,
    filters,
    skip_gain,
    output_weight,
    output_grad,
):
    local_rows = token_ids.shape[0]
    tokens = jnp.take(embed_table, token_ids, axis=0)
    token_values = tokens.astype(jnp.float32)
    inverse_rms = lax.rsqrt(jnp.mean(token_values * token_values, axis=-1, keepdims=True) + 1e-06)
    normed = (token_values * inverse_rms * norm_gain).astype(jnp.bfloat16)
    projected = jnp.einsum("td,djc->tjc", normed, input_weight, preferred_element_type=jnp.float32)
    short_taps = short_weight.shape[0]
    before = from_behind(projected[local_rows - (short_taps - 1) :], "ctx", 1)
    extended = jnp.concatenate([before, projected], axis=0)
    features = sum(
        (
            short_weight[tap_index]
            * extended[short_taps - 1 - tap_index : short_taps - 1 - tap_index + local_rows]
            for tap_index in range(short_taps)
        )
    )
    queries = features[:, 0]
    key_part = features[:, 1]
    value_part = features[:, 2]
    mixture = key_part * value_part
    weight_rows = lax.all_to_all(output_weight, TP, 0, 1, tiled=True)
    chip_weight = lax.all_gather(input_weight, "core", axis=2, tiled=True)
    mixture, weight_rows, chip_weight = lax.optimization_barrier((mixture, weight_rows, chip_weight))

    group_taps, reversed_taps = gather_taps(filters)
    causal_taps, anti_taps = conv_taps(group_taps, reversed_taps, BLOCK)
    long_part = to_rows(windowed_conv(causal_taps, to_channels(mixture), True, BLOCK))
    mixed_out = skip_gain * mixture + long_part
    hidden = (queries * mixed_out).astype(jnp.bfloat16)

    tp_size = lax.axis_size(TP)
    width = token_values.shape[1] // tp_size
    hidden_grad = jnp.dot(output_grad, output_weight, preferred_element_type=jnp.float32)
    mixed_grad = hidden_grad * queries
    hidden, mixed_grad, weight_rows = lax.optimization_barrier((hidden, mixed_grad, weight_rows))
    hidden_wide = lax.all_gather(hidden, TP, axis=1, tiled=True)
    carried = to_rows(windowed_conv(anti_taps, to_channels(mixed_grad), False, BLOCK))
    hidden_wide, carried = lax.optimization_barrier((hidden_wide, carried))
    own_sums = jnp.einsum("tc,dc->td", hidden_wide, weight_rows, preferred_element_type=jnp.float32)
    own_tokens = lax.dynamic_slice_in_dim(token_values, lax.axis_index(TP) * width, width, axis=1)
    own_output = (own_tokens + own_sums).astype(jnp.bfloat16)
    block_output = lax.all_gather(own_output, TP, axis=1, tiled=True)
    output_weight_grad = lax.psum_scatter(
        jnp.einsum("td,tc->dc", output_grad, hidden, preferred_element_type=jnp.float32),
        "ctx",
        scatter_dimension=0,
        tiled=True,
    )
    mixture_grad = skip_gain * mixed_grad + carried
    feature_grad = jnp.stack(
        [hidden_grad * mixed_out, mixture_grad * value_part, mixture_grad * key_part], axis=1
    )
    following = from_behind(feature_grad[: short_taps - 1], "ctx", -1)
    extended_grads = jnp.concatenate([feature_grad, following], axis=0)
    projection_grad = sum(
        (
            short_weight[tap_index] * extended_grads[tap_index : tap_index + local_rows]
            for tap_index in range(short_taps)
        )
    ).astype(jnp.bfloat16)
    chips = lax.axis_size("chip")
    cores = lax.axis_size("core")
    row_blocks = projection_grad.reshape(
        chips, cores, local_rows // tp_size, short_taps, projection_grad.shape[2]
    )
    chip_rows = lax.all_to_all(row_blocks, "core", 1, 4, tiled=True)
    chip_rows = chip_rows.reshape(local_rows // cores, short_taps, chip_rows.shape[4])
    partial_grad = jnp.einsum(
        "mjc,djc->md", chip_rows, chip_weight, preferred_element_type=jnp.float32
    ).astype(jnp.bfloat16)
    partial_grad = partial_grad.reshape(chips, local_rows // tp_size, partial_grad.shape[1])
    received = lax.all_to_all(partial_grad, "chip", 0, 0)
    normed_grad = jnp.sum(received.astype(jnp.float32), axis=0)
    return (block_output, output_weight_grad, projection_grad, normed_grad)


def solution(mesh):
    ctx_size, tp_size = mesh.devices.shape
    devices = mesh.devices.reshape(ctx_size, tp_size // 2, 2)
    split_mesh = jax.sharding.Mesh(devices, ("ctx", "chip", "core"))
    in_specs = (
        P("ctx"),
        P(),
        P(),
        P(None, None, TP),
        P(None, None, TP),
        P(TP, "ctx"),
        P(TP),
        P(None, TP),
        P("ctx", None),
    )
    out_specs = (P("ctx", None), P("ctx", TP), P("ctx", None, TP), P(("ctx",) + TP, None))
    return jax.shard_map(body, mesh=split_mesh, in_specs=in_specs, out_specs=out_specs, check_vma=False)
```

```python
import functools

import jax
import jax.numpy as jnp
from jax import lax
from jax.experimental import pallas as pl
from jax.experimental.pallas import tpu as pltpu
from jax.sharding import PartitionSpec as P

precise = lax.Precision.HIGHEST
BLOCK = 256
TP = ("chip", "core")


def from_behind(value, axis, steps):
    count = lax.axis_size(axis)
    first, last = (max(0, -steps), min(count, count - steps))
    return lax.ppermute(value, axis, [(source, source + steps) for source in range(first, last)])


def conv_taps(taps, reversed_taps, block):
    groups, length = taps.shape
    one = jnp.zeros((groups, 1), taps.dtype)
    causal = jnp.concatenate([one, reversed_taps, jnp.zeros((groups, block - 1), taps.dtype)], axis=1)
    anti = jnp.concatenate([jnp.zeros((groups, block), taps.dtype), taps], axis=1)
    return causal[:, None, :], anti[:, None, :]


def gather_taps(filters):
    width = filters.shape[1]
    rows = lax.broadcasted_iota(jnp.int32, (width, width), 0)
    cols = lax.broadcasted_iota(jnp.int32, (width, width), 1)
    exchange = (rows + cols == width - 1).astype(filters.dtype)
    flipped = jnp.dot(filters, exchange, precision=precise)
    both = lax.all_to_all(jnp.stack([filters, flipped]), "ctx", 1, 2, tiled=True)
    shards = lax.axis_size("ctx")
    pieces = both[1].reshape(both.shape[1], shards, width)
    reversed_taps = jnp.concatenate([pieces[:, k] for k in reversed(range(shards))], axis=1)
    return both[0], reversed_taps


def conv_kernel(causal, block, x_ref, taps_ref, o_ref):
    count, channels, rows = x_ref.shape
    length = count * rows
    wide = jnp.broadcast_to(taps_ref[0], (block, taps_ref.shape[2]))
    matrix = pltpu.roll(wide, 0, 1, stride=1, stride_axis=0)[:, block : block + length]
    signal = jnp.concatenate([x_ref[k] for k in range(count)], axis=1)
    zeros = jnp.zeros((channels, length - block), signal.dtype)
    padded = jnp.concatenate([zeros, signal] if causal else [signal, zeros], axis=1)
    steps = length // block
    windows = jnp.concatenate(
        [padded[:, i * block : i * block + length] for i in range(steps)], axis=0
    )
    result = lax.dot_general(
        windows, matrix, (((1,), (1,)), ((), ())),
        precision=precise, preferred_element_type=jnp.float32,
    )
    line = jnp.concatenate(
        [result[i * channels : (i + 1) * channels] for i in range(steps)], axis=1
    )
    for k in range(count):
        o_ref[k] = line[:, k * rows : (k + 1) * rows]


def windowed_conv(padded_taps, chunks, causal, block):
    count, channels, rows = chunks.shape
    groups, _, width = padded_taps.shape
    share = channels // groups
    return pl.pallas_call(
        functools.partial(conv_kernel, causal, block),
        out_shape=jax.ShapeDtypeStruct(chunks.shape, chunks.dtype),
        grid=(groups,),
        in_specs=[
            pl.BlockSpec((count, share, rows), lambda g: (0, g, 0)),
            pl.BlockSpec((1, 1, width), lambda g: (g, 0, 0)),
        ],
        out_specs=pl.BlockSpec((count, share, rows), lambda g: (0, g, 0)),
    )(chunks, padded_taps)


def exchange_kernel(x_ref, o_ref, send_sems, recv_sems, local_sem):
    count = x_ref.shape[0]
    me = lax.axis_index("ctx")
    chip = lax.axis_index("chip")
    core = lax.axis_index("core")
    mesh_id = pl.DeviceIdType.MESH
    barrier = pltpu.get_barrier_semaphore()
    for offset in range(1, count):
        peer = lax.rem(me + offset, count)
        pl.semaphore_signal(barrier, 1, device_id=(peer, chip, core), device_id_type=mesh_id)
    pl.semaphore_wait(barrier, count - 1)
    local = pltpu.make_async_copy(x_ref.at[me], o_ref.at[me], local_sem)
    local.start()
    sends = []
    for offset in range(1, count):
        peer = lax.rem(me + offset, count)
        copy = pltpu.make_async_remote_copy(
            src_ref=x_ref.at[peer],
            dst_ref=o_ref.at[me],
            send_sem=send_sems.at[offset],
            recv_sem=recv_sems.at[offset],
            device_id=(peer, chip, core),
            device_id_type=mesh_id,
        )
        copy.start()
        sends.append(copy)
    for copy in sends:
        copy.wait_send()
    for offset in range(1, count):
        source = lax.rem(me + count - offset, count)
        pltpu.make_async_remote_copy(
            src_ref=x_ref.at[source],
            dst_ref=o_ref.at[source],
            send_sem=send_sems.at[offset],
            recv_sem=recv_sems.at[offset],
            device_id=(source, chip, core),
            device_id_type=mesh_id,
        ).wait_recv()
    local.wait()


def exchange(chunks, collective=0):
    count = chunks.shape[0]
    return pl.pallas_call(
        exchange_kernel,
        out_shape=jax.ShapeDtypeStruct(chunks.shape, chunks.dtype),
        in_specs=[pl.BlockSpec(memory_space=pl.ANY)],
        out_specs=pl.BlockSpec(memory_space=pl.ANY),
        scratch_shapes=[
            pltpu.SemaphoreType.DMA((count,)),
            pltpu.SemaphoreType.DMA((count,)),
            pltpu.SemaphoreType.DMA,
        ],
        compiler_params=pltpu.CompilerParams(collective_id=collective, has_side_effects=True),
    )(chunks)


def to_channels(value):
    rows, channels = value.shape
    count = lax.axis_size("ctx")
    return exchange(value.T.reshape(count, channels // count, rows))


def to_rows(chunks):
    count, channels, rows = chunks.shape
    return exchange(chunks).reshape(count * channels, rows).T


def body(
    token_ids,
    embed_table,
    norm_gain,
    input_weight,
    short_weight,
    filters,
    skip_gain,
    output_weight,
    output_grad,
):
    local_rows = token_ids.shape[0]
    tokens = jnp.take(embed_table, token_ids, axis=0)
    token_values = tokens.astype(jnp.float32)
    inverse_rms = lax.rsqrt(jnp.mean(token_values * token_values, axis=-1, keepdims=True) + 1e-06)
    normed = (token_values * inverse_rms * norm_gain).astype(jnp.bfloat16)
    projected = jnp.einsum("td,djc->tjc", normed, input_weight, preferred_element_type=jnp.float32)
    short_taps = short_weight.shape[0]
    before = from_behind(projected[local_rows - (short_taps - 1) :], "ctx", 1)
    extended = jnp.concatenate([before, projected], axis=0)
    features = sum(
        (
            short_weight[tap_index]
            * extended[short_taps - 1 - tap_index : short_taps - 1 - tap_index + local_rows]
            for tap_index in range(short_taps)
        )
    )
    queries = features[:, 0]
    key_part = features[:, 1]
    value_part = features[:, 2]
    mixture = key_part * value_part
    weight_rows = lax.all_to_all(output_weight, TP, 0, 1, tiled=True)
    chip_weight = lax.all_gather(input_weight, "core", axis=2, tiled=True)
    mixture, weight_rows, chip_weight = lax.optimization_barrier((mixture, weight_rows, chip_weight))

    group_taps, reversed_taps = gather_taps(filters)
    causal_taps, anti_taps = conv_taps(group_taps, reversed_taps, BLOCK)
    long_part = to_rows(windowed_conv(causal_taps, to_channels(mixture), True, BLOCK))
    mixed_out = skip_gain * mixture + long_part
    hidden = (queries * mixed_out).astype(jnp.bfloat16)

    tp_size = lax.axis_size(TP)
    width = token_values.shape[1] // tp_size
    hidden_grad = jnp.dot(output_grad, output_weight, preferred_element_type=jnp.float32)
    mixed_grad = hidden_grad * queries
    hidden, mixed_grad, weight_rows = lax.optimization_barrier((hidden, mixed_grad, weight_rows))
    hidden_wide = lax.all_gather(hidden, TP, axis=1, tiled=True)
    carried = to_rows(windowed_conv(anti_taps, to_channels(mixed_grad), False, BLOCK))
    hidden_wide, carried = lax.optimization_barrier((hidden_wide, carried))
    own_sums = jnp.einsum("tc,dc->td", hidden_wide, weight_rows, preferred_element_type=jnp.float32)
    own_tokens = lax.dynamic_slice_in_dim(token_values, lax.axis_index(TP) * width, width, axis=1)
    own_output = (own_tokens + own_sums).astype(jnp.bfloat16)
    block_output = lax.all_gather(own_output, TP, axis=1, tiled=True)
    ctx_size = lax.axis_size("ctx")
    weight_partial = jnp.einsum(
        "td,tc->dc", output_grad, hidden, preferred_element_type=jnp.float32
    ).astype(jnp.bfloat16)
    weight_pieces = weight_partial.reshape(ctx_size, -1, weight_partial.shape[1])
    output_weight_grad = jnp.sum(exchange(weight_pieces, 1).astype(jnp.float32), axis=0)
    mixture_grad = skip_gain * mixed_grad + carried
    feature_grad = jnp.stack(
        [hidden_grad * mixed_out, mixture_grad * value_part, mixture_grad * key_part], axis=1
    )
    following = from_behind(feature_grad[: short_taps - 1], "ctx", -1)
    extended_grads = jnp.concatenate([feature_grad, following], axis=0)
    projection_grad = sum(
        (
            short_weight[tap_index] * extended_grads[tap_index : tap_index + local_rows]
            for tap_index in range(short_taps)
        )
    ).astype(jnp.bfloat16)
    chips = lax.axis_size("chip")
    cores = lax.axis_size("core")
    row_blocks = projection_grad.reshape(
        chips, cores, local_rows // tp_size, short_taps, projection_grad.shape[2]
    )
    chip_rows = lax.all_to_all(row_blocks, "core", 1, 4, tiled=True)
    chip_rows = chip_rows.reshape(local_rows // cores, short_taps, chip_rows.shape[4])
    partial_grad = jnp.einsum(
        "mjc,djc->md", chip_rows, chip_weight, preferred_element_type=jnp.float32
    ).astype(jnp.bfloat16)
    partial_grad = partial_grad.reshape(chips, local_rows // tp_size, partial_grad.shape[1])
    received = lax.all_to_all(partial_grad, "chip", 0, 0)
    normed_grad = jnp.sum(received.astype(jnp.float32), axis=0)
    return (block_output, output_weight_grad, projection_grad, normed_grad)


def solution(mesh):
    ctx_size, tp_size = mesh.devices.shape
    devices = mesh.devices.reshape(ctx_size, tp_size // 2, 2)
    split_mesh = jax.sharding.Mesh(devices, ("ctx", "chip", "core"))
    in_specs = (
        P("ctx"),
        P(),
        P(),
        P(None, None, TP),
        P(None, None, TP),
        P(TP, "ctx"),
        P(TP),
        P(None, TP),
        P("ctx", None),
    )
    out_specs = (P("ctx", None), P("ctx", TP), P("ctx", None, TP), P(("ctx",) + TP, None))
    return jax.shard_map(body, mesh=split_mesh, in_specs=in_specs, out_specs=out_specs, check_vma=False)
```

```python
import functools

import jax
import jax.numpy as jnp
from jax import lax
from jax.experimental import pallas as pl
from jax.experimental.pallas import tpu as pltpu
from jax.sharding import PartitionSpec as P

precise = lax.Precision.HIGHEST
BLOCK = 256
TP = ("chip", "core")


def from_behind(value, axis, steps):
    count = lax.axis_size(axis)
    first, last = (max(0, -steps), min(count, count - steps))
    return lax.ppermute(value, axis, [(source, source + steps) for source in range(first, last)])


def conv_taps(taps, reversed_taps, block):
    groups, length = taps.shape
    one = jnp.zeros((groups, 1), taps.dtype)
    causal = jnp.concatenate([one, reversed_taps, jnp.zeros((groups, block - 1), taps.dtype)], axis=1)
    anti = jnp.concatenate([jnp.zeros((groups, block), taps.dtype), taps], axis=1)
    return causal[:, None, :], anti[:, None, :]


def gather_taps(filters):
    width = filters.shape[1]
    rows = lax.broadcasted_iota(jnp.int32, (width, width), 0)
    cols = lax.broadcasted_iota(jnp.int32, (width, width), 1)
    exchange = (rows + cols == width - 1).astype(filters.dtype)
    flipped = jnp.dot(filters, exchange, precision=precise)
    both = lax.all_to_all(jnp.stack([filters, flipped]), "ctx", 1, 2, tiled=True)
    shards = lax.axis_size("ctx")
    pieces = both[1].reshape(both.shape[1], shards, width)
    reversed_taps = jnp.concatenate([pieces[:, k] for k in reversed(range(shards))], axis=1)
    return both[0], reversed_taps


def conv_kernel(causal, block, x_ref, taps_ref, o_ref):
    count, channels, rows = x_ref.shape
    length = count * rows
    wide = jnp.broadcast_to(taps_ref[0], (block, taps_ref.shape[2]))
    matrix = pltpu.roll(wide, 0, 1, stride=1, stride_axis=0)[:, block : block + length]
    signal = jnp.concatenate([x_ref[k] for k in range(count)], axis=1)
    zeros = jnp.zeros((channels, length - block), signal.dtype)
    padded = jnp.concatenate([zeros, signal] if causal else [signal, zeros], axis=1)
    steps = length // block
    windows = jnp.concatenate(
        [padded[:, i * block : i * block + length] for i in range(steps)], axis=0
    )
    result = lax.dot_general(
        windows, matrix, (((1,), (1,)), ((), ())),
        precision=precise, preferred_element_type=jnp.float32,
    )
    line = jnp.concatenate(
        [result[i * channels : (i + 1) * channels] for i in range(steps)], axis=1
    )
    for k in range(count):
        o_ref[k] = line[:, k * rows : (k + 1) * rows]


def windowed_conv(padded_taps, chunks, causal, block):
    count, channels, rows = chunks.shape
    groups, _, width = padded_taps.shape
    share = channels // groups
    return pl.pallas_call(
        functools.partial(conv_kernel, causal, block),
        out_shape=jax.ShapeDtypeStruct(chunks.shape, chunks.dtype),
        grid=(groups,),
        in_specs=[
            pl.BlockSpec((count, share, rows), lambda g: (0, g, 0)),
            pl.BlockSpec((1, 1, width), lambda g: (g, 0, 0)),
        ],
        out_specs=pl.BlockSpec((count, share, rows), lambda g: (0, g, 0)),
    )(chunks, padded_taps)


def exchange_kernel(x_ref, o_ref, send_sems, recv_sems, local_sem):
    count = x_ref.shape[0]
    me = lax.axis_index("ctx")
    chip = lax.axis_index("chip")
    core = lax.axis_index("core")
    mesh_id = pl.DeviceIdType.MESH
    barrier = pltpu.get_barrier_semaphore()
    for offset in range(1, count):
        peer = lax.rem(me + offset, count)
        pl.semaphore_signal(barrier, 1, device_id=(peer, chip, core), device_id_type=mesh_id)
    pl.semaphore_wait(barrier, count - 1)
    local = pltpu.make_async_copy(x_ref.at[me], o_ref.at[me], local_sem)
    local.start()
    sends = []
    for offset in range(1, count):
        peer = lax.rem(me + offset, count)
        copy = pltpu.make_async_remote_copy(
            src_ref=x_ref.at[peer],
            dst_ref=o_ref.at[me],
            send_sem=send_sems.at[offset],
            recv_sem=recv_sems.at[offset],
            device_id=(peer, chip, core),
            device_id_type=mesh_id,
        )
        copy.start()
        sends.append(copy)
    for copy in sends:
        copy.wait_send()
    for offset in range(1, count):
        source = lax.rem(me + count - offset, count)
        pltpu.make_async_remote_copy(
            src_ref=x_ref.at[source],
            dst_ref=o_ref.at[source],
            send_sem=send_sems.at[offset],
            recv_sem=recv_sems.at[offset],
            device_id=(source, chip, core),
            device_id_type=mesh_id,
        ).wait_recv()
    local.wait()


def exchange(chunks, collective=0):
    count = chunks.shape[0]
    return pl.pallas_call(
        exchange_kernel,
        out_shape=jax.ShapeDtypeStruct(chunks.shape, chunks.dtype),
        in_specs=[pl.BlockSpec(memory_space=pl.ANY)],
        out_specs=pl.BlockSpec(memory_space=pl.ANY),
        scratch_shapes=[
            pltpu.SemaphoreType.DMA((count,)),
            pltpu.SemaphoreType.DMA((count,)),
            pltpu.SemaphoreType.DMA,
        ],
        compiler_params=pltpu.CompilerParams(collective_id=collective, has_side_effects=True),
    )(chunks)


def to_channels(value):
    rows, channels = value.shape
    count = lax.axis_size("ctx")
    return exchange(value.T.reshape(count, channels // count, rows))


def to_rows(chunks):
    count, channels, rows = chunks.shape
    return exchange(chunks).reshape(count * channels, rows).T


def body(
    token_ids,
    embed_table,
    norm_gain,
    input_weight,
    short_weight,
    filters,
    skip_gain,
    output_weight,
    output_grad,
):
    local_rows = token_ids.shape[0]
    tokens = jnp.take(embed_table, token_ids, axis=0)
    token_values = tokens.astype(jnp.float32)
    inverse_rms = lax.rsqrt(jnp.mean(token_values * token_values, axis=-1, keepdims=True) + 1e-06)
    normed = (token_values * inverse_rms * norm_gain).astype(jnp.bfloat16)
    projected = jnp.einsum("td,djc->tjc", normed, input_weight, preferred_element_type=jnp.float32)
    short_taps = short_weight.shape[0]
    before = from_behind(projected[local_rows - (short_taps - 1) :], "ctx", 1)
    extended = jnp.concatenate([before, projected], axis=0)
    features = sum(
        (
            short_weight[tap_index]
            * extended[short_taps - 1 - tap_index : short_taps - 1 - tap_index + local_rows]
            for tap_index in range(short_taps)
        )
    )
    queries = features[:, 0]
    key_part = features[:, 1]
    value_part = features[:, 2]
    mixture = key_part * value_part
    weight_rows = lax.all_to_all(output_weight, TP, 0, 1, tiled=True)
    chip_weight = lax.all_gather(input_weight, "core", axis=2, tiled=True)
    mixture, weight_rows, chip_weight = lax.optimization_barrier((mixture, weight_rows, chip_weight))

    group_taps, reversed_taps = gather_taps(filters)
    causal_taps, anti_taps = conv_taps(group_taps, reversed_taps, BLOCK)
    long_part = to_rows(windowed_conv(causal_taps, to_channels(mixture), True, BLOCK))
    mixed_out = skip_gain * mixture + long_part
    hidden = (queries * mixed_out).astype(jnp.bfloat16)

    tp_size = lax.axis_size(TP)
    width = token_values.shape[1] // tp_size
    hidden_grad = jnp.dot(output_grad, output_weight, preferred_element_type=jnp.float32)
    mixed_grad = hidden_grad * queries
    hidden, mixed_grad, weight_rows = lax.optimization_barrier((hidden, mixed_grad, weight_rows))
    hidden_wide = lax.all_gather(hidden, TP, axis=1, tiled=True)
    ctx_size = lax.axis_size("ctx")
    weight_partial = jnp.einsum(
        "td,tc->dc", output_grad, hidden, preferred_element_type=jnp.float32
    ).astype(jnp.bfloat16)
    weight_pieces = weight_partial.reshape(ctx_size, -1, weight_partial.shape[1])
    output_weight_grad = jnp.sum(exchange(weight_pieces, 1).astype(jnp.float32), axis=0)
    output_weight_grad, mixed_grad = lax.optimization_barrier((output_weight_grad, mixed_grad))
    carried = to_rows(windowed_conv(anti_taps, to_channels(mixed_grad), False, BLOCK))
    hidden_wide, carried = lax.optimization_barrier((hidden_wide, carried))
    own_sums = jnp.einsum("tc,dc->td", hidden_wide, weight_rows, preferred_element_type=jnp.float32)
    own_tokens = lax.dynamic_slice_in_dim(token_values, lax.axis_index(TP) * width, width, axis=1)
    own_output = (own_tokens + own_sums).astype(jnp.bfloat16)
    block_output = lax.all_gather(own_output, TP, axis=1, tiled=True)
    mixture_grad = skip_gain * mixed_grad + carried
    feature_grad = jnp.stack(
        [hidden_grad * mixed_out, mixture_grad * value_part, mixture_grad * key_part], axis=1
    )
    following = from_behind(feature_grad[: short_taps - 1], "ctx", -1)
    extended_grads = jnp.concatenate([feature_grad, following], axis=0)
    projection_grad = sum(
        (
            short_weight[tap_index] * extended_grads[tap_index : tap_index + local_rows]
            for tap_index in range(short_taps)
        )
    ).astype(jnp.bfloat16)
    chips = lax.axis_size("chip")
    cores = lax.axis_size("core")
    row_blocks = projection_grad.reshape(
        chips, cores, local_rows // tp_size, short_taps, projection_grad.shape[2]
    )
    chip_rows = lax.all_to_all(row_blocks, "core", 1, 4, tiled=True)
    chip_rows = chip_rows.reshape(local_rows // cores, short_taps, chip_rows.shape[4])
    partial_grad = jnp.einsum(
        "mjc,djc->md", chip_rows, chip_weight, preferred_element_type=jnp.float32
    ).astype(jnp.bfloat16)
    partial_grad = partial_grad.reshape(chips, local_rows // tp_size, partial_grad.shape[1])
    received = lax.all_to_all(partial_grad, "chip", 0, 0)
    normed_grad = jnp.sum(received.astype(jnp.float32), axis=0)
    return (block_output, output_weight_grad, projection_grad, normed_grad)


def solution(mesh):
    ctx_size, tp_size = mesh.devices.shape
    devices = mesh.devices.reshape(ctx_size, tp_size // 2, 2)
    split_mesh = jax.sharding.Mesh(devices, ("ctx", "chip", "core"))
    in_specs = (
        P("ctx"),
        P(),
        P(),
        P(None, None, TP),
        P(None, None, TP),
        P(TP, "ctx"),
        P(TP),
        P(None, TP),
        P("ctx", None),
    )
    out_specs = (P("ctx", None), P("ctx", TP), P("ctx", None, TP), P(("ctx",) + TP, None))
    return jax.shard_map(body, mesh=split_mesh, in_specs=in_specs, out_specs=out_specs, check_vma=False)
```

```python
import functools

import jax
import jax.numpy as jnp
from jax import lax
from jax.experimental import pallas as pl
from jax.experimental.pallas import tpu as pltpu
from jax.sharding import PartitionSpec as P

precise = lax.Precision.HIGHEST
BLOCK = 256
TP = ("chip", "core")


def from_behind(value, axis, steps):
    count = lax.axis_size(axis)
    first, last = (max(0, -steps), min(count, count - steps))
    return lax.ppermute(value, axis, [(source, source + steps) for source in range(first, last)])


def conv_taps(taps, reversed_taps, block):
    groups, length = taps.shape
    one = jnp.zeros((groups, 1), taps.dtype)
    causal = jnp.concatenate([one, reversed_taps, jnp.zeros((groups, block - 1), taps.dtype)], axis=1)
    anti = jnp.concatenate([jnp.zeros((groups, block), taps.dtype), taps], axis=1)
    return causal[:, None, :], anti[:, None, :]


def gather_taps(filters):
    width = filters.shape[1]
    rows = lax.broadcasted_iota(jnp.int32, (width, width), 0)
    cols = lax.broadcasted_iota(jnp.int32, (width, width), 1)
    exchange = (rows + cols == width - 1).astype(filters.dtype)
    flipped = jnp.dot(filters, exchange, precision=precise)
    both = lax.all_to_all(jnp.stack([filters, flipped]), "ctx", 1, 2, tiled=True)
    shards = lax.axis_size("ctx")
    pieces = both[1].reshape(both.shape[1], shards, width)
    reversed_taps = jnp.concatenate([pieces[:, k] for k in reversed(range(shards))], axis=1)
    return both[0], reversed_taps


def conv_kernel(causal, block, x_ref, taps_ref, o_ref):
    count, channels, rows = x_ref.shape
    length = count * rows
    wide = jnp.broadcast_to(taps_ref[0], (block, taps_ref.shape[2]))
    matrix = pltpu.roll(wide, 0, 1, stride=1, stride_axis=0)[:, block : block + length]
    signal = jnp.concatenate([x_ref[k] for k in range(count)], axis=1)
    zeros = jnp.zeros((channels, length - block), signal.dtype)
    padded = jnp.concatenate([zeros, signal] if causal else [signal, zeros], axis=1)
    steps = length // block
    windows = jnp.concatenate(
        [padded[:, i * block : i * block + length] for i in range(steps)], axis=0
    )
    result = lax.dot_general(
        windows, matrix, (((1,), (1,)), ((), ())),
        precision=precise, preferred_element_type=jnp.float32,
    )
    line = jnp.concatenate(
        [result[i * channels : (i + 1) * channels] for i in range(steps)], axis=1
    )
    for k in range(count):
        o_ref[k] = line[:, k * rows : (k + 1) * rows]


def windowed_conv(padded_taps, chunks, causal, block):
    count, channels, rows = chunks.shape
    groups, _, width = padded_taps.shape
    share = channels // groups
    return pl.pallas_call(
        functools.partial(conv_kernel, causal, block),
        out_shape=jax.ShapeDtypeStruct(chunks.shape, chunks.dtype),
        grid=(groups,),
        in_specs=[
            pl.BlockSpec((count, share, rows), lambda g: (0, g, 0)),
            pl.BlockSpec((1, 1, width), lambda g: (g, 0, 0)),
        ],
        out_specs=pl.BlockSpec((count, share, rows), lambda g: (0, g, 0)),
    )(chunks, padded_taps)


def exchange_kernel(x_ref, o_ref, send_sems, recv_sems, local_sem):
    count = x_ref.shape[0]
    me = lax.axis_index("ctx")
    chip = lax.axis_index("chip")
    core = lax.axis_index("core")
    mesh_id = pl.DeviceIdType.MESH
    barrier = pltpu.get_barrier_semaphore()
    for offset in range(1, count):
        peer = lax.rem(me + offset, count)
        pl.semaphore_signal(barrier, 1, device_id=(peer, chip, core), device_id_type=mesh_id)
    pl.semaphore_wait(barrier, count - 1)
    local = pltpu.make_async_copy(x_ref.at[me], o_ref.at[me], local_sem)
    local.start()
    sends = []
    for offset in range(1, count):
        peer = lax.rem(me + offset, count)
        copy = pltpu.make_async_remote_copy(
            src_ref=x_ref.at[peer],
            dst_ref=o_ref.at[me],
            send_sem=send_sems.at[offset],
            recv_sem=recv_sems.at[offset],
            device_id=(peer, chip, core),
            device_id_type=mesh_id,
        )
        copy.start()
        sends.append(copy)
    for copy in sends:
        copy.wait_send()
    for offset in range(1, count):
        source = lax.rem(me + count - offset, count)
        pltpu.make_async_remote_copy(
            src_ref=x_ref.at[source],
            dst_ref=o_ref.at[source],
            send_sem=send_sems.at[offset],
            recv_sem=recv_sems.at[offset],
            device_id=(source, chip, core),
            device_id_type=mesh_id,
        ).wait_recv()
    local.wait()


def exchange(chunks, collective=0):
    count = chunks.shape[0]
    return pl.pallas_call(
        exchange_kernel,
        out_shape=jax.ShapeDtypeStruct(chunks.shape, chunks.dtype),
        in_specs=[pl.BlockSpec(memory_space=pl.ANY)],
        out_specs=pl.BlockSpec(memory_space=pl.ANY),
        scratch_shapes=[
            pltpu.SemaphoreType.DMA((count,)),
            pltpu.SemaphoreType.DMA((count,)),
            pltpu.SemaphoreType.DMA,
        ],
        compiler_params=pltpu.CompilerParams(collective_id=collective, has_side_effects=True),
    )(chunks)


def to_channels(value):
    rows, channels = value.shape
    count = lax.axis_size("ctx")
    return exchange(value.T.reshape(count, channels // count, rows))


def to_rows(chunks):
    count, channels, rows = chunks.shape
    return exchange(chunks).reshape(count * channels, rows).T


def body(
    token_ids,
    embed_table,
    norm_gain,
    input_weight,
    short_weight,
    filters,
    skip_gain,
    output_weight,
    output_grad,
):
    local_rows = token_ids.shape[0]
    tokens = jnp.take(embed_table, token_ids, axis=0)
    token_values = tokens.astype(jnp.float32)
    inverse_rms = lax.rsqrt(jnp.mean(token_values * token_values, axis=-1, keepdims=True) + 1e-06)
    normed = (token_values * inverse_rms * norm_gain).astype(jnp.bfloat16)
    projected = jnp.einsum("td,djc->tjc", normed, input_weight, preferred_element_type=jnp.float32)
    short_taps = short_weight.shape[0]
    before = from_behind(projected[local_rows - (short_taps - 1) :], "ctx", 1)
    extended = jnp.concatenate([before, projected], axis=0)
    features = sum(
        (
            short_weight[tap_index]
            * extended[short_taps - 1 - tap_index : short_taps - 1 - tap_index + local_rows]
            for tap_index in range(short_taps)
        )
    )
    queries = features[:, 0]
    key_part = features[:, 1]
    value_part = features[:, 2]
    mixture = key_part * value_part
    weight_rows = lax.all_to_all(output_weight, TP, 0, 1, tiled=True)
    chip_weight = lax.all_gather(input_weight, "core", axis=2, tiled=True)
    mixture, weight_rows, chip_weight = lax.optimization_barrier((mixture, weight_rows, chip_weight))

    group_taps, reversed_taps = gather_taps(filters)
    causal_taps, anti_taps = conv_taps(group_taps, reversed_taps, BLOCK)
    long_part = to_rows(windowed_conv(causal_taps, to_channels(mixture), True, BLOCK))
    mixed_out = skip_gain * mixture + long_part
    hidden = (queries * mixed_out).astype(jnp.bfloat16)

    tp_size = lax.axis_size(TP)
    width = token_values.shape[1] // tp_size
    hidden_grad = jnp.dot(output_grad, output_weight, preferred_element_type=jnp.float32)
    mixed_grad = hidden_grad * queries
    hidden, mixed_grad, weight_rows = lax.optimization_barrier((hidden, mixed_grad, weight_rows))
    hidden_wide = lax.all_gather(hidden, TP, axis=1, tiled=True)
    ctx_size = lax.axis_size("ctx")
    weight_partial = jnp.einsum(
        "td,tc->dc", output_grad, hidden, preferred_element_type=jnp.float32
    ).astype(jnp.bfloat16)
    weight_pieces = weight_partial.reshape(ctx_size, -1, weight_partial.shape[1])
    output_weight_grad = jnp.sum(exchange(weight_pieces, 1).astype(jnp.float32), axis=0)
    own_sums = jnp.einsum("tc,dc->td", hidden_wide, weight_rows, preferred_element_type=jnp.float32)
    own_tokens = lax.dynamic_slice_in_dim(token_values, lax.axis_index(TP) * width, width, axis=1)
    own_output = (own_tokens + own_sums).astype(jnp.bfloat16)
    own_output, output_weight_grad, mixed_grad = lax.optimization_barrier(
        (own_output, output_weight_grad, mixed_grad)
    )
    block_output = lax.all_gather(own_output, TP, axis=1, tiled=True)
    carried = to_rows(windowed_conv(anti_taps, to_channels(mixed_grad), False, BLOCK))
    mixture_grad = skip_gain * mixed_grad + carried
    feature_grad = jnp.stack(
        [hidden_grad * mixed_out, mixture_grad * value_part, mixture_grad * key_part], axis=1
    )
    following = from_behind(feature_grad[: short_taps - 1], "ctx", -1)
    extended_grads = jnp.concatenate([feature_grad, following], axis=0)
    projection_grad = sum(
        (
            short_weight[tap_index] * extended_grads[tap_index : tap_index + local_rows]
            for tap_index in range(short_taps)
        )
    ).astype(jnp.bfloat16)
    chips = lax.axis_size("chip")
    cores = lax.axis_size("core")
    row_blocks = projection_grad.reshape(
        chips, cores, local_rows // tp_size, short_taps, projection_grad.shape[2]
    )
    chip_rows = lax.all_to_all(row_blocks, "core", 1, 4, tiled=True)
    chip_rows = chip_rows.reshape(local_rows // cores, short_taps, chip_rows.shape[4])
    partial_grad = jnp.einsum(
        "mjc,djc->md", chip_rows, chip_weight, preferred_element_type=jnp.float32
    ).astype(jnp.bfloat16)
    partial_grad = partial_grad.reshape(chips, local_rows // tp_size, partial_grad.shape[1])
    received = lax.all_to_all(partial_grad, "chip", 0, 0)
    normed_grad = jnp.sum(received.astype(jnp.float32), axis=0)
    return (block_output, output_weight_grad, projection_grad, normed_grad)


def solution(mesh):
    ctx_size, tp_size = mesh.devices.shape
    devices = mesh.devices.reshape(ctx_size, tp_size // 2, 2)
    split_mesh = jax.sharding.Mesh(devices, ("ctx", "chip", "core"))
    in_specs = (
        P("ctx"),
        P(),
        P(),
        P(None, None, TP),
        P(None, None, TP),
        P(TP, "ctx"),
        P(TP),
        P(None, TP),
        P("ctx", None),
    )
    out_specs = (P("ctx", None), P("ctx", TP), P("ctx", None, TP), P(("ctx",) + TP, None))
    return jax.shard_map(body, mesh=split_mesh, in_specs=in_specs, out_specs=out_specs, check_vma=False)
```

```python
import functools

import jax
import jax.numpy as jnp
from jax import lax
from jax.experimental import pallas as pl
from jax.experimental.pallas import tpu as pltpu
from jax.sharding import PartitionSpec as P

precise = lax.Precision.HIGHEST
BLOCK = 256
TP = ("chip", "core")


def from_behind(value, axis, steps):
    count = lax.axis_size(axis)
    first, last = (max(0, -steps), min(count, count - steps))
    return lax.ppermute(value, axis, [(source, source + steps) for source in range(first, last)])


def conv_taps(taps, reversed_taps, block):
    groups, length = taps.shape
    one = jnp.zeros((groups, 1), taps.dtype)
    causal = jnp.concatenate([one, reversed_taps, jnp.zeros((groups, block - 1), taps.dtype)], axis=1)
    anti = jnp.concatenate([jnp.zeros((groups, block), taps.dtype), taps], axis=1)
    return causal[:, None, :], anti[:, None, :]


def gather_taps(filters):
    width = filters.shape[1]
    rows = lax.broadcasted_iota(jnp.int32, (width, width), 0)
    cols = lax.broadcasted_iota(jnp.int32, (width, width), 1)
    exchange = (rows + cols == width - 1).astype(filters.dtype)
    flipped = jnp.dot(filters, exchange, precision=precise)
    both = lax.all_to_all(jnp.stack([filters, flipped]), "ctx", 1, 2, tiled=True)
    shards = lax.axis_size("ctx")
    pieces = both[1].reshape(both.shape[1], shards, width)
    reversed_taps = jnp.concatenate([pieces[:, k] for k in reversed(range(shards))], axis=1)
    return both[0], reversed_taps


def conv_kernel(causal, block, x_ref, taps_ref, o_ref):
    count, channels, rows = x_ref.shape
    length = count * rows
    wide = jnp.broadcast_to(taps_ref[0], (block, taps_ref.shape[2]))
    matrix = pltpu.roll(wide, 0, 1, stride=1, stride_axis=0)[:, block : block + length]
    signal = jnp.concatenate([x_ref[k] for k in range(count)], axis=1)
    zeros = jnp.zeros((channels, length - block), signal.dtype)
    padded = jnp.concatenate([zeros, signal] if causal else [signal, zeros], axis=1)
    steps = length // block
    windows = jnp.concatenate(
        [padded[:, i * block : i * block + length] for i in range(steps)], axis=0
    )
    result = lax.dot_general(
        windows, matrix, (((1,), (1,)), ((), ())),
        precision=precise, preferred_element_type=jnp.float32,
    )
    line = jnp.concatenate(
        [result[i * channels : (i + 1) * channels] for i in range(steps)], axis=1
    )
    for k in range(count):
        o_ref[k] = line[:, k * rows : (k + 1) * rows]


def windowed_conv(padded_taps, chunks, causal, block):
    count, channels, rows = chunks.shape
    groups, _, width = padded_taps.shape
    share = channels // groups
    return pl.pallas_call(
        functools.partial(conv_kernel, causal, block),
        out_shape=jax.ShapeDtypeStruct(chunks.shape, chunks.dtype),
        grid=(groups,),
        in_specs=[
            pl.BlockSpec((count, share, rows), lambda g: (0, g, 0)),
            pl.BlockSpec((1, 1, width), lambda g: (g, 0, 0)),
        ],
        out_specs=pl.BlockSpec((count, share, rows), lambda g: (0, g, 0)),
    )(chunks, padded_taps)


def exchange_kernel(axis, x_ref, o_ref, send_sems, recv_sems, local_sem):
    count = x_ref.shape[0]
    place = {name: lax.axis_index(name) for name in ("ctx", "chip", "core")}
    me = place[axis]

    def device(index):
        return tuple(index if name == axis else place[name] for name in ("ctx", "chip", "core"))

    mesh_id = pl.DeviceIdType.MESH
    barrier = pltpu.get_barrier_semaphore()
    for offset in range(1, count):
        peer = lax.rem(me + offset, count)
        pl.semaphore_signal(barrier, 1, device_id=device(peer), device_id_type=mesh_id)
    pl.semaphore_wait(barrier, count - 1)
    local = pltpu.make_async_copy(x_ref.at[me], o_ref.at[me], local_sem)
    local.start()
    sends = []
    for offset in range(1, count):
        peer = lax.rem(me + offset, count)
        copy = pltpu.make_async_remote_copy(
            src_ref=x_ref.at[peer],
            dst_ref=o_ref.at[me],
            send_sem=send_sems.at[offset],
            recv_sem=recv_sems.at[offset],
            device_id=device(peer),
            device_id_type=mesh_id,
        )
        copy.start()
        sends.append(copy)
    for copy in sends:
        copy.wait_send()
    for offset in range(1, count):
        source = lax.rem(me + count - offset, count)
        pltpu.make_async_remote_copy(
            src_ref=x_ref.at[source],
            dst_ref=o_ref.at[source],
            send_sem=send_sems.at[offset],
            recv_sem=recv_sems.at[offset],
            device_id=device(source),
            device_id_type=mesh_id,
        ).wait_recv()
    local.wait()


def exchange(chunks, collective=0, axis="ctx"):
    count = chunks.shape[0]
    return pl.pallas_call(
        functools.partial(exchange_kernel, axis),
        out_shape=jax.ShapeDtypeStruct(chunks.shape, chunks.dtype),
        in_specs=[pl.BlockSpec(memory_space=pl.ANY)],
        out_specs=pl.BlockSpec(memory_space=pl.ANY),
        scratch_shapes=[
            pltpu.SemaphoreType.DMA((count,)),
            pltpu.SemaphoreType.DMA((count,)),
            pltpu.SemaphoreType.DMA,
        ],
        compiler_params=pltpu.CompilerParams(collective_id=collective, has_side_effects=True),
    )(chunks)


def to_channels(value):
    rows, channels = value.shape
    count = lax.axis_size("ctx")
    return exchange(value.T.reshape(count, channels // count, rows))


def to_rows(chunks):
    count, channels, rows = chunks.shape
    return exchange(chunks).reshape(count * channels, rows).T


def body(
    token_ids,
    embed_table,
    norm_gain,
    input_weight,
    short_weight,
    filters,
    skip_gain,
    output_weight,
    output_grad,
):
    local_rows = token_ids.shape[0]
    tokens = jnp.take(embed_table, token_ids, axis=0)
    token_values = tokens.astype(jnp.float32)
    inverse_rms = lax.rsqrt(jnp.mean(token_values * token_values, axis=-1, keepdims=True) + 1e-06)
    normed = (token_values * inverse_rms * norm_gain).astype(jnp.bfloat16)
    projected = jnp.einsum("td,djc->tjc", normed, input_weight, preferred_element_type=jnp.float32)
    short_taps = short_weight.shape[0]
    before = from_behind(projected[local_rows - (short_taps - 1) :], "ctx", 1)
    extended = jnp.concatenate([before, projected], axis=0)
    features = sum(
        (
            short_weight[tap_index]
            * extended[short_taps - 1 - tap_index : short_taps - 1 - tap_index + local_rows]
            for tap_index in range(short_taps)
        )
    )
    queries = features[:, 0]
    key_part = features[:, 1]
    value_part = features[:, 2]
    mixture = key_part * value_part
    weight_rows = lax.all_to_all(output_weight, TP, 0, 1, tiled=True)
    chip_weight = lax.all_gather(input_weight, "core", axis=2, tiled=True)
    mixture, weight_rows, chip_weight = lax.optimization_barrier((mixture, weight_rows, chip_weight))

    group_taps, reversed_taps = gather_taps(filters)
    causal_taps, anti_taps = conv_taps(group_taps, reversed_taps, BLOCK)
    long_part = to_rows(windowed_conv(causal_taps, to_channels(mixture), True, BLOCK))
    mixed_out = skip_gain * mixture + long_part
    hidden = (queries * mixed_out).astype(jnp.bfloat16)

    tp_size = lax.axis_size(TP)
    width = token_values.shape[1] // tp_size
    hidden_grad = jnp.dot(output_grad, output_weight, preferred_element_type=jnp.float32)
    mixed_grad = hidden_grad * queries
    hidden, mixed_grad, weight_rows = lax.optimization_barrier((hidden, mixed_grad, weight_rows))
    hidden_wide = lax.all_gather(hidden, TP, axis=1, tiled=True)
    ctx_size = lax.axis_size("ctx")
    weight_partial = jnp.einsum(
        "td,tc->dc", output_grad, hidden, preferred_element_type=jnp.float32
    ).astype(jnp.bfloat16)
    weight_pieces = weight_partial.reshape(ctx_size, -1, weight_partial.shape[1])
    output_weight_grad = jnp.sum(exchange(weight_pieces, 1).astype(jnp.float32), axis=0)
    output_weight_grad, mixed_grad = lax.optimization_barrier((output_weight_grad, mixed_grad))
    carried = to_rows(windowed_conv(anti_taps, to_channels(mixed_grad), False, BLOCK))
    hidden_wide, carried = lax.optimization_barrier((hidden_wide, carried))
    own_sums = jnp.einsum("tc,dc->td", hidden_wide, weight_rows, preferred_element_type=jnp.float32)
    own_tokens = lax.dynamic_slice_in_dim(token_values, lax.axis_index(TP) * width, width, axis=1)
    own_output = (own_tokens + own_sums).astype(jnp.bfloat16)
    block_output = lax.all_gather(own_output, TP, axis=1, tiled=True)
    mixture_grad = skip_gain * mixed_grad + carried
    feature_grad = jnp.stack(
        [hidden_grad * mixed_out, mixture_grad * value_part, mixture_grad * key_part], axis=1
    )
    following = from_behind(feature_grad[: short_taps - 1], "ctx", -1)
    extended_grads = jnp.concatenate([feature_grad, following], axis=0)
    projection_grad = sum(
        (
            short_weight[tap_index] * extended_grads[tap_index : tap_index + local_rows]
            for tap_index in range(short_taps)
        )
    ).astype(jnp.bfloat16)
    chips = lax.axis_size("chip")
    cores = lax.axis_size("core")
    row_blocks = projection_grad.reshape(
        chips, cores, local_rows // tp_size, short_taps, projection_grad.shape[2]
    )
    chip_rows = lax.all_to_all(row_blocks, "core", 1, 4, tiled=True)
    chip_rows = chip_rows.reshape(local_rows // cores, short_taps, chip_rows.shape[4])
    partial_grad = jnp.einsum(
        "mjc,djc->md", chip_rows, chip_weight, preferred_element_type=jnp.float32
    ).astype(jnp.bfloat16)
    partial_grad = partial_grad.reshape(chips, local_rows // tp_size, partial_grad.shape[1])
    received = exchange(partial_grad, 2, "chip")
    normed_grad = jnp.sum(received.astype(jnp.float32), axis=0)
    return (block_output, output_weight_grad, projection_grad, normed_grad)


def solution(mesh):
    ctx_size, tp_size = mesh.devices.shape
    devices = mesh.devices.reshape(ctx_size, tp_size // 2, 2)
    split_mesh = jax.sharding.Mesh(devices, ("ctx", "chip", "core"))
    in_specs = (
        P("ctx"),
        P(),
        P(),
        P(None, None, TP),
        P(None, None, TP),
        P(TP, "ctx"),
        P(TP),
        P(None, TP),
        P("ctx", None),
    )
    out_specs = (P("ctx", None), P("ctx", TP), P("ctx", None, TP), P(("ctx",) + TP, None))
    return jax.shard_map(body, mesh=split_mesh, in_specs=in_specs, out_specs=out_specs, check_vma=False)
```

```python
import functools

import jax
import jax.numpy as jnp
from jax import lax
from jax.experimental import pallas as pl
from jax.experimental.pallas import tpu as pltpu
from jax.sharding import PartitionSpec as P

precise = lax.Precision.HIGHEST
BLOCK = 256
TP = ("chip", "core")


def from_behind(value, axis, steps):
    count = lax.axis_size(axis)
    first, last = (max(0, -steps), min(count, count - steps))
    return lax.ppermute(value, axis, [(source, source + steps) for source in range(first, last)])


def conv_taps(taps, reversed_taps, block):
    groups, length = taps.shape
    one = jnp.zeros((groups, 1), taps.dtype)
    causal = jnp.concatenate([one, reversed_taps, jnp.zeros((groups, block - 1), taps.dtype)], axis=1)
    anti = jnp.concatenate([jnp.zeros((groups, block), taps.dtype), taps], axis=1)
    return causal[:, None, :], anti[:, None, :]


def gather_taps(filters):
    width = filters.shape[1]
    rows = lax.broadcasted_iota(jnp.int32, (width, width), 0)
    cols = lax.broadcasted_iota(jnp.int32, (width, width), 1)
    exchange = (rows + cols == width - 1).astype(filters.dtype)
    flipped = jnp.dot(filters, exchange, precision=precise)
    both = lax.all_to_all(jnp.stack([filters, flipped]), "ctx", 1, 2, tiled=True)
    shards = lax.axis_size("ctx")
    pieces = both[1].reshape(both.shape[1], shards, width)
    reversed_taps = jnp.concatenate([pieces[:, k] for k in reversed(range(shards))], axis=1)
    return both[0], reversed_taps


def conv_kernel(causal, block, x_ref, taps_ref, o_ref):
    count, channels, rows = x_ref.shape
    length = count * rows
    wide = jnp.broadcast_to(taps_ref[0], (block, taps_ref.shape[2]))
    matrix = pltpu.roll(wide, 0, 1, stride=1, stride_axis=0)[:, block : block + length]
    signal = jnp.concatenate([x_ref[k] for k in range(count)], axis=1)
    zeros = jnp.zeros((channels, length - block), signal.dtype)
    padded = jnp.concatenate([zeros, signal] if causal else [signal, zeros], axis=1)
    steps = length // block
    windows = jnp.concatenate(
        [padded[:, i * block : i * block + length] for i in range(steps)], axis=0
    )
    result = lax.dot_general(
        windows, matrix, (((1,), (1,)), ((), ())),
        precision=lax.Precision.HIGH, preferred_element_type=jnp.float32,
    )
    line = jnp.concatenate(
        [result[i * channels : (i + 1) * channels] for i in range(steps)], axis=1
    )
    for k in range(count):
        o_ref[k] = line[:, k * rows : (k + 1) * rows]


def windowed_conv(padded_taps, chunks, causal, block):
    count, channels, rows = chunks.shape
    groups, _, width = padded_taps.shape
    share = channels // groups
    return pl.pallas_call(
        functools.partial(conv_kernel, causal, block),
        out_shape=jax.ShapeDtypeStruct(chunks.shape, chunks.dtype),
        grid=(groups,),
        in_specs=[
            pl.BlockSpec((count, share, rows), lambda g: (0, g, 0)),
            pl.BlockSpec((1, 1, width), lambda g: (g, 0, 0)),
        ],
        out_specs=pl.BlockSpec((count, share, rows), lambda g: (0, g, 0)),
    )(chunks, padded_taps)


def exchange_kernel(x_ref, o_ref, send_sems, recv_sems, local_sem):
    count = x_ref.shape[0]
    me = lax.axis_index("ctx")
    chip = lax.axis_index("chip")
    core = lax.axis_index("core")
    mesh_id = pl.DeviceIdType.MESH
    barrier = pltpu.get_barrier_semaphore()
    for offset in range(1, count):
        peer = lax.rem(me + offset, count)
        pl.semaphore_signal(barrier, 1, device_id=(peer, chip, core), device_id_type=mesh_id)
    pl.semaphore_wait(barrier, count - 1)
    local = pltpu.make_async_copy(x_ref.at[me], o_ref.at[me], local_sem)
    local.start()
    sends = []
    for offset in range(1, count):
        peer = lax.rem(me + offset, count)
        copy = pltpu.make_async_remote_copy(
            src_ref=x_ref.at[peer],
            dst_ref=o_ref.at[me],
            send_sem=send_sems.at[offset],
            recv_sem=recv_sems.at[offset],
            device_id=(peer, chip, core),
            device_id_type=mesh_id,
        )
        copy.start()
        sends.append(copy)
    for copy in sends:
        copy.wait_send()
    for offset in range(1, count):
        source = lax.rem(me + count - offset, count)
        pltpu.make_async_remote_copy(
            src_ref=x_ref.at[source],
            dst_ref=o_ref.at[source],
            send_sem=send_sems.at[offset],
            recv_sem=recv_sems.at[offset],
            device_id=(source, chip, core),
            device_id_type=mesh_id,
        ).wait_recv()
    local.wait()


def exchange(chunks, collective=0):
    count = chunks.shape[0]
    return pl.pallas_call(
        exchange_kernel,
        out_shape=jax.ShapeDtypeStruct(chunks.shape, chunks.dtype),
        in_specs=[pl.BlockSpec(memory_space=pl.ANY)],
        out_specs=pl.BlockSpec(memory_space=pl.ANY),
        scratch_shapes=[
            pltpu.SemaphoreType.DMA((count,)),
            pltpu.SemaphoreType.DMA((count,)),
            pltpu.SemaphoreType.DMA,
        ],
        compiler_params=pltpu.CompilerParams(collective_id=collective, has_side_effects=True),
    )(chunks)


def to_channels(value):
    rows, channels = value.shape
    count = lax.axis_size("ctx")
    return exchange(value.T.reshape(count, channels // count, rows))


def to_rows(chunks):
    count, channels, rows = chunks.shape
    return exchange(chunks).reshape(count * channels, rows).T


def body(
    token_ids,
    embed_table,
    norm_gain,
    input_weight,
    short_weight,
    filters,
    skip_gain,
    output_weight,
    output_grad,
):
    local_rows = token_ids.shape[0]
    tokens = jnp.take(embed_table, token_ids, axis=0)
    token_values = tokens.astype(jnp.float32)
    inverse_rms = lax.rsqrt(jnp.mean(token_values * token_values, axis=-1, keepdims=True) + 1e-06)
    normed = (token_values * inverse_rms * norm_gain).astype(jnp.bfloat16)
    projected = jnp.einsum("td,djc->tjc", normed, input_weight, preferred_element_type=jnp.float32)
    short_taps = short_weight.shape[0]
    before = from_behind(projected[local_rows - (short_taps - 1) :], "ctx", 1)
    extended = jnp.concatenate([before, projected], axis=0)
    features = sum(
        (
            short_weight[tap_index]
            * extended[short_taps - 1 - tap_index : short_taps - 1 - tap_index + local_rows]
            for tap_index in range(short_taps)
        )
    )
    queries = features[:, 0]
    key_part = features[:, 1]
    value_part = features[:, 2]
    mixture = key_part * value_part
    weight_rows = lax.all_to_all(output_weight, TP, 0, 1, tiled=True)
    chip_weight = lax.all_gather(input_weight, "core", axis=2, tiled=True)
    mixture, weight_rows, chip_weight = lax.optimization_barrier((mixture, weight_rows, chip_weight))

    group_taps, reversed_taps = gather_taps(filters)
    causal_taps, anti_taps = conv_taps(group_taps, reversed_taps, BLOCK)
    long_part = to_rows(windowed_conv(causal_taps, to_channels(mixture), True, BLOCK))
    mixed_out = skip_gain * mixture + long_part
    hidden = (queries * mixed_out).astype(jnp.bfloat16)

    tp_size = lax.axis_size(TP)
    width = token_values.shape[1] // tp_size
    hidden_grad = jnp.dot(output_grad, output_weight, preferred_element_type=jnp.float32)
    mixed_grad = hidden_grad * queries
    hidden, mixed_grad, weight_rows = lax.optimization_barrier((hidden, mixed_grad, weight_rows))
    hidden_wide = lax.all_gather(hidden, TP, axis=1, tiled=True)
    ctx_size = lax.axis_size("ctx")
    weight_partial = jnp.einsum(
        "td,tc->dc", output_grad, hidden, preferred_element_type=jnp.float32
    ).astype(jnp.bfloat16)
    weight_pieces = weight_partial.reshape(ctx_size, -1, weight_partial.shape[1])
    output_weight_grad = jnp.sum(exchange(weight_pieces, 1).astype(jnp.float32), axis=0)
    output_weight_grad, mixed_grad = lax.optimization_barrier((output_weight_grad, mixed_grad))
    carried = to_rows(windowed_conv(anti_taps, to_channels(mixed_grad), False, BLOCK))
    hidden_wide, carried = lax.optimization_barrier((hidden_wide, carried))
    own_sums = jnp.einsum("tc,dc->td", hidden_wide, weight_rows, preferred_element_type=jnp.float32)
    own_tokens = lax.dynamic_slice_in_dim(token_values, lax.axis_index(TP) * width, width, axis=1)
    own_output = (own_tokens + own_sums).astype(jnp.bfloat16)
    block_output = lax.all_gather(own_output, TP, axis=1, tiled=True)
    mixture_grad = skip_gain * mixed_grad + carried
    feature_grad = jnp.stack(
        [hidden_grad * mixed_out, mixture_grad * value_part, mixture_grad * key_part], axis=1
    )
    following = from_behind(feature_grad[: short_taps - 1], "ctx", -1)
    extended_grads = jnp.concatenate([feature_grad, following], axis=0)
    projection_grad = sum(
        (
            short_weight[tap_index] * extended_grads[tap_index : tap_index + local_rows]
            for tap_index in range(short_taps)
        )
    ).astype(jnp.bfloat16)
    chips = lax.axis_size("chip")
    cores = lax.axis_size("core")
    row_blocks = projection_grad.reshape(
        chips, cores, local_rows // tp_size, short_taps, projection_grad.shape[2]
    )
    chip_rows = lax.all_to_all(row_blocks, "core", 1, 4, tiled=True)
    chip_rows = chip_rows.reshape(local_rows // cores, short_taps, chip_rows.shape[4])
    partial_grad = jnp.einsum(
        "mjc,djc->md", chip_rows, chip_weight, preferred_element_type=jnp.float32
    ).astype(jnp.bfloat16)
    partial_grad = partial_grad.reshape(chips, local_rows // tp_size, partial_grad.shape[1])
    received = lax.all_to_all(partial_grad, "chip", 0, 0)
    normed_grad = jnp.sum(received.astype(jnp.float32), axis=0)
    return (block_output, output_weight_grad, projection_grad, normed_grad)


def solution(mesh):
    ctx_size, tp_size = mesh.devices.shape
    devices = mesh.devices.reshape(ctx_size, tp_size // 2, 2)
    split_mesh = jax.sharding.Mesh(devices, ("ctx", "chip", "core"))
    in_specs = (
        P("ctx"),
        P(),
        P(),
        P(None, None, TP),
        P(None, None, TP),
        P(TP, "ctx"),
        P(TP),
        P(None, TP),
        P("ctx", None),
    )
    out_specs = (P("ctx", None), P("ctx", TP), P("ctx", None, TP), P(("ctx",) + TP, None))
    return jax.shard_map(body, mesh=split_mesh, in_specs=in_specs, out_specs=out_specs, check_vma=False)
```

```python
import functools

import jax
import jax.numpy as jnp
from jax import lax
from jax.experimental import pallas as pl
from jax.experimental.pallas import tpu as pltpu
from jax.sharding import PartitionSpec as P

precise = lax.Precision.HIGHEST
BLOCK = 256
TP = ("chip", "core")


def from_behind(value, axis, steps):
    count = lax.axis_size(axis)
    first, last = (max(0, -steps), min(count, count - steps))
    return lax.ppermute(value, axis, [(source, source + steps) for source in range(first, last)])


def conv_taps(taps, reversed_taps, block):
    groups, length = taps.shape
    one = jnp.zeros((groups, 1), taps.dtype)
    causal = jnp.concatenate([one, reversed_taps, jnp.zeros((groups, block - 1), taps.dtype)], axis=1)
    anti = jnp.concatenate([jnp.zeros((groups, block), taps.dtype), taps], axis=1)
    return causal[:, None, :], anti[:, None, :]


def gather_taps(filters):
    width = filters.shape[1]
    rows = lax.broadcasted_iota(jnp.int32, (width, width), 0)
    cols = lax.broadcasted_iota(jnp.int32, (width, width), 1)
    exchange = (rows + cols == width - 1).astype(filters.dtype)
    flipped = jnp.dot(filters, exchange, precision=precise)
    both = lax.all_to_all(jnp.stack([filters, flipped]), "ctx", 1, 2, tiled=True)
    shards = lax.axis_size("ctx")
    pieces = both[1].reshape(both.shape[1], shards, width)
    reversed_taps = jnp.concatenate([pieces[:, k] for k in reversed(range(shards))], axis=1)
    return both[0], reversed_taps


def conv_kernel(causal, block, x_ref, taps_ref, o_ref):
    count, channels, rows = x_ref.shape
    length = count * rows
    wide = jnp.broadcast_to(taps_ref[0], (block, taps_ref.shape[2]))
    matrix = pltpu.roll(wide, 0, 1, stride=1, stride_axis=0)[:, block : block + length]
    signal = jnp.concatenate([x_ref[k] for k in range(count)], axis=1)
    zeros = jnp.zeros((channels, length - block), signal.dtype)
    padded = jnp.concatenate([zeros, signal] if causal else [signal, zeros], axis=1)
    steps = length // block
    windows = jnp.concatenate(
        [padded[:, i * block : i * block + length] for i in range(steps)], axis=0
    )
    result = lax.dot_general(
        windows, matrix, (((1,), (1,)), ((), ())),
        precision=lax.Precision.HIGH, preferred_element_type=jnp.float32,
    )
    line = jnp.concatenate(
        [result[i * channels : (i + 1) * channels] for i in range(steps)], axis=1
    )
    for k in range(count):
        o_ref[k] = line[:, k * rows : (k + 1) * rows]


def windowed_conv(padded_taps, chunks, causal, block):
    count, channels, rows = chunks.shape
    groups, _, width = padded_taps.shape
    share = channels // groups
    return pl.pallas_call(
        functools.partial(conv_kernel, causal, block),
        out_shape=jax.ShapeDtypeStruct(chunks.shape, chunks.dtype),
        grid=(groups,),
        in_specs=[
            pl.BlockSpec((count, share, rows), lambda g: (0, g, 0)),
            pl.BlockSpec((1, 1, width), lambda g: (g, 0, 0)),
        ],
        out_specs=pl.BlockSpec((count, share, rows), lambda g: (0, g, 0)),
    )(chunks, padded_taps)


def exchange_kernel(x_ref, o_ref, send_sems, recv_sems, local_sem):
    count = x_ref.shape[0]
    me = lax.axis_index("ctx")
    chip = lax.axis_index("chip")
    core = lax.axis_index("core")
    mesh_id = pl.DeviceIdType.MESH
    barrier = pltpu.get_barrier_semaphore()
    for offset in range(1, count):
        peer = lax.rem(me + offset, count)
        pl.semaphore_signal(barrier, 1, device_id=(peer, chip, core), device_id_type=mesh_id)
    pl.semaphore_wait(barrier, count - 1)
    local = pltpu.make_async_copy(x_ref.at[me], o_ref.at[me], local_sem)
    local.start()
    sends = []
    for offset in range(1, count):
        peer = lax.rem(me + offset, count)
        copy = pltpu.make_async_remote_copy(
            src_ref=x_ref.at[peer],
            dst_ref=o_ref.at[me],
            send_sem=send_sems.at[offset],
            recv_sem=recv_sems.at[offset],
            device_id=(peer, chip, core),
            device_id_type=mesh_id,
        )
        copy.start()
        sends.append(copy)
    for copy in sends:
        copy.wait_send()
    for offset in range(1, count):
        source = lax.rem(me + count - offset, count)
        pltpu.make_async_remote_copy(
            src_ref=x_ref.at[source],
            dst_ref=o_ref.at[source],
            send_sem=send_sems.at[offset],
            recv_sem=recv_sems.at[offset],
            device_id=(source, chip, core),
            device_id_type=mesh_id,
        ).wait_recv()
    local.wait()


def exchange(chunks, collective=0):
    count = chunks.shape[0]
    return pl.pallas_call(
        exchange_kernel,
        out_shape=jax.ShapeDtypeStruct(chunks.shape, chunks.dtype),
        in_specs=[pl.BlockSpec(memory_space=pl.ANY)],
        out_specs=pl.BlockSpec(memory_space=pl.ANY),
        scratch_shapes=[
            pltpu.SemaphoreType.DMA((count,)),
            pltpu.SemaphoreType.DMA((count,)),
            pltpu.SemaphoreType.DMA,
        ],
        compiler_params=pltpu.CompilerParams(collective_id=collective, has_side_effects=True),
    )(chunks)


def to_channels(value):
    rows, channels = value.shape
    count = lax.axis_size("ctx")
    return exchange(value.T.reshape(count, channels // count, rows))


def to_rows(chunks):
    count, channels, rows = chunks.shape
    return exchange(chunks).reshape(count * channels, rows).T


def body(
    token_ids,
    embed_table,
    norm_gain,
    input_weight,
    short_weight,
    filters,
    skip_gain,
    output_weight,
    output_grad,
):
    local_rows = token_ids.shape[0]
    vocab = embed_table.shape[0]
    picks = (token_ids[:, None] == lax.broadcasted_iota(jnp.int32, (1, vocab), 1)).astype(embed_table.dtype)
    tokens = jnp.dot(picks, embed_table, preferred_element_type=jnp.float32).astype(embed_table.dtype)
    token_values = tokens.astype(jnp.float32)
    inverse_rms = lax.rsqrt(jnp.mean(token_values * token_values, axis=-1, keepdims=True) + 1e-06)
    normed = (token_values * inverse_rms * norm_gain).astype(jnp.bfloat16)
    projected = jnp.einsum("td,djc->tjc", normed, input_weight, preferred_element_type=jnp.float32)
    short_taps = short_weight.shape[0]
    before = from_behind(projected[local_rows - (short_taps - 1) :], "ctx", 1)
    extended = jnp.concatenate([before, projected], axis=0)
    features = sum(
        (
            short_weight[tap_index]
            * extended[short_taps - 1 - tap_index : short_taps - 1 - tap_index + local_rows]
            for tap_index in range(short_taps)
        )
    )
    queries = features[:, 0]
    key_part = features[:, 1]
    value_part = features[:, 2]
    mixture = key_part * value_part
    weight_rows = lax.all_to_all(output_weight, TP, 0, 1, tiled=True)
    chip_weight = lax.all_gather(input_weight, "core", axis=2, tiled=True)
    mixture, weight_rows, chip_weight = lax.optimization_barrier((mixture, weight_rows, chip_weight))

    group_taps, reversed_taps = gather_taps(filters)
    causal_taps, anti_taps = conv_taps(group_taps, reversed_taps, BLOCK)
    long_part = to_rows(windowed_conv(causal_taps, to_channels(mixture), True, BLOCK))
    mixed_out = skip_gain * mixture + long_part
    hidden = (queries * mixed_out).astype(jnp.bfloat16)

    tp_size = lax.axis_size(TP)
    width = token_values.shape[1] // tp_size
    hidden_grad = jnp.dot(output_grad, output_weight, preferred_element_type=jnp.float32)
    mixed_grad = hidden_grad * queries
    hidden, mixed_grad, weight_rows = lax.optimization_barrier((hidden, mixed_grad, weight_rows))
    hidden_wide = lax.all_gather(hidden, TP, axis=1, tiled=True)
    ctx_size = lax.axis_size("ctx")
    weight_partial = jnp.einsum(
        "td,tc->dc", output_grad, hidden, preferred_element_type=jnp.float32
    ).astype(jnp.bfloat16)
    weight_pieces = weight_partial.reshape(ctx_size, -1, weight_partial.shape[1])
    output_weight_grad = jnp.sum(exchange(weight_pieces, 1).astype(jnp.float32), axis=0)
    output_weight_grad, mixed_grad = lax.optimization_barrier((output_weight_grad, mixed_grad))
    carried = to_rows(windowed_conv(anti_taps, to_channels(mixed_grad), False, BLOCK))
    hidden_wide, carried = lax.optimization_barrier((hidden_wide, carried))
    own_sums = jnp.einsum("tc,dc->td", hidden_wide, weight_rows, preferred_element_type=jnp.float32)
    own_tokens = lax.dynamic_slice_in_dim(token_values, lax.axis_index(TP) * width, width, axis=1)
    own_output = (own_tokens + own_sums).astype(jnp.bfloat16)
    block_output = lax.all_gather(own_output, TP, axis=1, tiled=True)
    mixture_grad = skip_gain * mixed_grad + carried
    feature_grad = jnp.stack(
        [hidden_grad * mixed_out, mixture_grad * value_part, mixture_grad * key_part], axis=1
    )
    following = from_behind(feature_grad[: short_taps - 1], "ctx", -1)
    extended_grads = jnp.concatenate([feature_grad, following], axis=0)
    projection_grad = sum(
        (
            short_weight[tap_index] * extended_grads[tap_index : tap_index + local_rows]
            for tap_index in range(short_taps)
        )
    ).astype(jnp.bfloat16)
    chips = lax.axis_size("chip")
    cores = lax.axis_size("core")
    row_blocks = projection_grad.reshape(
        chips, cores, local_rows // tp_size, short_taps, projection_grad.shape[2]
    )
    chip_rows = lax.all_to_all(row_blocks, "core", 1, 4, tiled=True)
    chip_rows = chip_rows.reshape(local_rows // cores, short_taps, chip_rows.shape[4])
    partial_grad = jnp.einsum(
        "mjc,djc->md", chip_rows, chip_weight, preferred_element_type=jnp.float32
    ).astype(jnp.bfloat16)
    partial_grad = partial_grad.reshape(chips, local_rows // tp_size, partial_grad.shape[1])
    received = lax.all_to_all(partial_grad, "chip", 0, 0)
    normed_grad = jnp.sum(received.astype(jnp.float32), axis=0)
    return (block_output, output_weight_grad, projection_grad, normed_grad)


def solution(mesh):
    ctx_size, tp_size = mesh.devices.shape
    devices = mesh.devices.reshape(ctx_size, tp_size // 2, 2)
    split_mesh = jax.sharding.Mesh(devices, ("ctx", "chip", "core"))
    in_specs = (
        P("ctx"),
        P(),
        P(),
        P(None, None, TP),
        P(None, None, TP),
        P(TP, "ctx"),
        P(TP),
        P(None, TP),
        P("ctx", None),
    )
    out_specs = (P("ctx", None), P("ctx", TP), P("ctx", None, TP), P(("ctx",) + TP, None))
    return jax.shard_map(body, mesh=split_mesh, in_specs=in_specs, out_specs=out_specs, check_vma=False)
```

```python
import functools

import jax
import jax.numpy as jnp
from jax import lax
from jax.experimental import pallas as pl
from jax.experimental.pallas import tpu as pltpu
from jax.sharding import PartitionSpec as P

precise = lax.Precision.HIGHEST
BLOCK = 256
TP = ("chip", "core")


def from_behind(value, axis, steps):
    count = lax.axis_size(axis)
    first, last = (max(0, -steps), min(count, count - steps))
    return lax.ppermute(value, axis, [(source, source + steps) for source in range(first, last)])


def conv_taps(taps, reversed_taps, block):
    groups, length = taps.shape
    one = jnp.zeros((groups, 1), taps.dtype)
    causal = jnp.concatenate([one, reversed_taps, jnp.zeros((groups, block - 1), taps.dtype)], axis=1)
    anti = jnp.concatenate([jnp.zeros((groups, block), taps.dtype), taps], axis=1)
    return causal[:, None, :], anti[:, None, :]


def gather_taps(filters):
    width = filters.shape[1]
    rows = lax.broadcasted_iota(jnp.int32, (width, width), 0)
    cols = lax.broadcasted_iota(jnp.int32, (width, width), 1)
    exchange = (rows + cols == width - 1).astype(filters.dtype)
    flipped = jnp.dot(filters, exchange, precision=precise)
    both = lax.all_to_all(jnp.stack([filters, flipped]), "ctx", 1, 2, tiled=True)
    shards = lax.axis_size("ctx")
    pieces = both[1].reshape(both.shape[1], shards, width)
    reversed_taps = jnp.concatenate([pieces[:, k] for k in reversed(range(shards))], axis=1)
    return both[0], reversed_taps


def conv_kernel(causal, block, x_ref, taps_ref, o_ref):
    count, channels, rows = x_ref.shape
    length = count * rows
    wide = jnp.broadcast_to(taps_ref[0], (block, taps_ref.shape[2]))
    matrix = pltpu.roll(wide, 0, 1, stride=1, stride_axis=0)[:, block : block + length]
    signal = jnp.concatenate([x_ref[k] for k in range(count)], axis=1)
    zeros = jnp.zeros((channels, length - block), signal.dtype)
    padded = jnp.concatenate([zeros, signal] if causal else [signal, zeros], axis=1)
    steps = length // block
    windows = jnp.concatenate(
        [padded[:, i * block : i * block + length] for i in range(steps)], axis=0
    )
    result = lax.dot_general(
        windows, matrix, (((1,), (1,)), ((), ())),
        precision=lax.Precision.HIGH, preferred_element_type=jnp.float32,
    )
    line = jnp.concatenate(
        [result[i * channels : (i + 1) * channels] for i in range(steps)], axis=1
    )
    for k in range(count):
        o_ref[k] = line[:, k * rows : (k + 1) * rows]


def windowed_conv(padded_taps, chunks, causal, block):
    count, channels, rows = chunks.shape
    groups, _, width = padded_taps.shape
    share = channels // groups
    return pl.pallas_call(
        functools.partial(conv_kernel, causal, block),
        out_shape=jax.ShapeDtypeStruct(chunks.shape, chunks.dtype),
        grid=(groups,),
        in_specs=[
            pl.BlockSpec((count, share, rows), lambda g: (0, g, 0)),
            pl.BlockSpec((1, 1, width), lambda g: (g, 0, 0)),
        ],
        out_specs=pl.BlockSpec((count, share, rows), lambda g: (0, g, 0)),
    )(chunks, padded_taps)


def exchange_kernel(axis, parts, *refs):
    inputs, outputs = refs[:parts], refs[parts : 2 * parts]
    send_sems, recv_sems, local_sems = refs[2 * parts :]
    count = inputs[0].shape[0]
    place = {name: lax.axis_index(name) for name in ("ctx", "chip", "core")}
    me = place[axis]

    def device(index):
        return tuple(index if name == axis else place[name] for name in ("ctx", "chip", "core"))

    mesh_id = pl.DeviceIdType.MESH
    barrier = pltpu.get_barrier_semaphore()
    for offset in range(1, count):
        peer = lax.rem(me + offset, count)
        pl.semaphore_signal(barrier, 1, device_id=device(peer), device_id_type=mesh_id)
    pl.semaphore_wait(barrier, count - 1)
    locals_ = []
    sends = []
    for part in range(parts):
        x_ref, o_ref = inputs[part], outputs[part]
        local = pltpu.make_async_copy(x_ref.at[me], o_ref.at[me], local_sems.at[part])
        local.start()
        locals_.append(local)
        for offset in range(1, count):
            peer = lax.rem(me + offset, count)
            copy = pltpu.make_async_remote_copy(
                src_ref=x_ref.at[peer],
                dst_ref=o_ref.at[me],
                send_sem=send_sems.at[part, offset],
                recv_sem=recv_sems.at[part, offset],
                device_id=device(peer),
                device_id_type=mesh_id,
            )
            copy.start()
            sends.append(copy)
    for copy in sends:
        copy.wait_send()
    for part in range(parts):
        x_ref, o_ref = inputs[part], outputs[part]
        for offset in range(1, count):
            source = lax.rem(me + count - offset, count)
            pltpu.make_async_remote_copy(
                src_ref=x_ref.at[source],
                dst_ref=o_ref.at[source],
                send_sem=send_sems.at[part, offset],
                recv_sem=recv_sems.at[part, offset],
                device_id=device(source),
                device_id_type=mesh_id,
            ).wait_recv()
    for local in locals_:
        local.wait()


def exchange_many(chunk_list, collective, axis="ctx"):
    parts = len(chunk_list)
    count = chunk_list[0].shape[0]
    return pl.pallas_call(
        functools.partial(exchange_kernel, axis, parts),
        out_shape=[jax.ShapeDtypeStruct(c.shape, c.dtype) for c in chunk_list],
        in_specs=[pl.BlockSpec(memory_space=pl.ANY)] * parts,
        out_specs=[pl.BlockSpec(memory_space=pl.ANY)] * parts,
        scratch_shapes=[
            pltpu.SemaphoreType.DMA((parts, count)),
            pltpu.SemaphoreType.DMA((parts, count)),
            pltpu.SemaphoreType.DMA((parts,)),
        ],
        compiler_params=pltpu.CompilerParams(collective_id=collective, has_side_effects=True),
    )(*chunk_list)


def exchange(chunks, collective=0, axis="ctx"):
    return exchange_many([chunks], collective, axis)[0]


def channel_chunks(value):
    rows, channels = value.shape
    count = lax.axis_size("ctx")
    return value.T.reshape(count, channels // count, rows)


def to_channels(value):
    return exchange(channel_chunks(value))


def to_rows(chunks):
    count, channels, rows = chunks.shape
    return exchange(chunks).reshape(count * channels, rows).T


def body(
    token_ids,
    embed_table,
    norm_gain,
    input_weight,
    short_weight,
    filters,
    skip_gain,
    output_weight,
    output_grad,
):
    local_rows = token_ids.shape[0]
    vocab = embed_table.shape[0]
    picks = (token_ids[:, None] == lax.broadcasted_iota(jnp.int32, (1, vocab), 1)).astype(embed_table.dtype)
    tokens = jnp.dot(picks, embed_table, preferred_element_type=jnp.float32).astype(embed_table.dtype)
    token_values = tokens.astype(jnp.float32)
    inverse_rms = lax.rsqrt(jnp.mean(token_values * token_values, axis=-1, keepdims=True) + 1e-06)
    normed = (token_values * inverse_rms * norm_gain).astype(jnp.bfloat16)
    projected = jnp.einsum("td,djc->tjc", normed, input_weight, preferred_element_type=jnp.float32)
    short_taps = short_weight.shape[0]
    before = from_behind(projected[local_rows - (short_taps - 1) :], "ctx", 1)
    extended = jnp.concatenate([before, projected], axis=0)
    features = sum(
        (
            short_weight[tap_index]
            * extended[short_taps - 1 - tap_index : short_taps - 1 - tap_index + local_rows]
            for tap_index in range(short_taps)
        )
    )
    queries = features[:, 0]
    key_part = features[:, 1]
    value_part = features[:, 2]
    mixture = key_part * value_part
    weight_rows = lax.all_to_all(output_weight, TP, 0, 1, tiled=True)
    chip_weight = lax.all_gather(input_weight, "core", axis=2, tiled=True)
    mixture, weight_rows, chip_weight = lax.optimization_barrier((mixture, weight_rows, chip_weight))

    group_taps, reversed_taps = gather_taps(filters)
    causal_taps, anti_taps = conv_taps(group_taps, reversed_taps, BLOCK)
    long_part = to_rows(windowed_conv(causal_taps, to_channels(mixture), True, BLOCK))
    mixed_out = skip_gain * mixture + long_part
    hidden = (queries * mixed_out).astype(jnp.bfloat16)

    tp_size = lax.axis_size(TP)
    width = token_values.shape[1] // tp_size
    hidden_grad = jnp.dot(output_grad, output_weight, preferred_element_type=jnp.float32)
    mixed_grad = hidden_grad * queries
    hidden, mixed_grad, weight_rows = lax.optimization_barrier((hidden, mixed_grad, weight_rows))
    hidden_wide = lax.all_gather(hidden, TP, axis=1, tiled=True)
    ctx_size = lax.axis_size("ctx")
    weight_partial = jnp.einsum(
        "td,tc->dc", output_grad, hidden, preferred_element_type=jnp.float32
    ).astype(jnp.bfloat16)
    weight_pieces = weight_partial.reshape(ctx_size, -1, weight_partial.shape[1])
    grad_chunks, weight_received = exchange_many([channel_chunks(mixed_grad), weight_pieces], 1)
    output_weight_grad = jnp.sum(weight_received.astype(jnp.float32), axis=0)
    carried = to_rows(windowed_conv(anti_taps, grad_chunks, False, BLOCK))
    hidden_wide, carried = lax.optimization_barrier((hidden_wide, carried))
    own_sums = jnp.einsum("tc,dc->td", hidden_wide, weight_rows, preferred_element_type=jnp.float32)
    own_tokens = lax.dynamic_slice_in_dim(token_values, lax.axis_index(TP) * width, width, axis=1)
    own_output = (own_tokens + own_sums).astype(jnp.bfloat16)
    block_output = lax.all_gather(own_output, TP, axis=1, tiled=True)
    mixture_grad = skip_gain * mixed_grad + carried
    feature_grad = jnp.stack(
        [hidden_grad * mixed_out, mixture_grad * value_part, mixture_grad * key_part], axis=1
    )
    following = from_behind(feature_grad[: short_taps - 1], "ctx", -1)
    extended_grads = jnp.concatenate([feature_grad, following], axis=0)
    projection_grad = sum(
        (
            short_weight[tap_index] * extended_grads[tap_index : tap_index + local_rows]
            for tap_index in range(short_taps)
        )
    ).astype(jnp.bfloat16)
    chips = lax.axis_size("chip")
    cores = lax.axis_size("core")
    row_blocks = projection_grad.reshape(
        chips, cores, local_rows // tp_size, short_taps, projection_grad.shape[2]
    )
    chip_rows = lax.all_to_all(row_blocks, "core", 1, 4, tiled=True)
    chip_rows = chip_rows.reshape(local_rows // cores, short_taps, chip_rows.shape[4])
    partial_grad = jnp.einsum(
        "mjc,djc->md", chip_rows, chip_weight, preferred_element_type=jnp.float32
    ).astype(jnp.bfloat16)
    partial_grad = partial_grad.reshape(chips, local_rows // tp_size, partial_grad.shape[1])
    received = lax.all_to_all(partial_grad, "chip", 0, 0)
    normed_grad = jnp.sum(received.astype(jnp.float32), axis=0)
    return (block_output, output_weight_grad, projection_grad, normed_grad)


def solution(mesh):
    ctx_size, tp_size = mesh.devices.shape
    devices = mesh.devices.reshape(ctx_size, tp_size // 2, 2)
    split_mesh = jax.sharding.Mesh(devices, ("ctx", "chip", "core"))
    in_specs = (
        P("ctx"),
        P(),
        P(),
        P(None, None, TP),
        P(None, None, TP),
        P(TP, "ctx"),
        P(TP),
        P(None, TP),
        P("ctx", None),
    )
    out_specs = (P("ctx", None), P("ctx", TP), P("ctx", None, TP), P(("ctx",) + TP, None))
    return jax.shard_map(body, mesh=split_mesh, in_specs=in_specs, out_specs=out_specs, check_vma=False)
```

```python
import functools

import jax
import jax.numpy as jnp
from jax import lax
from jax.experimental import pallas as pl
from jax.experimental.pallas import tpu as pltpu
from jax.sharding import PartitionSpec as P

precise = lax.Precision.HIGHEST
BLOCK = 256
TP = ("chip", "core")


def from_behind(value, axis, steps):
    count = lax.axis_size(axis)
    first, last = (max(0, -steps), min(count, count - steps))
    return lax.ppermute(value, axis, [(source, source + steps) for source in range(first, last)])


def conv_taps(taps, reversed_taps, block):
    groups, length = taps.shape
    one = jnp.zeros((groups, 1), taps.dtype)
    causal = jnp.concatenate([one, reversed_taps, jnp.zeros((groups, block - 1), taps.dtype)], axis=1)
    anti = jnp.concatenate([jnp.zeros((groups, block), taps.dtype), taps], axis=1)
    return causal[:, None, :], anti[:, None, :]


def tap_chunks(filters):
    width = filters.shape[1]
    rows = lax.broadcasted_iota(jnp.int32, (width, width), 0)
    cols = lax.broadcasted_iota(jnp.int32, (width, width), 1)
    exchange_matrix = (rows + cols == width - 1).astype(filters.dtype)
    flipped = jnp.dot(filters, exchange_matrix, precision=precise)
    shards = lax.axis_size("ctx")
    both = jnp.stack([filters, flipped]).reshape(2, shards, filters.shape[0] // shards, width)
    return both.transpose(1, 0, 2, 3)


def taps_from(received):
    shards, _, groups, width = received.shape
    both = received.transpose(1, 2, 0, 3).reshape(2, groups, shards * width)
    pieces = both[1].reshape(groups, shards, width)
    reversed_taps = jnp.concatenate([pieces[:, k] for k in reversed(range(shards))], axis=1)
    return both[0], reversed_taps


def conv_kernel(causal, block, x_ref, taps_ref, o_ref):
    count, channels, rows = x_ref.shape
    length = count * rows
    wide = jnp.broadcast_to(taps_ref[0], (block, taps_ref.shape[2]))
    matrix = pltpu.roll(wide, 0, 1, stride=1, stride_axis=0)[:, block : block + length]
    signal = jnp.concatenate([x_ref[k] for k in range(count)], axis=1)
    zeros = jnp.zeros((channels, length - block), signal.dtype)
    padded = jnp.concatenate([zeros, signal] if causal else [signal, zeros], axis=1)
    steps = length // block
    windows = jnp.concatenate(
        [padded[:, i * block : i * block + length] for i in range(steps)], axis=0
    )
    result = lax.dot_general(
        windows, matrix, (((1,), (1,)), ((), ())),
        precision=lax.Precision.HIGH, preferred_element_type=jnp.float32,
    )
    line = jnp.concatenate(
        [result[i * channels : (i + 1) * channels] for i in range(steps)], axis=1
    )
    for k in range(count):
        o_ref[k] = line[:, k * rows : (k + 1) * rows]


def windowed_conv(padded_taps, chunks, causal, block):
    count, channels, rows = chunks.shape
    groups, _, width = padded_taps.shape
    share = channels // groups
    return pl.pallas_call(
        functools.partial(conv_kernel, causal, block),
        out_shape=jax.ShapeDtypeStruct(chunks.shape, chunks.dtype),
        grid=(groups,),
        in_specs=[
            pl.BlockSpec((count, share, rows), lambda g: (0, g, 0)),
            pl.BlockSpec((1, 1, width), lambda g: (g, 0, 0)),
        ],
        out_specs=pl.BlockSpec((count, share, rows), lambda g: (0, g, 0)),
    )(chunks, padded_taps)


def exchange_kernel(axis, parts, *refs):
    inputs, outputs = refs[:parts], refs[parts : 2 * parts]
    send_sems, recv_sems, local_sems = refs[2 * parts :]
    count = inputs[0].shape[0]
    place = {name: lax.axis_index(name) for name in ("ctx", "chip", "core")}
    me = place[axis]

    def device(index):
        return tuple(index if name == axis else place[name] for name in ("ctx", "chip", "core"))

    mesh_id = pl.DeviceIdType.MESH
    barrier = pltpu.get_barrier_semaphore()
    for offset in range(1, count):
        peer = lax.rem(me + offset, count)
        pl.semaphore_signal(barrier, 1, device_id=device(peer), device_id_type=mesh_id)
    pl.semaphore_wait(barrier, count - 1)
    locals_ = []
    sends = []
    for part in range(parts):
        x_ref, o_ref = inputs[part], outputs[part]
        local = pltpu.make_async_copy(x_ref.at[me], o_ref.at[me], local_sems.at[part])
        local.start()
        locals_.append(local)
        for offset in range(1, count):
            peer = lax.rem(me + offset, count)
            copy = pltpu.make_async_remote_copy(
                src_ref=x_ref.at[peer],
                dst_ref=o_ref.at[me],
                send_sem=send_sems.at[part, offset],
                recv_sem=recv_sems.at[part, offset],
                device_id=device(peer),
                device_id_type=mesh_id,
            )
            copy.start()
            sends.append(copy)
    for copy in sends:
        copy.wait_send()
    for part in range(parts):
        x_ref, o_ref = inputs[part], outputs[part]
        for offset in range(1, count):
            source = lax.rem(me + count - offset, count)
            pltpu.make_async_remote_copy(
                src_ref=x_ref.at[source],
                dst_ref=o_ref.at[source],
                send_sem=send_sems.at[part, offset],
                recv_sem=recv_sems.at[part, offset],
                device_id=device(source),
                device_id_type=mesh_id,
            ).wait_recv()
    for local in locals_:
        local.wait()


def exchange_many(chunk_list, collective, axis="ctx"):
    parts = len(chunk_list)
    count = chunk_list[0].shape[0]
    return pl.pallas_call(
        functools.partial(exchange_kernel, axis, parts),
        out_shape=[jax.ShapeDtypeStruct(c.shape, c.dtype) for c in chunk_list],
        in_specs=[pl.BlockSpec(memory_space=pl.ANY)] * parts,
        out_specs=[pl.BlockSpec(memory_space=pl.ANY)] * parts,
        scratch_shapes=[
            pltpu.SemaphoreType.DMA((parts, count)),
            pltpu.SemaphoreType.DMA((parts, count)),
            pltpu.SemaphoreType.DMA((parts,)),
        ],
        compiler_params=pltpu.CompilerParams(collective_id=collective, has_side_effects=True),
    )(*chunk_list)


def exchange(chunks, collective=0, axis="ctx"):
    return exchange_many([chunks], collective, axis)[0]


def channel_chunks(value):
    rows, channels = value.shape
    count = lax.axis_size("ctx")
    return value.T.reshape(count, channels // count, rows)


def to_channels(value):
    return exchange(channel_chunks(value))


def to_rows(chunks):
    count, channels, rows = chunks.shape
    return exchange(chunks).reshape(count * channels, rows).T


def body(
    token_ids,
    embed_table,
    norm_gain,
    input_weight,
    short_weight,
    filters,
    skip_gain,
    output_weight,
    output_grad,
):
    local_rows = token_ids.shape[0]
    vocab = embed_table.shape[0]
    picks = (token_ids[:, None] == lax.broadcasted_iota(jnp.int32, (1, vocab), 1)).astype(embed_table.dtype)
    tokens = jnp.dot(picks, embed_table, preferred_element_type=jnp.float32).astype(embed_table.dtype)
    token_values = tokens.astype(jnp.float32)
    inverse_rms = lax.rsqrt(jnp.mean(token_values * token_values, axis=-1, keepdims=True) + 1e-06)
    normed = (token_values * inverse_rms * norm_gain).astype(jnp.bfloat16)
    projected = jnp.einsum("td,djc->tjc", normed, input_weight, preferred_element_type=jnp.float32)
    short_taps = short_weight.shape[0]
    before = from_behind(projected[local_rows - (short_taps - 1) :], "ctx", 1)
    extended = jnp.concatenate([before, projected], axis=0)
    features = sum(
        (
            short_weight[tap_index]
            * extended[short_taps - 1 - tap_index : short_taps - 1 - tap_index + local_rows]
            for tap_index in range(short_taps)
        )
    )
    queries = features[:, 0]
    key_part = features[:, 1]
    value_part = features[:, 2]
    mixture = key_part * value_part
    weight_rows = lax.all_to_all(output_weight, TP, 0, 1, tiled=True)
    chip_weight = lax.all_gather(input_weight, "core", axis=2, tiled=True)
    mixture, weight_rows, chip_weight = lax.optimization_barrier((mixture, weight_rows, chip_weight))

    mixture_chunks, taps_received = exchange_many([channel_chunks(mixture), tap_chunks(filters)], 2)
    group_taps, reversed_taps = taps_from(taps_received)
    causal_taps, anti_taps = conv_taps(group_taps, reversed_taps, BLOCK)
    long_part = to_rows(windowed_conv(causal_taps, mixture_chunks, True, BLOCK))
    mixed_out = skip_gain * mixture + long_part
    hidden = (queries * mixed_out).astype(jnp.bfloat16)

    tp_size = lax.axis_size(TP)
    width = token_values.shape[1] // tp_size
    hidden_grad = jnp.dot(output_grad, output_weight, preferred_element_type=jnp.float32)
    mixed_grad = hidden_grad * queries
    hidden, mixed_grad, weight_rows = lax.optimization_barrier((hidden, mixed_grad, weight_rows))
    hidden_wide = lax.all_gather(hidden, TP, axis=1, tiled=True)
    ctx_size = lax.axis_size("ctx")
    weight_partial = jnp.einsum(
        "td,tc->dc", output_grad, hidden, preferred_element_type=jnp.float32
    ).astype(jnp.bfloat16)
    weight_pieces = weight_partial.reshape(ctx_size, -1, weight_partial.shape[1])
    grad_chunks, weight_received = exchange_many([channel_chunks(mixed_grad), weight_pieces], 1)
    output_weight_grad = jnp.sum(weight_received.astype(jnp.float32), axis=0)
    carried = to_rows(windowed_conv(anti_taps, grad_chunks, False, BLOCK))
    hidden_wide, carried = lax.optimization_barrier((hidden_wide, carried))
    own_sums = jnp.einsum("tc,dc->td", hidden_wide, weight_rows, preferred_element_type=jnp.float32)
    own_tokens = lax.dynamic_slice_in_dim(token_values, lax.axis_index(TP) * width, width, axis=1)
    own_output = (own_tokens + own_sums).astype(jnp.bfloat16)
    block_output = lax.all_gather(own_output, TP, axis=1, tiled=True)
    mixture_grad = skip_gain * mixed_grad + carried
    feature_grad = jnp.stack(
        [hidden_grad * mixed_out, mixture_grad * value_part, mixture_grad * key_part], axis=1
    )
    following = from_behind(feature_grad[: short_taps - 1], "ctx", -1)
    extended_grads = jnp.concatenate([feature_grad, following], axis=0)
    projection_grad = sum(
        (
            short_weight[tap_index] * extended_grads[tap_index : tap_index + local_rows]
            for tap_index in range(short_taps)
        )
    ).astype(jnp.bfloat16)
    chips = lax.axis_size("chip")
    cores = lax.axis_size("core")
    row_blocks = projection_grad.reshape(
        chips, cores, local_rows // tp_size, short_taps, projection_grad.shape[2]
    )
    chip_rows = lax.all_to_all(row_blocks, "core", 1, 4, tiled=True)
    chip_rows = chip_rows.reshape(local_rows // cores, short_taps, chip_rows.shape[4])
    partial_grad = jnp.einsum(
        "mjc,djc->md", chip_rows, chip_weight, preferred_element_type=jnp.float32
    ).astype(jnp.bfloat16)
    partial_grad = partial_grad.reshape(chips, local_rows // tp_size, partial_grad.shape[1])
    received = lax.all_to_all(partial_grad, "chip", 0, 0)
    normed_grad = jnp.sum(received.astype(jnp.float32), axis=0)
    return (block_output, output_weight_grad, projection_grad, normed_grad)


def solution(mesh):
    ctx_size, tp_size = mesh.devices.shape
    devices = mesh.devices.reshape(ctx_size, tp_size // 2, 2)
    split_mesh = jax.sharding.Mesh(devices, ("ctx", "chip", "core"))
    in_specs = (
        P("ctx"),
        P(),
        P(),
        P(None, None, TP),
        P(None, None, TP),
        P(TP, "ctx"),
        P(TP),
        P(None, TP),
        P("ctx", None),
    )
    out_specs = (P("ctx", None), P("ctx", TP), P("ctx", None, TP), P(("ctx",) + TP, None))
    return jax.shard_map(body, mesh=split_mesh, in_specs=in_specs, out_specs=out_specs, check_vma=False)
```

```python
import functools

import jax
import jax.numpy as jnp
from jax import lax
from jax.experimental import pallas as pl
from jax.experimental.pallas import tpu as pltpu
from jax.sharding import PartitionSpec as P

precise = lax.Precision.HIGHEST
BLOCK = 256
TP = ("chip", "core")


def from_behind(value, axis, steps):
    count = lax.axis_size(axis)
    first, last = (max(0, -steps), min(count, count - steps))
    return lax.ppermute(value, axis, [(source, source + steps) for source in range(first, last)])


def conv_taps(taps, reversed_taps, block):
    groups, length = taps.shape
    one = jnp.zeros((groups, 1), taps.dtype)
    causal = jnp.concatenate([one, reversed_taps, jnp.zeros((groups, block - 1), taps.dtype)], axis=1)
    anti = jnp.concatenate([jnp.zeros((groups, block), taps.dtype), taps], axis=1)
    return causal[:, None, :], anti[:, None, :]


def tap_chunks(filters):
    width = filters.shape[1]
    rows = lax.broadcasted_iota(jnp.int32, (width, width), 0)
    cols = lax.broadcasted_iota(jnp.int32, (width, width), 1)
    exchange_matrix = (rows + cols == width - 1).astype(filters.dtype)
    flipped = jnp.dot(filters, exchange_matrix, precision=precise)
    shards = lax.axis_size("ctx")
    both = jnp.stack([filters, flipped]).reshape(2, shards, filters.shape[0] // shards, width)
    return both.transpose(1, 0, 2, 3)


def taps_from(received):
    shards, _, groups, width = received.shape
    both = received.transpose(1, 2, 0, 3).reshape(2, groups, shards * width)
    pieces = both[1].reshape(groups, shards, width)
    reversed_taps = jnp.concatenate([pieces[:, k] for k in reversed(range(shards))], axis=1)
    return both[0], reversed_taps


def conv_kernel(causal, block, x_ref, taps_ref, o_ref):
    count, channels, rows = x_ref.shape
    length = count * rows
    wide = jnp.broadcast_to(taps_ref[0], (block, taps_ref.shape[2]))
    matrix = pltpu.roll(wide, 0, 1, stride=1, stride_axis=0)[:, block : block + length]
    signal = jnp.concatenate([x_ref[k] for k in range(count)], axis=1)
    zeros = jnp.zeros((channels, length - block), signal.dtype)
    padded = jnp.concatenate([zeros, signal] if causal else [signal, zeros], axis=1)
    steps = length // block
    windows = jnp.concatenate(
        [padded[:, i * block : i * block + length] for i in range(steps)], axis=0
    )
    result = lax.dot_general(
        windows, matrix, (((1,), (1,)), ((), ())),
        precision=lax.Precision.HIGH, preferred_element_type=jnp.float32,
    )
    line = jnp.concatenate(
        [result[i * channels : (i + 1) * channels] for i in range(steps)], axis=1
    )
    for k in range(count):
        o_ref[k] = line[:, k * rows : (k + 1) * rows]


def windowed_conv(padded_taps, chunks, causal, block):
    count, channels, rows = chunks.shape
    groups, _, width = padded_taps.shape
    share = channels // groups
    return pl.pallas_call(
        functools.partial(conv_kernel, causal, block),
        out_shape=jax.ShapeDtypeStruct(chunks.shape, chunks.dtype),
        grid=(groups,),
        in_specs=[
            pl.BlockSpec((count, share, rows), lambda g: (0, g, 0)),
            pl.BlockSpec((1, 1, width), lambda g: (g, 0, 0)),
        ],
        out_specs=pl.BlockSpec((count, share, rows), lambda g: (0, g, 0)),
    )(chunks, padded_taps)


def exchange_kernel(axis, parts, *refs):
    inputs, outputs = refs[:parts], refs[parts : 2 * parts]
    send_sems, recv_sems, local_sems = refs[2 * parts :]
    count = inputs[0].shape[0]
    place = {name: lax.axis_index(name) for name in ("ctx", "chip", "core")}
    me = place[axis]

    def device(index):
        return tuple(index if name == axis else place[name] for name in ("ctx", "chip", "core"))

    mesh_id = pl.DeviceIdType.MESH
    barrier = pltpu.get_barrier_semaphore()
    for offset in range(1, count):
        peer = lax.rem(me + offset, count)
        pl.semaphore_signal(barrier, 1, device_id=device(peer), device_id_type=mesh_id)
    pl.semaphore_wait(barrier, count - 1)
    locals_ = []
    sends = []
    for part in range(parts):
        x_ref, o_ref = inputs[part], outputs[part]
        local = pltpu.make_async_copy(x_ref.at[me], o_ref.at[me], local_sems.at[part])
        local.start()
        locals_.append(local)
        for offset in range(1, count):
            peer = lax.rem(me + offset, count)
            copy = pltpu.make_async_remote_copy(
                src_ref=x_ref.at[peer],
                dst_ref=o_ref.at[me],
                send_sem=send_sems.at[part, offset],
                recv_sem=recv_sems.at[part, offset],
                device_id=device(peer),
                device_id_type=mesh_id,
            )
            copy.start()
            sends.append(copy)
    for copy in sends:
        copy.wait_send()
    for part in range(parts):
        x_ref, o_ref = inputs[part], outputs[part]
        for offset in range(1, count):
            source = lax.rem(me + count - offset, count)
            pltpu.make_async_remote_copy(
                src_ref=x_ref.at[source],
                dst_ref=o_ref.at[source],
                send_sem=send_sems.at[part, offset],
                recv_sem=recv_sems.at[part, offset],
                device_id=device(source),
                device_id_type=mesh_id,
            ).wait_recv()
    for local in locals_:
        local.wait()


def exchange_many(chunk_list, collective, axis="ctx"):
    parts = len(chunk_list)
    count = chunk_list[0].shape[0]
    return pl.pallas_call(
        functools.partial(exchange_kernel, axis, parts),
        out_shape=[jax.ShapeDtypeStruct(c.shape, c.dtype) for c in chunk_list],
        in_specs=[pl.BlockSpec(memory_space=pl.ANY)] * parts,
        out_specs=[pl.BlockSpec(memory_space=pl.ANY)] * parts,
        scratch_shapes=[
            pltpu.SemaphoreType.DMA((parts, count)),
            pltpu.SemaphoreType.DMA((parts, count)),
            pltpu.SemaphoreType.DMA((parts,)),
        ],
        compiler_params=pltpu.CompilerParams(collective_id=collective, has_side_effects=True),
    )(*chunk_list)


def exchange(chunks, collective=0, axis="ctx"):
    return exchange_many([chunks], collective, axis)[0]


def channel_chunks(value):
    rows, channels = value.shape
    count = lax.axis_size("ctx")
    return value.T.reshape(count, channels // count, rows)


def to_channels(value):
    return exchange(channel_chunks(value))


def to_rows(chunks):
    count, channels, rows = chunks.shape
    return exchange(chunks).reshape(count * channels, rows).T


def body(
    token_ids,
    embed_table,
    norm_gain,
    input_weight,
    short_weight,
    filters,
    skip_gain,
    output_weight,
    output_grad,
):
    local_rows = token_ids.shape[0]
    vocab = embed_table.shape[0]
    picks = (token_ids[:, None] == lax.broadcasted_iota(jnp.int32, (1, vocab), 1)).astype(embed_table.dtype)
    tokens = jnp.dot(picks, embed_table, preferred_element_type=jnp.float32).astype(embed_table.dtype)
    token_values = tokens.astype(jnp.float32)
    inverse_rms = lax.rsqrt(jnp.mean(token_values * token_values, axis=-1, keepdims=True) + 1e-06)
    normed = (token_values * inverse_rms * norm_gain).astype(jnp.bfloat16)
    projected = jnp.einsum("td,djc->tjc", normed, input_weight, preferred_element_type=jnp.float32)
    short_taps = short_weight.shape[0]
    before = from_behind(projected[local_rows - (short_taps - 1) :], "ctx", 1)
    extended = jnp.concatenate([before, projected], axis=0)
    features = sum(
        (
            short_weight[tap_index]
            * extended[short_taps - 1 - tap_index : short_taps - 1 - tap_index + local_rows]
            for tap_index in range(short_taps)
        )
    )
    queries = features[:, 0]
    key_part = features[:, 1]
    value_part = features[:, 2]
    mixture = key_part * value_part
    weight_rows = lax.all_to_all(output_weight, TP, 0, 1, tiled=True)
    chip_weight = lax.all_gather(input_weight, "core", axis=2, tiled=True)
    mixture, weight_rows, chip_weight = lax.optimization_barrier((mixture, weight_rows, chip_weight))

    mixture_chunks, taps_received = exchange_many([channel_chunks(mixture), tap_chunks(filters)], 2)
    group_taps, reversed_taps = taps_from(taps_received)
    causal_taps, anti_taps = conv_taps(group_taps, reversed_taps, BLOCK)
    long_part = to_rows(windowed_conv(causal_taps, mixture_chunks, True, BLOCK))
    mixed_out = skip_gain * mixture + long_part
    hidden = (queries * mixed_out).astype(jnp.bfloat16)

    tp_size = lax.axis_size(TP)
    width = token_values.shape[1] // tp_size
    hidden_grad = jnp.dot(output_grad, output_weight, preferred_element_type=jnp.float32)
    mixed_grad = hidden_grad * queries
    hidden, mixed_grad, weight_rows = lax.optimization_barrier((hidden, mixed_grad, weight_rows))
    hidden_wide = lax.all_gather(hidden, TP, axis=1, tiled=True)
    ctx_size = lax.axis_size("ctx")
    weight_partial = jnp.einsum(
        "td,tc->dc", output_grad, hidden, preferred_element_type=jnp.float32
    ).astype(jnp.bfloat16)
    weight_pieces = weight_partial.reshape(ctx_size, -1, weight_partial.shape[1])
    grad_chunks, weight_received = exchange_many([channel_chunks(mixed_grad), weight_pieces], 1)
    output_weight_grad = jnp.sum(weight_received.astype(jnp.float32), axis=0)
    carried = to_rows(windowed_conv(anti_taps, grad_chunks, False, BLOCK))
    hidden_wide, carried = lax.optimization_barrier((hidden_wide, carried))
    own_sums = jnp.einsum("tc,dc->td", hidden_wide, weight_rows, preferred_element_type=jnp.float32)
    own_tokens = lax.dynamic_slice_in_dim(token_values, lax.axis_index(TP) * width, width, axis=1)
    own_output = (own_tokens + own_sums).astype(jnp.bfloat16)
    block_output = lax.all_gather(own_output, TP, axis=1, tiled=True)
    mixture_grad = skip_gain * mixed_grad + carried
    feature_grad = jnp.stack(
        [hidden_grad * mixed_out, mixture_grad * value_part, mixture_grad * key_part], axis=1
    )
    following = from_behind(feature_grad[: short_taps - 1], "ctx", -1)
    extended_grads = jnp.concatenate([feature_grad, following], axis=0)
    projection_grad = sum(
        (
            short_weight[tap_index] * extended_grads[tap_index : tap_index + local_rows]
            for tap_index in range(short_taps)
        )
    ).astype(jnp.bfloat16)
    chips = lax.axis_size("chip")
    cores = lax.axis_size("core")
    row_blocks = projection_grad.reshape(
        chips, cores, local_rows // tp_size, short_taps, projection_grad.shape[2]
    )
    chip_rows = lax.all_to_all(row_blocks, "core", 1, 4, tiled=True)
    chip_rows = chip_rows.reshape(local_rows // cores, short_taps, chip_rows.shape[4])
    halves = []
    features = chip_weight.shape[0] // 2
    for half in range(2):
        partial_grad = jnp.einsum(
            "mjc,djc->md",
            chip_rows,
            chip_weight[half * features : (half + 1) * features],
            preferred_element_type=jnp.float32,
        ).astype(jnp.bfloat16)
        partial_grad = partial_grad.reshape(chips, local_rows // tp_size, features)
        received = lax.all_to_all(partial_grad, "chip", 0, 0)
        halves.append(jnp.sum(received.astype(jnp.float32), axis=0))
    normed_grad = jnp.concatenate(halves, axis=1)
    return (block_output, output_weight_grad, projection_grad, normed_grad)


def solution(mesh):
    ctx_size, tp_size = mesh.devices.shape
    devices = mesh.devices.reshape(ctx_size, tp_size // 2, 2)
    split_mesh = jax.sharding.Mesh(devices, ("ctx", "chip", "core"))
    in_specs = (
        P("ctx"),
        P(),
        P(),
        P(None, None, TP),
        P(None, None, TP),
        P(TP, "ctx"),
        P(TP),
        P(None, TP),
        P("ctx", None),
    )
    out_specs = (P("ctx", None), P("ctx", TP), P("ctx", None, TP), P(("ctx",) + TP, None))
    return jax.shard_map(body, mesh=split_mesh, in_specs=in_specs, out_specs=out_specs, check_vma=False)
```

```python
import functools

import jax
import jax.numpy as jnp
from jax import lax
from jax.experimental import pallas as pl
from jax.experimental.pallas import tpu as pltpu
from jax.sharding import PartitionSpec as P

precise = lax.Precision.HIGHEST
BLOCK = 384
TP = ("chip", "core")


def from_behind(value, axis, steps):
    count = lax.axis_size(axis)
    first, last = (max(0, -steps), min(count, count - steps))
    return lax.ppermute(value, axis, [(source, source + steps) for source in range(first, last)])


def conv_taps(taps, reversed_taps, block):
    groups, length = taps.shape
    one = jnp.zeros((groups, 1), taps.dtype)
    causal = jnp.concatenate([one, reversed_taps, jnp.zeros((groups, block - 1), taps.dtype)], axis=1)
    anti = jnp.concatenate([jnp.zeros((groups, block), taps.dtype), taps], axis=1)
    return causal[:, None, :], anti[:, None, :]


def tap_chunks(filters):
    width = filters.shape[1]
    rows = lax.broadcasted_iota(jnp.int32, (width, width), 0)
    cols = lax.broadcasted_iota(jnp.int32, (width, width), 1)
    exchange_matrix = (rows + cols == width - 1).astype(filters.dtype)
    flipped = jnp.dot(filters, exchange_matrix, precision=precise)
    shards = lax.axis_size("ctx")
    both = jnp.stack([filters, flipped]).reshape(2, shards, filters.shape[0] // shards, width)
    return both.transpose(1, 0, 2, 3)


def taps_from(received):
    shards, _, groups, width = received.shape
    both = received.transpose(1, 2, 0, 3).reshape(2, groups, shards * width)
    pieces = both[1].reshape(groups, shards, width)
    reversed_taps = jnp.concatenate([pieces[:, k] for k in reversed(range(shards))], axis=1)
    return both[0], reversed_taps


def conv_kernel(causal, block, x_ref, taps_ref, o_ref):
    count, channels, rows = x_ref.shape
    length = count * rows
    wide = jnp.broadcast_to(taps_ref[0], (block, taps_ref.shape[2]))
    matrix = pltpu.roll(wide, 0, 1, stride=1, stride_axis=0)[:, block : block + length]
    signal = jnp.concatenate([x_ref[k] for k in range(count)], axis=1)
    zeros = jnp.zeros((channels, length - block), signal.dtype)
    padded = jnp.concatenate([zeros, signal] if causal else [signal, zeros], axis=1)
    steps = length // block
    windows = jnp.concatenate(
        [padded[:, i * block : i * block + length] for i in range(steps)], axis=0
    )
    result = lax.dot_general(
        windows, matrix, (((1,), (1,)), ((), ())),
        precision=lax.Precision.HIGH, preferred_element_type=jnp.float32,
    )
    line = jnp.concatenate(
        [result[i * channels : (i + 1) * channels] for i in range(steps)], axis=1
    )
    for k in range(count):
        o_ref[k] = line[:, k * rows : (k + 1) * rows]


def windowed_conv(padded_taps, chunks, causal, block):
    count, channels, rows = chunks.shape
    groups, _, width = padded_taps.shape
    share = channels // groups
    return pl.pallas_call(
        functools.partial(conv_kernel, causal, block),
        out_shape=jax.ShapeDtypeStruct(chunks.shape, chunks.dtype),
        grid=(groups,),
        in_specs=[
            pl.BlockSpec((count, share, rows), lambda g: (0, g, 0)),
            pl.BlockSpec((1, 1, width), lambda g: (g, 0, 0)),
        ],
        out_specs=pl.BlockSpec((count, share, rows), lambda g: (0, g, 0)),
    )(chunks, padded_taps)


def exchange_kernel(axis, parts, *refs):
    inputs, outputs = refs[:parts], refs[parts : 2 * parts]
    send_sems, recv_sems, local_sems = refs[2 * parts :]
    count = inputs[0].shape[0]
    place = {name: lax.axis_index(name) for name in ("ctx", "chip", "core")}
    me = place[axis]

    def device(index):
        return tuple(index if name == axis else place[name] for name in ("ctx", "chip", "core"))

    mesh_id = pl.DeviceIdType.MESH
    barrier = pltpu.get_barrier_semaphore()
    for offset in range(1, count):
        peer = lax.rem(me + offset, count)
        pl.semaphore_signal(barrier, 1, device_id=device(peer), device_id_type=mesh_id)
    pl.semaphore_wait(barrier, count - 1)
    locals_ = []
    sends = []
    for part in range(parts):
        x_ref, o_ref = inputs[part], outputs[part]
        local = pltpu.make_async_copy(x_ref.at[me], o_ref.at[me], local_sems.at[part])
        local.start()
        locals_.append(local)
        for offset in range(1, count):
            peer = lax.rem(me + offset, count)
            copy = pltpu.make_async_remote_copy(
                src_ref=x_ref.at[peer],
                dst_ref=o_ref.at[me],
                send_sem=send_sems.at[part, offset],
                recv_sem=recv_sems.at[part, offset],
                device_id=device(peer),
                device_id_type=mesh_id,
            )
            copy.start()
            sends.append(copy)
    for copy in sends:
        copy.wait_send()
    for part in range(parts):
        x_ref, o_ref = inputs[part], outputs[part]
        for offset in range(1, count):
            source = lax.rem(me + count - offset, count)
            pltpu.make_async_remote_copy(
                src_ref=x_ref.at[source],
                dst_ref=o_ref.at[source],
                send_sem=send_sems.at[part, offset],
                recv_sem=recv_sems.at[part, offset],
                device_id=device(source),
                device_id_type=mesh_id,
            ).wait_recv()
    for local in locals_:
        local.wait()


def exchange_many(chunk_list, collective, axis="ctx"):
    parts = len(chunk_list)
    count = chunk_list[0].shape[0]
    return pl.pallas_call(
        functools.partial(exchange_kernel, axis, parts),
        out_shape=[jax.ShapeDtypeStruct(c.shape, c.dtype) for c in chunk_list],
        in_specs=[pl.BlockSpec(memory_space=pl.ANY)] * parts,
        out_specs=[pl.BlockSpec(memory_space=pl.ANY)] * parts,
        scratch_shapes=[
            pltpu.SemaphoreType.DMA((parts, count)),
            pltpu.SemaphoreType.DMA((parts, count)),
            pltpu.SemaphoreType.DMA((parts,)),
        ],
        compiler_params=pltpu.CompilerParams(collective_id=collective, has_side_effects=True),
    )(*chunk_list)


def exchange(chunks, collective=0, axis="ctx"):
    return exchange_many([chunks], collective, axis)[0]


def channel_chunks(value):
    rows, channels = value.shape
    count = lax.axis_size("ctx")
    return value.T.reshape(count, channels // count, rows)


def to_channels(value):
    return exchange(channel_chunks(value))


def to_rows(chunks):
    count, channels, rows = chunks.shape
    return exchange(chunks).reshape(count * channels, rows).T


def body(
    token_ids,
    embed_table,
    norm_gain,
    input_weight,
    short_weight,
    filters,
    skip_gain,
    output_weight,
    output_grad,
):
    local_rows = token_ids.shape[0]
    vocab = embed_table.shape[0]
    picks = (token_ids[:, None] == lax.broadcasted_iota(jnp.int32, (1, vocab), 1)).astype(embed_table.dtype)
    tokens = jnp.dot(picks, embed_table, preferred_element_type=jnp.float32).astype(embed_table.dtype)
    token_values = tokens.astype(jnp.float32)
    inverse_rms = lax.rsqrt(jnp.mean(token_values * token_values, axis=-1, keepdims=True) + 1e-06)
    normed = (token_values * inverse_rms * norm_gain).astype(jnp.bfloat16)
    projected = jnp.einsum("td,djc->tjc", normed, input_weight, preferred_element_type=jnp.float32)
    short_taps = short_weight.shape[0]
    before = from_behind(projected[local_rows - (short_taps - 1) :], "ctx", 1)
    extended = jnp.concatenate([before, projected], axis=0)
    features = sum(
        (
            short_weight[tap_index]
            * extended[short_taps - 1 - tap_index : short_taps - 1 - tap_index + local_rows]
            for tap_index in range(short_taps)
        )
    )
    queries = features[:, 0]
    key_part = features[:, 1]
    value_part = features[:, 2]
    mixture = key_part * value_part
    weight_rows = lax.all_to_all(output_weight, TP, 0, 1, tiled=True)
    chip_weight = lax.all_gather(input_weight, "core", axis=2, tiled=True)
    mixture, weight_rows, chip_weight = lax.optimization_barrier((mixture, weight_rows, chip_weight))

    mixture_chunks, taps_received = exchange_many([channel_chunks(mixture), tap_chunks(filters)], 2)
    group_taps, reversed_taps = taps_from(taps_received)
    causal_taps, anti_taps = conv_taps(group_taps, reversed_taps, BLOCK)
    long_part = to_rows(windowed_conv(causal_taps, mixture_chunks, True, BLOCK))
    mixed_out = skip_gain * mixture + long_part
    hidden = (queries * mixed_out).astype(jnp.bfloat16)

    tp_size = lax.axis_size(TP)
    width = token_values.shape[1] // tp_size
    hidden_grad = jnp.dot(output_grad, output_weight, preferred_element_type=jnp.float32)
    mixed_grad = hidden_grad * queries
    hidden, mixed_grad, weight_rows = lax.optimization_barrier((hidden, mixed_grad, weight_rows))
    hidden_wide = lax.all_gather(hidden, TP, axis=1, tiled=True)
    ctx_size = lax.axis_size("ctx")
    weight_partial = jnp.einsum(
        "td,tc->dc", output_grad, hidden, preferred_element_type=jnp.float32
    ).astype(jnp.bfloat16)
    weight_pieces = weight_partial.reshape(ctx_size, -1, weight_partial.shape[1])
    grad_chunks, weight_received = exchange_many([channel_chunks(mixed_grad), weight_pieces], 1)
    output_weight_grad = jnp.sum(weight_received.astype(jnp.float32), axis=0)
    carried = to_rows(windowed_conv(anti_taps, grad_chunks, False, BLOCK))
    hidden_wide, carried = lax.optimization_barrier((hidden_wide, carried))
    own_sums = jnp.einsum("tc,dc->td", hidden_wide, weight_rows, preferred_element_type=jnp.float32)
    own_tokens = lax.dynamic_slice_in_dim(token_values, lax.axis_index(TP) * width, width, axis=1)
    own_output = (own_tokens + own_sums).astype(jnp.bfloat16)
    block_output = lax.all_gather(own_output, TP, axis=1, tiled=True)
    mixture_grad = skip_gain * mixed_grad + carried
    feature_grad = jnp.stack(
        [hidden_grad * mixed_out, mixture_grad * value_part, mixture_grad * key_part], axis=1
    )
    following = from_behind(feature_grad[: short_taps - 1], "ctx", -1)
    extended_grads = jnp.concatenate([feature_grad, following], axis=0)
    projection_grad = sum(
        (
            short_weight[tap_index] * extended_grads[tap_index : tap_index + local_rows]
            for tap_index in range(short_taps)
        )
    ).astype(jnp.bfloat16)
    chips = lax.axis_size("chip")
    cores = lax.axis_size("core")
    row_blocks = projection_grad.reshape(
        chips, cores, local_rows // tp_size, short_taps, projection_grad.shape[2]
    )
    chip_rows = lax.all_to_all(row_blocks, "core", 1, 4, tiled=True)
    chip_rows = chip_rows.reshape(local_rows // cores, short_taps, chip_rows.shape[4])
    partial_grad = jnp.einsum(
        "mjc,djc->md", chip_rows, chip_weight, preferred_element_type=jnp.float32
    ).astype(jnp.bfloat16)
    partial_grad = partial_grad.reshape(chips, local_rows // tp_size, partial_grad.shape[1])
    received = lax.all_to_all(partial_grad, "chip", 0, 0)
    normed_grad = jnp.sum(received.astype(jnp.float32), axis=0)
    return (block_output, output_weight_grad, projection_grad, normed_grad)


def solution(mesh):
    ctx_size, tp_size = mesh.devices.shape
    devices = mesh.devices.reshape(ctx_size, tp_size // 2, 2)
    split_mesh = jax.sharding.Mesh(devices, ("ctx", "chip", "core"))
    in_specs = (
        P("ctx"),
        P(),
        P(),
        P(None, None, TP),
        P(None, None, TP),
        P(TP, "ctx"),
        P(TP),
        P(None, TP),
        P("ctx", None),
    )
    out_specs = (P("ctx", None), P("ctx", TP), P("ctx", None, TP), P(("ctx",) + TP, None))
    return jax.shard_map(body, mesh=split_mesh, in_specs=in_specs, out_specs=out_specs, check_vma=False)
```
